32 devices in a mesh: groups: 2 (over y), seq: 4 (over z), tp: 2 (over x), rep: 2 (over core).
Axes of the slice: x: 2, y: 2, z: 4, core: 2. Of those that a mesh axis runs over, the one named last changes fastest.
Arguments:
- queries: bfloat16 [2, 128, 8192], P('rep', ('groups', 'seq', 'tp')), parts along dimension 1, may hold values from -8 to 8
- fresh_key_rows: bfloat16 [2, 128, 1024], P('rep', ('groups', 'seq', 'tp')), parts along dimension 1, may hold values from -8 to 8
- fresh_value_rows: bfloat16 [2, 128, 1024], P('rep', ('groups', 'seq', 'tp')), parts along dimension 1, may hold values from -8 to 8
- visible: int32 [2, 128], P('rep', 'groups'), parts along dimension 1, may hold values from 128 to 2048, as said below
- prefix_keys: bfloat16 [4096, 1024], P(('groups', 'seq'), 'tp'), parts along dimension 0, may hold values from -6 to 6
- cached_value_rows: bfloat16 [4096, 1024], P(('groups', 'seq'), 'tp'), parts along dimension 0, may hold values from -8 to 8
- out_weight: bfloat16 [8192, 8192], P('tp', 'seq'), may hold values from -0.0625 to 0.0625
Outputs:
- mixed: bfloat16 [2, 128, 8192], P('rep', ('groups', 'tp'), 'seq'), parts along dimension 1
The draws below stay inside these ranges and needn't reach their ends.
There are 2 independent parts, one for each index of `groups`. The reference program is written for one: setup_inputs(seed, part) draws one part's arguments, and reference() takes and returns one part's arrays. A program takes and returns all parts, laid end to end along the dimension named above; an argument that names none is the same for every part. Nothing has to cross between parts.
Inputs may be any that keep to these rules, and one draw needn't show every extreme that they name: Token i of half r sees prefix positions 0 to visible[r, i] - 1; in each half some token sees the whole prefix.
All inputs are finite; a program needn't handle non-finite values.
Results may differ from the reference program's by a relative error of at most 0.0051.
Values may be sent and summed in bfloat16 or wider, within the bound.
A program may use at most 64 MiB of HBM per device.

```python
import math
import jax
import jax.numpy as jnp
from jax import lax

D = 8192
QUERY_HEAD_COUNT = 64
KEY_VALUE_HEADS = 8
HEAD_WIDTH = 128
PB = 512
PREFIX_LENGTH = 2048
HALF_TOKENS = 64
N_REP = 2


def draw_queries(key, part):
    sampled_items = 2.5 * jax.random.normal(jax.random.fold_in(key, 11), (N_REP, HALF_TOKENS, QUERY_HEAD_COUNT * HEAD_WIDTH), jnp.float32)
    sampled_items = jnp.clip(sampled_items, -7.5, 7.5)
    return sampled_items.astype(jnp.bfloat16)


def draw_prefix_keys(key, part):
    sampled_items = jax.random.normal(jax.random.fold_in(key, 12), (PREFIX_LENGTH, KEY_VALUE_HEADS * HEAD_WIDTH), jnp.float32)
    sampled_items = jnp.clip(sampled_items, -6.0, 6.0)
    return sampled_items.astype(jnp.bfloat16)


def draw_visible(key, part):
    cutoffs = jax.random.randint(jax.random.fold_in(key, 21), (N_REP, HALF_TOKENS), PREFIX_LENGTH // 16, PREFIX_LENGTH + 1)
    full_rows = jax.random.randint(jax.random.fold_in(key, 22), (N_REP, HALF_TOKENS), 0, 16) == 0
    cutoffs = jnp.where(full_rows, PREFIX_LENGTH, cutoffs)
    return cutoffs.at[:, 0].set(PREFIX_LENGTH).astype(jnp.int32)


def steps_of(own_key, extent, cuts, smallest, largest):
    level = 1.0
    for axis_at, blocks in cuts:
        heights = jax.random.uniform(jax.random.fold_in(jax.random.fold_in(own_key, 6), axis_at), (blocks,), jnp.float32, smallest / len(cuts), largest / len(cuts))
        level = level * jnp.repeat(jnp.exp(heights), extent[axis_at] // blocks).reshape((-1,) + (1,) * (len(extent) - 1 - axis_at))
    return level


def centred(rng, shape, scale, limit, cuts=(), held_as=jnp.bfloat16):
    gain = steps_of(rng, shape, cuts, -0.22, 0.18) if cuts else 1.0
    array = jax.random.normal(rng, shape, jnp.float32) * scale * gain
    return jnp.minimum(jnp.maximum(array, -limit), limit).astype(held_as)


def setup_inputs(seed: int = 0, part: int = 0) -> dict:
    arg_keys = jax.random.split(jax.random.key(seed), 8)
    part_keys = jax.random.split(jax.random.fold_in(arg_keys[7], part), 8)
    return {
        "queries": draw_queries(jax.random.fold_in(jax.random.fold_in(arg_keys[7], part), 71), part),
        "fresh_key_rows": centred(part_keys[1], (N_REP, HALF_TOKENS, KEY_VALUE_HEADS * HEAD_WIDTH), 2.0, 8.0, ((0, 2), (1, 8))),
        "fresh_value_rows": centred(part_keys[2], (N_REP, HALF_TOKENS, KEY_VALUE_HEADS * HEAD_WIDTH), 2.0, 8.0, ((0, 2), (1, 8))),
        "visible": draw_visible(jax.random.fold_in(jax.random.fold_in(arg_keys[7], part), 71), part),
        "prefix_keys": draw_prefix_keys(jax.random.fold_in(jax.random.fold_in(arg_keys[7], part), 71), part),
        "cached_value_rows": centred(part_keys[5], (PREFIX_LENGTH, KEY_VALUE_HEADS * HEAD_WIDTH), 2.0, 8.0, ((0, 4), (1, 2))),
        "out_weight": centred(arg_keys[6], (QUERY_HEAD_COUNT * HEAD_WIDTH, D), (QUERY_HEAD_COUNT * HEAD_WIDTH) ** -0.5, 0.0625, ((0, 2), (1, 4))),
    }


def attend(query_tile_rows, self_key_rows, own_values, lengths, key_table, value_table):
    logit_scale = 1.0 / math.sqrt(query_tile_rows.shape[-1])
    block_count = key_table.shape[0] // PB
    scores = jnp.einsum('bkgd,pkd->bkgp', query_tile_rows, key_table) * logit_scale
    self_score_row = jnp.einsum('tprl,tpl->tpr', query_tile_rows, self_key_rows) * logit_scale
    position = jnp.arange(key_table.shape[0])
    visible_mask = (position[None, :] < lengths[:, None])[:, None, None, :]
    shape_now = scores.shape[:3] + (block_count, PB)
    scores = scores.reshape(shape_now)
    visible_mask = jnp.broadcast_to(visible_mask, scores.shape[:3] + (key_table.shape[0],)).reshape(shape_now)
    block_peak = lax.optimization_barrier(jnp.max(jnp.where(visible_mask, scores, -jnp.inf), axis=-1))
    anchor = jnp.where(jnp.isinf(block_peak), 0.0, block_peak)
    raw_weights = jnp.where(visible_mask, jnp.exp(scores - anchor[..., None]), 0.0)
    block_sum = lax.optimization_barrier(jnp.sum(raw_weights, axis=-1))
    weights = lax.optimization_barrier(raw_weights.astype(jnp.bfloat16)).astype(jnp.float32)
    values_blocked = value_table.reshape(block_count, PB, value_table.shape[1], value_table.shape[2])
    block_context = jnp.einsum('bkgnp,npkd->bkgnd', weights, values_blocked)
    row_peak = jnp.maximum(lax.optimization_barrier(jnp.max(block_peak, axis=-1)), self_score_row)
    fade = jnp.exp(block_peak - row_peak[..., None])
    raw_own = jnp.exp(self_score_row - row_peak)
    weight_own = lax.optimization_barrier(raw_own.astype(jnp.bfloat16)).astype(jnp.float32)
    denominator = lax.optimization_barrier(jnp.sum(block_sum * fade, axis=-1)) + raw_own
    summed = lax.optimization_barrier(jnp.sum(block_context * fade[..., None], axis=3))
    summed = summed + weight_own[..., None] * own_values[:, :, None, :]
    return (summed / denominator[..., None]).astype(jnp.bfloat16)

def reference(queries, fresh_key_rows, fresh_value_rows, visible, prefix_keys, cached_value_rows, out_weight):
    halves, tokens, feature_width = queries.shape
    kv_heads = prefix_keys.shape[1] // HEAD_WIDTH
    per_group = feature_width // (kv_heads * HEAD_WIDTH)
    key_table = prefix_keys.astype(jnp.float32).reshape(-1, kv_heads, HEAD_WIDTH)
    value_table = cached_value_rows.astype(jnp.float32).reshape(-1, kv_heads, HEAD_WIDTH)
    token_block = math.gcd(tokens, 32)
    blocks_count = tokens // token_block
    outputs = []
    for half_index in range(halves):
        query_all = queries[half_index].astype(jnp.float32).reshape(blocks_count, token_block, kv_heads, per_group, HEAD_WIDTH)
        keys_own = fresh_key_rows[half_index].astype(jnp.float32).reshape(blocks_count, token_block, kv_heads, HEAD_WIDTH)
        values_own = fresh_value_rows[half_index].astype(jnp.float32).reshape(blocks_count, token_block, kv_heads, HEAD_WIDTH)
        lengths = visible[half_index].reshape(blocks_count, token_block)

        def attend_block(pieces):
            return attend(pieces[0], pieces[1], pieces[2], pieces[3], key_table, value_table)
        context = lax.map(attend_block, (query_all, keys_own, values_own, lengths)).reshape(tokens, feature_width)
        outputs.append(jnp.dot(context, out_weight, preferred_element_type=jnp.float32).astype(jnp.bfloat16))
    return jnp.stack(outputs)
```

```python
import functools
import math

import jax
import jax.numpy as jnp
from jax import lax
from jax.experimental import pallas as pl
from jax.experimental.pallas import tpu as pltpu
from jax.sharding import PartitionSpec as P

HEAD_WIDTH = 128
MASKED = -1e30
MESH = pl.DeviceIdType.MESH


class Sizes:
    def __init__(self, mesh_shape, queries, visible, prefix_keys, out_weight):
        self.seq = mesh_shape["seq"]
        self.tp = mesh_shape["tp"]
        self.rep = mesh_shape["rep"]
        self.tok = queries.shape[1]
        self.all_tok = visible.shape[1]
        self.block = prefix_keys.shape[0]
        kv_heads = prefix_keys.shape[1] // HEAD_WIDTH
        self.features, self.cols = out_weight.shape
        self.group = self.features // (kv_heads * HEAD_WIDTH)
        self.a = self.seq if kv_heads % self.seq == 0 else 1
        self.b = self.seq // self.a
        self.kl = kv_heads // self.a
        self.slots = self.a * self.tp
        self.nt = self.slots * self.tok
        self.np = self.tp if self.b == 1 else 1
        self.pt = self.nt // self.np
        self.ps = self.slots // self.np
        self.fb = self.kl * self.group * HEAD_WIDTH
        self.kb = self.kl * HEAD_WIDTH
        self.rows = self.group * self.pt
        self.no = self.all_tok // self.tp
        self.tile = math.gcd(self.cols, 512)
        self.tiles = self.cols // self.tile


def kernel(
    z, q_hbm, fk_hbm, fv_hbm, vis_ref, k_hbm, v_hbm, w_hbm, out_ref,
    qbuf, fkbuf, fvbuf, kbuf, vbuf, wbuf, qs, lens, peak, total, acc, cbuf, oacc, osend, orecv,
    q_send, q_recv, kv_send, kv_recv, f_send, f_recv, kv_own, w_sem, c_send, c_recv, o_send, o_recv,
):
    s, t, r = lax.axis_index("seq"), lax.axis_index("tp"), lax.axis_index("rep")
    partner = lax.rem(r + 1, z.rep)
    scale = 1.0 / math.sqrt(HEAD_WIDTH)

    def near(base, step, size):
        return lax.rem(base + step, size)

    def head_of(index):
        return index if z.a > 1 else 0

    barrier = pltpu.get_barrier_semaphore()
    for j in range(z.seq):
        for i in range(z.tp):
            if i or j:
                pl.semaphore_signal(
                    barrier, inc=1, device_id={"seq": near(s, j, z.seq), "tp": near(t, i, z.tp)},
                    device_id_type=MESH,
                )
    pl.semaphore_signal(barrier, inc=1, device_id={"rep": partner}, device_id_type=MESH)

    my_slot = head_of(s) * z.tp + t

    def query_parts(s_to, t_to):
        head = t_to * z.a + head_of(s_to)
        wide = pl.ds(pl.multiple_of(head * z.fb, 128), z.fb)
        thin = pl.ds(pl.multiple_of(head * z.kb, 128), z.kb)
        return (
            (q_hbm.at[0, :, wide], qbuf.at[my_slot]),
            (fk_hbm.at[0, :, thin], fkbuf.at[my_slot]),
            (fv_hbm.at[0, :, thin], fvbuf.at[my_slot]),
        )

    own_parts = [
        pltpu.make_async_copy(src, dst, q_recv.at[n, my_slot])
        for n, (src, dst) in enumerate(query_parts(s, t))
    ]
    thin_own = pl.ds(pl.multiple_of(head_of(s) * z.kb, 128), z.kb)
    own_kv = [
        pltpu.make_async_copy(k_hbm.at[:, thin_own], kbuf.at[s], kv_own.at[0]),
        pltpu.make_async_copy(v_hbm.at[:, thin_own], vbuf.at[s], kv_own.at[1]),
    ]
    weights = [
        pltpu.make_async_copy(w_hbm.at[pl.ds(n * z.fb, z.fb), :], wbuf.at[n], w_sem.at[n])
        for n in range(z.a)
    ]
    for copy in own_parts + own_kv + weights:
        copy.start()
    pl.semaphore_wait(barrier, z.seq * z.tp)

    sent, sent_if = [], []

    def send(copy, s_to=None):
        if s_to is None:
            copy.start()
            sent.append(copy)
        else:
            pl.when(s != s_to)(copy.start)
            sent_if.append((s_to, copy))

    def send_queries(s_to, t_step, only_if):
        t_to = near(t, t_step, z.tp)
        slot = (s_to if z.a > 1 else 0) * z.tp + t_step
        for n, (src, dst) in enumerate(query_parts(s_to, t_to)):
            send(pltpu.make_async_remote_copy(
                src_ref=src, dst_ref=dst, send_sem=q_send.at[n, slot],
                recv_sem=q_recv.at[n, my_slot], device_id={"seq": s_to, "tp": t_to},
                device_id_type=MESH,
            ), s_to if only_if else None)

    half = z.block // z.rep
    my_rows = pl.ds(pl.multiple_of(r * half, half), half)
    if z.a == 1:
        for i in range(1, z.tp):
            send_queries(s, i, False)
    for s_to in sorted(range(z.seq), key=lambda n: abs(2 * n + 1 - z.seq)):
        if z.a > 1:
            for i in range(z.tp):
                send_queries(s_to, i, i == 0)
        thin = pl.ds(head_of(s_to) * z.kb, z.kb)
        for n, (src, dst) in enumerate(((k_hbm, kbuf), (v_hbm, vbuf))):
            send(pltpu.make_async_remote_copy(
                src_ref=src.at[my_rows, thin], dst_ref=dst.at[s, my_rows, :],
                send_sem=kv_send.at[n, s_to], recv_sem=kv_recv.at[n, s],
                device_id={"seq": s_to}, device_id_type=MESH,
            ), s_to)

    def nearest(k):
        flip = s // (z.seq // 2) if z.seq > 1 else 0
        edge = s + flip * (z.seq - 1 - 2 * s)
        both = k <= 2 * edge
        away = jnp.where(both, (k + 1) // 2 * (1 - 2 * (k % 2)), k - edge)
        return s + away * (1 - 2 * flip)

    def owner_of(p):
        return near(t, p + 1, z.tp) if z.np > 1 else 0

    for p in range(z.np):
        want = lax.broadcasted_iota(jnp.int32, (z.pt, z.all_tok), 0) + owner_of(p) * z.pt
        if z.b > 1:
            want = want + s * z.nt
        have = lax.broadcasted_iota(jnp.int32, (z.pt, z.all_tok), 1)
        seen = jnp.where(want == have, jnp.broadcast_to(vis_ref[...], (z.pt, z.all_tok)), 0)
        column = jnp.sum(seen.astype(jnp.float32), axis=1, keepdims=True)
        lens[p] = jnp.concatenate([column] * z.group, axis=0)

    for j in range(z.a):
        for i in range(z.tp):
            slot = (near(s, j, z.seq) if z.a > 1 else 0) * z.tp + near(t, i, z.tp)
            for n, buf in enumerate((qbuf, fkbuf, fvbuf)):
                pltpu.make_async_copy(buf.at[slot], buf.at[slot], q_recv.at[n, slot]).wait()

    def rows_of(buf, p, first):
        some = pl.ds(owner_of(p) * z.ps, z.ps)
        value = buf[some, :, first:first + HEAD_WIDTH].astype(jnp.float32)
        return value.reshape(z.pt, HEAD_WIDTH)

    for p in range(z.np):
        for h in range(z.kl):
            own_key = rows_of(fkbuf, p, h * HEAD_WIDTH)
            own_value = rows_of(fvbuf, p, h * HEAD_WIDTH)
            for g in range(z.group):
                query = rows_of(qbuf, p, (h * z.group + g) * HEAD_WIDTH)
                span = slice(g * z.pt, (g + 1) * z.pt)
                qs[p, h, span, :] = query.astype(jnp.bfloat16)
                peak[p, h, span, :] = jnp.sum(query * own_key, axis=1, keepdims=True) * scale
                total[p, h, span, :] = jnp.ones((z.pt, 1), jnp.float32)
                acc[p, h, span, :] = own_value

    def attend(p, source):
        for h in range(z.kl):
            at = slice(h * HEAD_WIDTH, (h + 1) * HEAD_WIDTH)
            keys, values = kbuf[source, :, at], vbuf[source, :, at]
            scores = lax.dot_general(
                qs[p, h], keys, (((1,), (1,)), ((), ())), preferred_element_type=jnp.float32
            ) * scale
            spot = lax.broadcasted_iota(jnp.int32, scores.shape, 1) + source * z.block
            scores = jnp.where(spot.astype(jnp.float32) < lens[p], scores, MASKED)
            before = peak[p, h]
            now = jnp.maximum(before, jnp.max(scores, axis=1, keepdims=True))
            fade = jnp.exp(before - now)
            part = jnp.exp(scores - now)
            peak[p, h] = now
            total[p, h] = total[p, h] * fade + jnp.sum(part, axis=1, keepdims=True)
            acc[p, h] = acc[p, h] * fade + jnp.dot(
                part.astype(jnp.bfloat16), values, preferred_element_type=jnp.float32
            )

    def finish(p):
        for h in range(z.kl):
            context = (acc[p, h] / total[p, h]).astype(jnp.bfloat16)
            for g in range(z.group):
                at = (h * z.group + g) * HEAD_WIDTH
                cbuf[s, p, :, at:at + HEAD_WIDTH] = context[g * z.pt:(g + 1) * z.pt, :]
        for j in range(1, z.seq):
            sent.append(pltpu.make_async_remote_copy(
                src_ref=cbuf.at[s, p], dst_ref=cbuf.at[s, p],
                send_sem=c_send.at[j, p], recv_sem=c_recv.at[s, p],
                device_id={"seq": near(s, j, z.seq)}, device_id_type=MESH,
            ))
            sent[-1].start()

    for j in range(z.seq):
        source = nearest(j) if j else s
        if j == 0:
            for copy in own_kv:
                copy.wait()
        else:
            passed = []
            for n, buf in enumerate((kbuf, vbuf)):
                mine = buf.at[source, my_rows, :]
                pltpu.make_async_copy(mine, mine, kv_recv.at[n, source]).wait()
                passed.append(pltpu.make_async_remote_copy(
                    src_ref=mine, dst_ref=mine, send_sem=f_send.at[n, j], recv_sem=f_recv.at[n, source],
                    device_id={"rep": partner}, device_id_type=MESH,
                ))
                passed[-1].start()
            other = pl.ds(pl.multiple_of(partner * half, half), half)
            for n, buf in enumerate((kbuf, vbuf)):
                theirs = buf.at[source, other, :]
                pltpu.make_async_copy(theirs, theirs, f_recv.at[n, source]).wait()
            sent.extend(passed)
        for p in range(z.np):
            attend(p, source)
            if j == z.seq - 1:
                finish(p)

    for copy in weights:
        copy.wait()

    def project(j, source, p, at):
        value = jnp.dot(
            cbuf[source, p], wbuf[head_of(source), :, at], preferred_element_type=jnp.float32
        )
        if z.b > 1:
            oacc[pl.ds(pl.multiple_of(source * z.nt, z.nt), z.nt), at] = value
            return value
        rows = slice(p * z.pt, (p + 1) * z.pt)
        if j:
            value = value + oacc[rows, at]
        if j < z.seq - 1:
            oacc[rows, at] = value
        return value

    def give(i, n, value):
        osend[i, n] = value.astype(jnp.bfloat16)
        sent.append(pltpu.make_async_remote_copy(
            src_ref=osend.at[i, n], dst_ref=orecv.at[i, n],
            send_sem=o_send.at[i, n], recv_sem=o_recv.at[i, n],
            device_id={"tp": near(t, i + 1, z.tp)}, device_id_type=MESH,
        ))
        sent[-1].start()

    def keep(n, at, value):
        for i in range(z.tp - 1):
            pltpu.make_async_copy(orecv.at[i, n], orecv.at[i, n], o_recv.at[i, n]).wait()
            value = value + orecv[i, n].astype(jnp.float32)
        out_ref[0, :, at] = value.astype(jnp.bfloat16)

    spans = [slice(n * z.tile, (n + 1) * z.tile) for n in range(z.tiles)]
    for p in range(z.np):
        for j in range(z.seq):
            source = nearest(j) if j else s
            if j:
                landed = cbuf.at[source, p]
                pltpu.make_async_copy(landed, landed, c_recv.at[source, p]).wait()
            for n, at in enumerate(spans):
                value = project(j, source, p, at)
                if z.b == 1 and j == z.seq - 1:
                    if p < z.np - 1:
                        give(p, n, value)
                    else:
                        keep(n, at, value)
    if z.b > 1:
        for n, at in enumerate(spans):
            for i in range(z.tp - 1):
                rows = pl.ds(pl.multiple_of(near(t, i + 1, z.tp) * z.no, z.no), z.no)
                give(i, n, oacc[rows, at])
        for n, at in enumerate(spans):
            keep(n, at, oacc[pl.ds(pl.multiple_of(t * z.no, z.no), z.no), at])
    for copy in sent:
        copy.wait_send()
    for s_to, copy in sent_if:
        pl.when(s != s_to)(copy.wait_send)


def line_kernel(
    z, q_hbm, fk_hbm, fv_hbm, vis_ref, k_hbm, v_hbm, w_hbm, out_ref,
    qbuf, fkbuf, fvbuf, kbuf, vbuf, wbuf, qs, lens, peak, total, acc, cbuf, oacc, osend, orecv,
    q_send, q_recv, kv_send, kv_recv, f_send, f_recv, kv_own, w_sem, c_send, c_recv, o_send, o_recv,
):
    s, t, r = lax.axis_index("seq"), lax.axis_index("tp"), lax.axis_index("rep")
    partner, t_other = 1 - r, 1 - t
    scale = 1.0 / math.sqrt(HEAD_WIDTH)
    low = s < 2
    is_end = (s == 0) | (s == 3)
    mate = s + 1 - 2 * lax.rem(s, 2)
    far_end = jnp.where(low, 3, 0)
    far_mid = jnp.where(low, 2, 1)

    barrier = pltpu.get_barrier_semaphore()
    for j in range(4):
        for i in range(2):
            if i or j:
                pl.semaphore_signal(
                    barrier, inc=1, device_id={"seq": lax.rem(s + j, 4), "tp": lax.rem(t + i, 2)},
                    device_id_type=MESH,
                )
    pl.semaphore_signal(barrier, inc=1, device_id={"rep": partner}, device_id_type=MESH)

    my_slot = s * 2 + t

    def query_parts(s_to, t_to):
        head = t_to * 4 + s_to
        wide = pl.ds(pl.multiple_of(head * z.fb, 128), z.fb)
        thin = pl.ds(pl.multiple_of(head * z.kb, 128), z.kb)
        return (
            (q_hbm.at[0, :, wide], qbuf.at[my_slot]),
            (fk_hbm.at[0, :, thin], fkbuf.at[my_slot]),
            (fv_hbm.at[0, :, thin], fvbuf.at[my_slot]),
        )

    own_parts = [
        pltpu.make_async_copy(src, dst, q_recv.at[n, my_slot])
        for n, (src, dst) in enumerate(query_parts(s, t))
    ]
    thin_own = pl.ds(pl.multiple_of(s * z.kb, 128), z.kb)
    own_kv = [
        pltpu.make_async_copy(k_hbm.at[:, thin_own], kbuf.at[s], kv_own.at[0]),
        pltpu.make_async_copy(v_hbm.at[:, thin_own], vbuf.at[s], kv_own.at[1]),
    ]
    weights = [
        pltpu.make_async_copy(w_hbm.at[pl.ds(n * z.fb, z.fb), :], wbuf.at[n], w_sem.at[n])
        for n in range(4)
    ]
    for copy in own_parts + own_kv + weights:
        copy.start()

    def column_of_lengths(p):
        want = lax.broadcasted_iota(jnp.int32, (z.pt, z.all_tok), 0) + owner_of(p) * z.pt
        have = lax.broadcasted_iota(jnp.int32, (z.pt, z.all_tok), 1)
        seen = jnp.where(want == have, jnp.broadcast_to(vis_ref[...], (z.pt, z.all_tok)), 0)
        column = jnp.sum(seen.astype(jnp.float32), axis=1, keepdims=True)
        lens[p] = jnp.concatenate([column] * z.group, axis=0)

    def owner_of(p):
        return t_other if p == 0 else t

    for p in range(2):
        column_of_lengths(p)
    pl.semaphore_wait(barrier, 8)

    sent = []

    def send(copy):
        copy.start()
        sent.append(copy)

    def send_queries(k, s_to, t_to):
        for n, (src, dst) in enumerate(query_parts(s_to, t_to)):
            send(pltpu.make_async_remote_copy(
                src_ref=src, dst_ref=dst, send_sem=q_send.at[n, k],
                recv_sem=q_recv.at[n, my_slot], device_id={"seq": s_to, "tp": t_to},
                device_id_type=MESH,
            ))

    half = z.block // 2
    my_rows = pl.ds(pl.multiple_of(r * half, half), half)
    other_rows = pl.ds(pl.multiple_of(partner * half, half), half)
    send_queries(0, s, t_other)
    for k, s_to in enumerate((far_end, mate, far_mid)):
        send_queries(2 * k + 2, s_to, t)
        send_queries(2 * k + 3, s_to, t_other)
        thin = pl.ds(pl.multiple_of(s_to * z.kb, 128), z.kb)
        for n, (src, dst) in enumerate(((k_hbm, kbuf), (v_hbm, vbuf))):
            send(pltpu.make_async_remote_copy(
                src_ref=src.at[my_rows, thin], dst_ref=dst.at[s, my_rows, :],
                send_sem=kv_send.at[n, k], recv_sem=kv_recv.at[n, s],
                device_id={"seq": s_to}, device_id_type=MESH,
            ))

    for slot in range(8):
        for n, buf in enumerate((qbuf, fkbuf, fvbuf)):
            pltpu.make_async_copy(buf.at[slot], buf.at[slot], q_recv.at[n, slot]).wait()

    def rows_of(buf, p, first):
        some = pl.ds(owner_of(p) * z.ps, z.ps)
        value = buf[some, :, first:first + HEAD_WIDTH].astype(jnp.float32)
        return value.reshape(z.pt, HEAD_WIDTH)

    for p in range(2):
        for h in range(z.kl):
            own_key = rows_of(fkbuf, p, h * HEAD_WIDTH)
            own_value = rows_of(fvbuf, p, h * HEAD_WIDTH)
            for g in range(z.group):
                query = rows_of(qbuf, p, (h * z.group + g) * HEAD_WIDTH)
                span = slice(g * z.pt, (g + 1) * z.pt)
                qs[p, h, span, :] = query.astype(jnp.bfloat16)
                peak[p, h, span, :] = jnp.sum(query * own_key, axis=1, keepdims=True) * scale
                total[p, h, span, :] = jnp.ones((z.pt, 1), jnp.float32)
                acc[p, h, span, :] = own_value

    def attend(p, source):
        for h in range(z.kl):
            at = slice(h * HEAD_WIDTH, (h + 1) * HEAD_WIDTH)
            keys, values = kbuf[source, :, at], vbuf[source, :, at]
            scores = lax.dot_general(
                qs[p, h], keys, (((1,), (1,)), ((), ())), preferred_element_type=jnp.float32
            ) * scale
            spot = lax.broadcasted_iota(jnp.int32, scores.shape, 1) + source * z.block
            scores = jnp.where(spot.astype(jnp.float32) < lens[p], scores, MASKED)
            before = peak[p, h]
            now = jnp.maximum(before, jnp.max(scores, axis=1, keepdims=True))
            fade = jnp.exp(before - now)
            part = jnp.exp(scores - now)
            peak[p, h] = now
            total[p, h] = total[p, h] * fade + jnp.sum(part, axis=1, keepdims=True)
            acc[p, h] = acc[p, h] * fade + jnp.dot(
                part.astype(jnp.bfloat16), values, preferred_element_type=jnp.float32
            )

    def receive_kv(j, source):
        passed = []
        for n, buf in enumerate((kbuf, vbuf)):
            mine = buf.at[source, my_rows, :]
            pltpu.make_async_copy(mine, mine, kv_recv.at[n, source]).wait()
            passed.append(pltpu.make_async_remote_copy(
                src_ref=mine, dst_ref=mine, send_sem=f_send.at[n, j], recv_sem=f_recv.at[n, source],
                device_id={"rep": partner}, device_id_type=MESH,
            ))
            passed[-1].start()
        for n, buf in enumerate((kbuf, vbuf)):
            theirs = buf.at[source, other_rows, :]
            pltpu.make_async_copy(theirs, theirs, f_recv.at[n, source]).wait()
        return passed

    def finish(p):
        for h in range(z.kl):
            context = (acc[p, h] / total[p, h]).astype(jnp.bfloat16)
            for g in range(z.group):
                at = (h * z.group + g) * HEAD_WIDTH
                cbuf[s, p, :, at:at + HEAD_WIDTH] = context[g * z.pt:(g + 1) * z.pt, :]
        for k, s_to in enumerate((far_mid, mate)):
            pltpu.make_async_remote_copy(
                src_ref=cbuf.at[s, p], dst_ref=cbuf.at[s, p],
                send_sem=c_send.at[k, p], recv_sem=c_recv.at[s, p],
                device_id={"seq": s_to}, device_id_type=MESH,
            ).start()

    def landed(source, p):
        pltpu.make_async_copy(cbuf.at[source, p], cbuf.at[source, p], c_recv.at[source, p]).wait()

    def pass_on(k, source, p):
        return pltpu.make_async_remote_copy(
            src_ref=cbuf.at[source, p], dst_ref=cbuf.at[source, p],
            send_sem=c_send.at[k, p], recv_sem=c_recv.at[source, p],
            device_id={"seq": mate}, device_id_type=MESH,
        )

    spans = [slice(n * z.tile, (n + 1) * z.tile) for n in range(z.tiles)]

    def project_all(source, first):
        for at in spans:
            value = jnp.dot(
                cbuf[source].reshape(2 * z.pt, z.fb), wbuf[source, :, at], preferred_element_type=jnp.float32
            )
            oacc[:, at] = value if first else oacc[:, at] + value

    def project_half(source, p, at):
        return oacc[p * z.pt:(p + 1) * z.pt, at] + jnp.dot(
            cbuf[source, p], wbuf[source, :, at], preferred_element_type=jnp.float32
        )

    for copy in own_kv:
        copy.wait()
    for p in range(2):
        attend(p, s)
    sources = (
        jnp.where(is_end, far_end, mate), jnp.where(is_end, far_mid, far_end), jnp.where(is_end, mate, far_mid)
    )
    for j in range(2):
        sent.extend(receive_kv(j, sources[j]))
        for p in range(2):
            attend(p, sources[j])

    for copy in weights:
        copy.wait()

    @pl.when(jnp.logical_not(is_end))
    def _():
        for p in range(2):
            landed(mate, p)
        project_all(mate, True)
        for p in range(2):
            landed(far_end, p)
            pass_on(2, far_end, p).start()
        project_all(far_end, False)

    sent.extend(receive_kv(2, sources[2]))
    for p in range(2):
        attend(p, sources[2])
        finish(p)

    @pl.when(is_end)
    def _():
        project_all(s, True)
        for p in range(2):
            landed(far_end, p)
        project_all(far_end, False)

    third = jnp.where(is_end, mate, s)
    for p in range(2):
        @pl.when(is_end)
        def _():
            landed(mate, p)
        for at in spans:
            oacc[p * z.pt:(p + 1) * z.pt, at] = project_half(third, p, at)
        landed(far_mid, p)

        @pl.when(jnp.logical_not(is_end))
        def _():
            pass_on(3, far_mid, p).start()
        for n, at in enumerate(spans):
            value = project_half(far_mid, p, at)
            if p == 0:
                osend[0, n] = value.astype(jnp.bfloat16)
                send(pltpu.make_async_remote_copy(
                    src_ref=osend.at[0, n], dst_ref=orecv.at[0, n],
                    send_sem=o_send.at[0, n], recv_sem=o_recv.at[0, n],
                    device_id={"tp": t_other}, device_id_type=MESH,
                ))
            else:
                pltpu.make_async_copy(orecv.at[0, n], orecv.at[0, n], o_recv.at[0, n]).wait()
                out_ref[0, :, at] = (value + orecv[0, n].astype(jnp.float32)).astype(jnp.bfloat16)
    for copy in sent:
        copy.wait_send()
    for p in range(2):
        for k in range(2):
            pltpu.make_async_remote_copy(
                src_ref=cbuf.at[s, p], dst_ref=cbuf.at[s, p],
                send_sem=c_send.at[k, p], recv_sem=c_recv.at[s, p],
                device_id={"seq": mate}, device_id_type=MESH,
            ).wait_send()

        @pl.when(jnp.logical_not(is_end))
        def _():
            pass_on(2, far_end, p).wait_send()
            pass_on(3, far_mid, p).wait_send()


def shards(mesh_shape, *args):
    queries, fresh_key_rows, fresh_value_rows, visible, prefix_keys, cached_value_rows, out_weight = args
    z = Sizes(mesh_shape, queries, visible, prefix_keys, out_weight)
    staged = z.seq == 4 and z.tp == 2 and z.rep == 2 and z.b == 1
    bf16, f32 = jnp.bfloat16, jnp.float32
    vmem, dma = pltpu.VMEM, pltpu.SemaphoreType.DMA
    anywhere = pl.BlockSpec(memory_space=pl.ANY)
    inside = pl.BlockSpec(memory_space=pltpu.VMEM)
    return pl.pallas_call(
        functools.partial(line_kernel if staged else kernel, z),
        out_shape=jax.ShapeDtypeStruct((1, z.no, z.cols), bf16),
        in_specs=[anywhere, anywhere, anywhere, inside, anywhere, anywhere, anywhere],
        out_specs=inside,
        scratch_shapes=[
            vmem((z.slots, z.tok, z.fb), bf16),
            vmem((z.slots, z.tok, z.kb), bf16),
            vmem((z.slots, z.tok, z.kb), bf16),
            vmem((z.seq, z.block, z.kb), bf16),
            vmem((z.seq, z.block, z.kb), bf16),
            vmem((z.a, z.fb, z.cols), bf16),
            vmem((z.np, z.kl, z.rows, HEAD_WIDTH), bf16),
            vmem((z.np, z.rows, 1), f32),
            vmem((z.np, z.kl, z.rows, 1), f32),
            vmem((z.np, z.kl, z.rows, 1), f32),
            vmem((z.np, z.kl, z.rows, HEAD_WIDTH), f32),
            vmem((z.seq, z.np, z.pt, z.fb), bf16),
            vmem((z.all_tok, z.cols), f32),
            vmem((z.tp, z.tiles, z.no, z.tile), bf16),
            vmem((z.tp, z.tiles, z.no, z.tile), bf16),
            dma((3, z.slots)), dma((3, z.slots)),
            dma((2, z.seq)), dma((2, z.seq)),
            dma((2, z.seq)), dma((2, z.seq)),
            dma((2,)), dma((z.a,)),
            dma((z.seq, z.np)), dma((z.seq, z.np)),
            dma((z.tp, z.tiles)), dma((z.tp, z.tiles)),
        ],
        compiler_params=pltpu.CompilerParams(
            collective_id=0, has_side_effects=True, vmem_limit_bytes=56 * 1024 * 1024
        ),
        name="attend_and_project",
    )(*args)


def solution(mesh):
    in_specs = (
        P("rep", ("groups", "seq", "tp"), None),
        P("rep", ("groups", "seq", "tp"), None),
        P("rep", ("groups", "seq", "tp"), None),
        P("rep", "groups"),
        P(("groups", "seq"), "tp"),
        P(("groups", "seq"), "tp"),
        P("tp", "seq"),
    )
    out_specs = P("rep", ("groups", "tp"), "seq")
    body = functools.partial(shards, dict(mesh.shape))
    return jax.shard_map(body, mesh=mesh, in_specs=in_specs, out_specs=out_specs, check_vma=False)
```

```python
import functools
import math

import jax
import jax.numpy as jnp
from jax import lax
from jax.experimental import pallas as pl
from jax.experimental.pallas import tpu as pltpu
from jax.sharding import PartitionSpec as P

HEAD_WIDTH = 128
MASKED = -1e30
MESH = pl.DeviceIdType.MESH


class Sizes:
    def __init__(self, mesh_shape, queries, visible, prefix_keys, out_weight):
        self.seq = mesh_shape["seq"]
        self.tp = mesh_shape["tp"]
        self.rep = mesh_shape["rep"]
        self.tok = queries.shape[1]
        self.all_tok = visible.shape[1]
        self.block = prefix_keys.shape[0]
        kv_heads = prefix_keys.shape[1] // HEAD_WIDTH
        self.features, self.cols = out_weight.shape
        self.group = self.features // (kv_heads * HEAD_WIDTH)
        self.a = self.seq if kv_heads % self.seq == 0 else 1
        self.b = self.seq // self.a
        self.kl = kv_heads // self.a
        self.slots = self.a * self.tp
        self.nt = self.slots * self.tok
        self.np = self.tp if self.b == 1 else 1
        self.pt = self.nt // self.np
        self.ps = self.slots // self.np
        self.fb = self.kl * self.group * HEAD_WIDTH
        self.kb = self.kl * HEAD_WIDTH
        self.rows = self.group * self.pt
        self.no = self.all_tok // self.tp
        self.tile = math.gcd(self.cols, 512)
        self.tiles = self.cols // self.tile


def kernel(
    z, q_hbm, fk_hbm, fv_hbm, vis_ref, k_hbm, v_hbm, w_hbm, out_ref,
    qbuf, fkbuf, fvbuf, kbuf, vbuf, wbuf, qs, lens, peak, total, acc, cbuf, oacc, osend, orecv,
    q_send, q_recv, kv_send, kv_recv, f_send, f_recv, kv_own, w_sem, c_send, c_recv, o_send, o_recv,
):
    s, t, r = lax.axis_index("seq"), lax.axis_index("tp"), lax.axis_index("rep")
    partner = lax.rem(r + 1, z.rep)
    scale = 1.0 / math.sqrt(HEAD_WIDTH)

    def near(base, step, size):
        return lax.rem(base + step, size)

    def head_of(index):
        return index if z.a > 1 else 0

    barrier = pltpu.get_barrier_semaphore()
    for j in range(z.seq):
        for i in range(z.tp):
            if i or j:
                pl.semaphore_signal(
                    barrier, inc=1, device_id={"seq": near(s, j, z.seq), "tp": near(t, i, z.tp)},
                    device_id_type=MESH,
                )
    pl.semaphore_signal(barrier, inc=1, device_id={"rep": partner}, device_id_type=MESH)

    my_slot = head_of(s) * z.tp + t

    def query_parts(s_to, t_to):
        head = t_to * z.a + head_of(s_to)
        wide = pl.ds(pl.multiple_of(head * z.fb, 128), z.fb)
        thin = pl.ds(pl.multiple_of(head * z.kb, 128), z.kb)
        return (
            (q_hbm.at[0, :, wide], qbuf.at[my_slot]),
            (fk_hbm.at[0, :, thin], fkbuf.at[my_slot]),
            (fv_hbm.at[0, :, thin], fvbuf.at[my_slot]),
        )

    own_parts = [
        pltpu.make_async_copy(src, dst, q_recv.at[n, my_slot])
        for n, (src, dst) in enumerate(query_parts(s, t))
    ]
    thin_own = pl.ds(pl.multiple_of(head_of(s) * z.kb, 128), z.kb)
    own_kv = [
        pltpu.make_async_copy(k_hbm.at[:, thin_own], kbuf.at[s], kv_own.at[0]),
        pltpu.make_async_copy(v_hbm.at[:, thin_own], vbuf.at[s], kv_own.at[1]),
    ]
    weights = [
        pltpu.make_async_copy(w_hbm.at[pl.ds(n * z.fb, z.fb), :], wbuf.at[n], w_sem.at[n])
        for n in range(z.a)
    ]
    for copy in own_parts + own_kv + weights:
        copy.start()
    pl.semaphore_wait(barrier, z.seq * z.tp)

    sent, sent_if = [], []

    def send(copy, s_to=None):
        if s_to is None:
            copy.start()
            sent.append(copy)
        else:
            pl.when(s != s_to)(copy.start)
            sent_if.append((s_to, copy))

    def send_queries(s_to, t_step, only_if):
        t_to = near(t, t_step, z.tp)
        slot = (s_to if z.a > 1 else 0) * z.tp + t_step
        for n, (src, dst) in enumerate(query_parts(s_to, t_to)):
            send(pltpu.make_async_remote_copy(
                src_ref=src, dst_ref=dst, send_sem=q_send.at[n, slot],
                recv_sem=q_recv.at[n, my_slot], device_id={"seq": s_to, "tp": t_to},
                device_id_type=MESH,
            ), s_to if only_if else None)

    half = z.block // z.rep
    my_rows = pl.ds(pl.multiple_of(r * half, half), half)
    if z.a == 1:
        for i in range(1, z.tp):
            send_queries(s, i, False)
    for s_to in sorted(range(z.seq), key=lambda n: abs(2 * n + 1 - z.seq)):
        if z.a > 1:
            for i in range(z.tp):
                send_queries(s_to, i, i == 0)
        thin = pl.ds(head_of(s_to) * z.kb, z.kb)
        for n, (src, dst) in enumerate(((k_hbm, kbuf), (v_hbm, vbuf))):
            send(pltpu.make_async_remote_copy(
                src_ref=src.at[my_rows, thin], dst_ref=dst.at[s, my_rows, :],
                send_sem=kv_send.at[n, s_to], recv_sem=kv_recv.at[n, s],
                device_id={"seq": s_to}, device_id_type=MESH,
            ), s_to)

    def nearest(k):
        flip = s // (z.seq // 2) if z.seq > 1 else 0
        edge = s + flip * (z.seq - 1 - 2 * s)
        both = k <= 2 * edge
        away = jnp.where(both, (k + 1) // 2 * (1 - 2 * (k % 2)), k - edge)
        return s + away * (1 - 2 * flip)

    def owner_of(p):
        return near(t, p + 1, z.tp) if z.np > 1 else 0

    for p in range(z.np):
        want = lax.broadcasted_iota(jnp.int32, (z.pt, z.all_tok), 0) + owner_of(p) * z.pt
        if z.b > 1:
            want = want + s * z.nt
        have = lax.broadcasted_iota(jnp.int32, (z.pt, z.all_tok), 1)
        seen = jnp.where(want == have, jnp.broadcast_to(vis_ref[...], (z.pt, z.all_tok)), 0)
        column = jnp.sum(seen.astype(jnp.float32), axis=1, keepdims=True)
        lens[p] = jnp.concatenate([column] * z.group, axis=0)

    for j in range(z.a):
        for i in range(z.tp):
            slot = (near(s, j, z.seq) if z.a > 1 else 0) * z.tp + near(t, i, z.tp)
            for n, buf in enumerate((qbuf, fkbuf, fvbuf)):
                pltpu.make_async_copy(buf.at[slot], buf.at[slot], q_recv.at[n, slot]).wait()

    def rows_of(buf, p, first):
        some = pl.ds(owner_of(p) * z.ps, z.ps)
        value = buf[some, :, first:first + HEAD_WIDTH].astype(jnp.float32)
        return value.reshape(z.pt, HEAD_WIDTH)

    for p in range(z.np):
        for h in range(z.kl):
            own_key = rows_of(fkbuf, p, h * HEAD_WIDTH)
            own_value = rows_of(fvbuf, p, h * HEAD_WIDTH)
            for g in range(z.group):
                query = rows_of(qbuf, p, (h * z.group + g) * HEAD_WIDTH)
                span = slice(g * z.pt, (g + 1) * z.pt)
                qs[p, h, span, :] = query.astype(jnp.bfloat16)
                peak[p, h, span, :] = jnp.sum(query * own_key, axis=1, keepdims=True) * scale
                total[p, h, span, :] = jnp.ones((z.pt, 1), jnp.float32)
                acc[p, h, span, :] = own_value

    def attend(p, source):
        for h in range(z.kl):
            at = slice(h * HEAD_WIDTH, (h + 1) * HEAD_WIDTH)
            keys, values = kbuf[source, :, at], vbuf[source, :, at]
            scores = lax.dot_general(
                qs[p, h], keys, (((1,), (1,)), ((), ())), preferred_element_type=jnp.float32
            ) * scale
            spot = lax.broadcasted_iota(jnp.int32, scores.shape, 1) + source * z.block
            scores = jnp.where(spot.astype(jnp.float32) < lens[p], scores, MASKED)
            before = peak[p, h]
            now = jnp.maximum(before, jnp.max(scores, axis=1, keepdims=True))
            fade = jnp.exp(before - now)
            part = jnp.exp(scores - now)
            peak[p, h] = now
            total[p, h] = total[p, h] * fade + jnp.sum(part, axis=1, keepdims=True)
            acc[p, h] = acc[p, h] * fade + jnp.dot(
                part.astype(jnp.bfloat16), values, preferred_element_type=jnp.float32
            )

    def finish(p):
        for h in range(z.kl):
            context = (acc[p, h] / total[p, h]).astype(jnp.bfloat16)
            for g in range(z.group):
                at = (h * z.group + g) * HEAD_WIDTH
                cbuf[s, p, :, at:at + HEAD_WIDTH] = context[g * z.pt:(g + 1) * z.pt, :]
        for j in range(1, z.seq):
            sent.append(pltpu.make_async_remote_copy(
                src_ref=cbuf.at[s, p], dst_ref=cbuf.at[s, p],
                send_sem=c_send.at[j, p], recv_sem=c_recv.at[s, p],
                device_id={"seq": near(s, j, z.seq)}, device_id_type=MESH,
            ))
            sent[-1].start()

    for j in range(z.seq):
        source = nearest(j) if j else s
        if j == 0:
            for copy in own_kv:
                copy.wait()
        else:
            passed = []
            for n, buf in enumerate((kbuf, vbuf)):
                mine = buf.at[source, my_rows, :]
                pltpu.make_async_copy(mine, mine, kv_recv.at[n, source]).wait()
                passed.append(pltpu.make_async_remote_copy(
                    src_ref=mine, dst_ref=mine, send_sem=f_send.at[n, j], recv_sem=f_recv.at[n, source],
                    device_id={"rep": partner}, device_id_type=MESH,
                ))
                passed[-1].start()
            other = pl.ds(pl.multiple_of(partner * half, half), half)
            for n, buf in enumerate((kbuf, vbuf)):
                theirs = buf.at[source, other, :]
                pltpu.make_async_copy(theirs, theirs, f_recv.at[n, source]).wait()
            sent.extend(passed)
        for p in range(z.np):
            attend(p, source)
            if j == z.seq - 1:
                finish(p)

    for copy in weights:
        copy.wait()

    def project(j, source, p, at):
        value = jnp.dot(
            cbuf[source, p], wbuf[head_of(source), :, at], preferred_element_type=jnp.float32
        )
        if z.b > 1:
            oacc[pl.ds(pl.multiple_of(source * z.nt, z.nt), z.nt), at] = value
            return value
        rows = slice(p * z.pt, (p + 1) * z.pt)
        if j:
            value = value + oacc[rows, at]
        if j < z.seq - 1:
            oacc[rows, at] = value
        return value

    def give(i, n, value):
        osend[i, n] = value.astype(jnp.bfloat16)
        sent.append(pltpu.make_async_remote_copy(
            src_ref=osend.at[i, n], dst_ref=orecv.at[i, n],
            send_sem=o_send.at[i, n], recv_sem=o_recv.at[i, n],
            device_id={"tp": near(t, i + 1, z.tp)}, device_id_type=MESH,
        ))
        sent[-1].start()

    def keep(n, at, value):
        for i in range(z.tp - 1):
            pltpu.make_async_copy(orecv.at[i, n], orecv.at[i, n], o_recv.at[i, n]).wait()
            value = value + orecv[i, n].astype(jnp.float32)
        out_ref[0, :, at] = value.astype(jnp.bfloat16)

    spans = [slice(n * z.tile, (n + 1) * z.tile) for n in range(z.tiles)]
    for p in range(z.np):
        for j in range(z.seq):
            source = nearest(j) if j else s
            if j:
                landed = cbuf.at[source, p]
                pltpu.make_async_copy(landed, landed, c_recv.at[source, p]).wait()
            for n, at in enumerate(spans):
                value = project(j, source, p, at)
                if z.b == 1 and j == z.seq - 1:
                    if p < z.np - 1:
                        give(p, n, value)
                    else:
                        keep(n, at, value)
    if z.b > 1:
        for n, at in enumerate(spans):
            for i in range(z.tp - 1):
                rows = pl.ds(pl.multiple_of(near(t, i + 1, z.tp) * z.no, z.no), z.no)
                give(i, n, oacc[rows, at])
        for n, at in enumerate(spans):
            keep(n, at, oacc[pl.ds(pl.multiple_of(t * z.no, z.no), z.no), at])
    for copy in sent:
        copy.wait_send()
    for s_to, copy in sent_if:
        pl.when(s != s_to)(copy.wait_send)


def line_kernel(
    z, q_hbm, fk_hbm, fv_hbm, vis_ref, k_hbm, v_hbm, w_hbm, out_ref,
    qbuf, fkbuf, fvbuf, kbuf, vbuf, wbuf, qs, lens, peak, acc, cbuf, oacc, osend, orecv,
    q_send, q_recv, kv_send, kv_recv, f_send, f_recv, kv_own, w_sem, c_send, c_recv, o_send, o_recv,
):
    s, t, r = lax.axis_index("seq"), lax.axis_index("tp"), lax.axis_index("rep")
    partner, t_other = 1 - r, 1 - t
    log_scale = math.log2(math.e) / math.sqrt(HEAD_WIDTH)
    low = s < 2
    is_end = (s == 0) | (s == 3)
    mate = s + 1 - 2 * lax.rem(s, 2)
    far_end = jnp.where(low, 3, 0)
    far_mid = jnp.where(low, 2, 1)

    barrier = pltpu.get_barrier_semaphore()
    for j in range(4):
        for i in range(2):
            if i or j:
                pl.semaphore_signal(
                    barrier, inc=1, device_id={"seq": lax.rem(s + j, 4), "tp": lax.rem(t + i, 2)},
                    device_id_type=MESH,
                )
    pl.semaphore_signal(barrier, inc=1, device_id={"rep": partner}, device_id_type=MESH)

    my_slot = s * 2 + t

    def query_parts(s_to, t_to):
        head = t_to * 4 + s_to
        wide = pl.ds(pl.multiple_of(head * z.fb, 128), z.fb)
        thin = pl.ds(pl.multiple_of(head * z.kb, 128), z.kb)
        return (
            (q_hbm.at[0, :, wide], qbuf.at[my_slot]),
            (fk_hbm.at[0, :, thin], fkbuf.at[my_slot]),
            (fv_hbm.at[0, :, thin], fvbuf.at[my_slot]),
        )

    own_parts = [
        pltpu.make_async_copy(src, dst, q_recv.at[n, my_slot])
        for n, (src, dst) in enumerate(query_parts(s, t))
    ]
    thin_own = pl.ds(pl.multiple_of(s * z.kb, 128), z.kb)
    own_kv = [
        pltpu.make_async_copy(k_hbm.at[:, thin_own], kbuf.at[s], kv_own.at[0]),
        pltpu.make_async_copy(v_hbm.at[:, thin_own], vbuf.at[s, :, 0:HEAD_WIDTH], kv_own.at[1]),
    ]
    weights = [
        pltpu.make_async_copy(w_hbm.at[pl.ds(n * z.fb, z.fb), :], wbuf.at[n], w_sem.at[n])
        for n in range(4)
    ]
    for copy in own_parts + own_kv + weights:
        copy.start()

    def column_of_lengths(p):
        want = lax.broadcasted_iota(jnp.int32, (z.pt, z.all_tok), 0) + owner_of(p) * z.pt
        have = lax.broadcasted_iota(jnp.int32, (z.pt, z.all_tok), 1)
        seen = jnp.where(want == have, jnp.broadcast_to(vis_ref[...], (z.pt, z.all_tok)), 0)
        column = jnp.sum(seen.astype(jnp.float32), axis=1, keepdims=True)
        lens[p] = jnp.broadcast_to(jnp.concatenate([column] * z.group, axis=0), (z.rows, HEAD_WIDTH))

    def owner_of(p):
        return t_other if p == 0 else t

    for p in range(2):
        column_of_lengths(p)
    head_lanes = slice(0, HEAD_WIDTH)
    vbuf[:, :, HEAD_WIDTH:] = jnp.ones((4, z.block, HEAD_WIDTH), jnp.bfloat16)
    pl.semaphore_wait(barrier, 8)

    sent = []

    def send(copy):
        copy.start()
        sent.append(copy)

    def query_copies(k, s_to, t_to):
        return [
            pltpu.make_async_remote_copy(
                src_ref=src, dst_ref=dst, send_sem=q_send.at[n, k],
                recv_sem=q_recv.at[n, my_slot], device_id={"seq": s_to, "tp": t_to},
                device_id_type=MESH,
            )
            for n, (src, dst) in enumerate(query_parts(s_to, t_to))
        ]

    half = z.block // 2
    my_rows = pl.ds(pl.multiple_of(r * half, half), half)
    other_rows = pl.ds(pl.multiple_of(partner * half, half), half)

    def prefix_copies(k, s_to):
        thin = pl.ds(pl.multiple_of(s_to * z.kb, 128), z.kb)
        return [
            pltpu.make_async_remote_copy(
                src_ref=src.at[my_rows, thin], dst_ref=dst.at[s, my_rows, 0:HEAD_WIDTH],
                send_sem=kv_send.at[n, k], recv_sem=kv_recv.at[n, s],
                device_id={"seq": s_to}, device_id_type=MESH,
            )
            for n, (src, dst) in enumerate(((k_hbm, kbuf), (v_hbm, vbuf)))
        ]

    targets = (far_end, far_mid, mate)
    queries = [query_copies(2 * k + 2, s_to, t) + query_copies(2 * k + 3, s_to, t_other) for k, s_to in enumerate(targets)]
    prefix = [prefix_copies(k, s_to) for k, s_to in enumerate(targets)]
    for copy in query_copies(0, s, t_other) + queries[0]:
        send(copy)

    @pl.when(is_end)
    def _():
        for copy in prefix[0] + queries[1]:
            copy.start()

    @pl.when(jnp.logical_not(is_end))
    def _():
        for copy in queries[1] + prefix[0]:
            copy.start()

    for copy in queries[2] + prefix[2] + prefix[1]:
        send(copy)
    sent.extend(prefix[0] + queries[1])

    for slot in range(8):
        for n, buf in enumerate((qbuf, fkbuf, fvbuf)):
            pltpu.make_async_copy(buf.at[slot], buf.at[slot], q_recv.at[n, slot]).wait()

    def rows_of(buf, p, first):
        some = pl.ds(owner_of(p) * z.ps, z.ps)
        value = buf[some, :, first:first + HEAD_WIDTH].astype(jnp.float32)
        return value.reshape(z.pt, HEAD_WIDTH)

    for p in range(2):
        own_key, own_value = rows_of(fkbuf, p, 0), rows_of(fvbuf, p, 0)
        for g in range(z.group):
            query = rows_of(qbuf, p, g * HEAD_WIDTH)
            span = slice(g * z.pt, (g + 1) * z.pt)
            qs[p, span, :] = query.astype(jnp.bfloat16)
            own = jnp.sum(query * own_key, axis=1, keepdims=True)
            peak[p, span, :] = jnp.broadcast_to(own, (z.pt, HEAD_WIDTH))
            acc[p, span, head_lanes] = own_value
            acc[p, span, HEAD_WIDTH:] = jnp.ones((z.pt, HEAD_WIDTH), jnp.float32)

    def attend(p, source, first=0, count=None):
        count = count or z.block
        repeat = count // HEAD_WIDTH
        rows = pl.ds(first if isinstance(first, int) else pl.multiple_of(first, half), count)
        scores = lax.dot_general(
            qs[p], kbuf[source, rows, :], (((1,), (1,)), ((), ())), preferred_element_type=jnp.float32
        )
        spot = lax.broadcasted_iota(jnp.int32, scores.shape, 1).astype(jnp.float32)
        left = lens[p] - (source * z.block + first).astype(jnp.float32)
        scores = jnp.where(spot < jnp.concatenate([left] * repeat, axis=1), scores, MASKED)
        before = peak[p]
        now = jnp.maximum(before, jnp.broadcast_to(jnp.max(scores, axis=1, keepdims=True), before.shape))
        fade = jnp.exp2((before - now) * log_scale)
        part = jnp.exp2((scores - jnp.concatenate([now] * repeat, axis=1)) * log_scale)
        peak[p] = now
        acc[p] = acc[p] * jnp.concatenate([fade] * 2, axis=1) + jnp.dot(
            part.astype(jnp.bfloat16), vbuf[source, rows, :], preferred_element_type=jnp.float32
        )

    def pass_kv(j, source):
        passed = []
        for n, buf in enumerate((kbuf, vbuf)):
            mine = buf.at[source, my_rows, 0:HEAD_WIDTH]
            pltpu.make_async_copy(mine, mine, kv_recv.at[n, source]).wait()
            passed.append(pltpu.make_async_remote_copy(
                src_ref=mine, dst_ref=mine, send_sem=f_send.at[n, j], recv_sem=f_recv.at[n, source],
                device_id={"rep": partner}, device_id_type=MESH,
            ))
            passed[-1].start()
        return passed

    def passed_kv(source):
        for n, buf in enumerate((kbuf, vbuf)):
            theirs = buf.at[source, other_rows, 0:HEAD_WIDTH]
            pltpu.make_async_copy(theirs, theirs, f_recv.at[n, source]).wait()

    def finish(p):
        context = (acc[p, :, head_lanes] / acc[p, :, HEAD_WIDTH:]).astype(jnp.bfloat16)
        for g in range(z.group):
            cbuf[s, p, :, g * HEAD_WIDTH:(g + 1) * HEAD_WIDTH] = context[g * z.pt:(g + 1) * z.pt, :]
        for k, s_to in enumerate((far_end, mate)):
            send(context_copy(k, s, p, s_to))

        @pl.when(jnp.logical_not(is_end))
        def _():
            context_copy(2, s, p, far_mid).start()

    def context_copy(k, source, p, s_to):
        return pltpu.make_async_remote_copy(
            src_ref=cbuf.at[source, p], dst_ref=cbuf.at[source, p],
            send_sem=c_send.at[k, p], recv_sem=c_recv.at[source, p],
            device_id={"seq": s_to}, device_id_type=MESH,
        )

    def landed(source, p):
        pltpu.make_async_copy(cbuf.at[source, p], cbuf.at[source, p], c_recv.at[source, p]).wait()

    spans = [slice(n * z.tile, (n + 1) * z.tile) for n in range(z.tiles)]

    def project_all(source, first):
        for at in spans:
            value = jnp.dot(
                cbuf[source].reshape(2 * z.pt, z.fb), wbuf[source, :, at], preferred_element_type=jnp.float32
            )
            oacc[:, at] = value if first else oacc[:, at] + value

    def project_half(source, p, at):
        return oacc[p * z.pt:(p + 1) * z.pt, at] + jnp.dot(
            cbuf[source, p], wbuf[source, :, at], preferred_element_type=jnp.float32
        )

    for copy in own_kv:
        copy.wait()
    for p in range(2):
        attend(p, s)
    sources = (
        jnp.where(is_end, far_end, mate), jnp.where(is_end, far_mid, far_end), jnp.where(is_end, mate, far_mid)
    )
    for j in range(2):
        sent.extend(pass_kv(j, sources[j]))
        passed_kv(sources[j])
        for p in range(2):
            attend(p, sources[j])
    sent.extend(pass_kv(2, sources[2]))
    for p in range(2):
        attend(p, sources[2], r * half, half)
    passed_kv(sources[2])
    for p in range(2):
        attend(p, sources[2], partner * half, half)
        finish(p)

    for copy in weights:
        copy.wait()
    project_all(s, True)
    second = jnp.where(is_end, far_end, mate)
    for p in range(2):
        landed(second, p)

        @pl.when(is_end)
        def _():
            context_copy(2, far_end, p, mate).start()
    project_all(second, False)

    third = jnp.where(is_end, mate, far_end)
    for p in range(2):
        landed(third, p)
        for at in spans:
            oacc[p * z.pt:(p + 1) * z.pt, at] = project_half(third, p, at)
        landed(far_mid, p)
        for n, at in enumerate(spans):
            value = project_half(far_mid, p, at)
            if p == 0:
                osend[0, n] = value.astype(jnp.bfloat16)
                send(pltpu.make_async_remote_copy(
                    src_ref=osend.at[0, n], dst_ref=orecv.at[0, n],
                    send_sem=o_send.at[0, n], recv_sem=o_recv.at[0, n],
                    device_id={"tp": t_other}, device_id_type=MESH,
                ))
            else:
                pltpu.make_async_copy(orecv.at[0, n], orecv.at[0, n], o_recv.at[0, n]).wait()
                out_ref[0, :, at] = (value + orecv[0, n].astype(jnp.float32)).astype(jnp.bfloat16)
    for copy in sent:
        copy.wait_send()
    for p in range(2):
        context_copy(2, s, p, mate).wait_send()


def shards(mesh_shape, *args):
    queries, fresh_key_rows, fresh_value_rows, visible, prefix_keys, cached_value_rows, out_weight = args
    z = Sizes(mesh_shape, queries, visible, prefix_keys, out_weight)
    staged = z.seq == 4 and z.tp == 2 and z.rep == 2 and z.b == 1 and z.kl == 1
    bf16, f32 = jnp.bfloat16, jnp.float32
    vmem, dma = pltpu.VMEM, pltpu.SemaphoreType.DMA
    if staged:
        state = [
            vmem((2, z.rows, HEAD_WIDTH), bf16),
            vmem((2, z.rows, HEAD_WIDTH), f32),
            vmem((2, z.rows, HEAD_WIDTH), f32),
            vmem((2, z.rows, 2 * HEAD_WIDTH), f32),
        ]
    else:
        state = [
                vmem((z.np, z.kl, z.rows, HEAD_WIDTH), bf16),
                vmem((z.np, z.rows, 1), f32),
                vmem((z.np, z.kl, z.rows, 1), f32),
                vmem((z.np, z.kl, z.rows, 1), f32),
                vmem((z.np, z.kl, z.rows, HEAD_WIDTH), f32),
        ]
    anywhere = pl.BlockSpec(memory_space=pl.ANY)
    inside = pl.BlockSpec(memory_space=pltpu.VMEM)
    return pl.pallas_call(
        functools.partial(line_kernel if staged else kernel, z),
        out_shape=jax.ShapeDtypeStruct((1, z.no, z.cols), bf16),
        in_specs=[anywhere, anywhere, anywhere, inside, anywhere, anywhere, anywhere],
        out_specs=inside,
        scratch_shapes=[
            vmem((z.slots, z.tok, z.fb), bf16),
            vmem((z.slots, z.tok, z.kb), bf16),
            vmem((z.slots, z.tok, z.kb), bf16),
            vmem((z.seq, z.block, z.kb), bf16),
            vmem((z.seq, z.block, z.kb + staged * HEAD_WIDTH), bf16),
            vmem((z.a, z.fb, z.cols), bf16),
            *state,
            vmem((z.seq, z.np, z.pt, z.fb), bf16),
            vmem((z.all_tok, z.cols), f32),
            vmem((z.tp, z.tiles, z.no, z.tile), bf16),
            vmem((z.tp, z.tiles, z.no, z.tile), bf16),
            dma((3, z.slots)), dma((3, z.slots)),
            dma((2, z.seq)), dma((2, z.seq)),
            dma((2, z.seq)), dma((2, z.seq)),
            dma((2,)), dma((z.a,)),
            dma((z.seq, z.np)), dma((z.seq, z.np)),
            dma((z.tp, z.tiles)), dma((z.tp, z.tiles)),
        ],
        compiler_params=pltpu.CompilerParams(
            collective_id=0, has_side_effects=True, vmem_limit_bytes=56 * 1024 * 1024
        ),
        name="attend_and_project",
    )(*args)


def solution(mesh):
    in_specs = (
        P("rep", ("groups", "seq", "tp"), None),
        P("rep", ("groups", "seq", "tp"), None),
        P("rep", ("groups", "seq", "tp"), None),
        P("rep", "groups"),
        P(("groups", "seq"), "tp"),
        P(("groups", "seq"), "tp"),
        P("tp", "seq"),
    )
    out_specs = P("rep", ("groups", "tp"), "seq")
    body = functools.partial(shards, dict(mesh.shape))
    return jax.shard_map(body, mesh=mesh, in_specs=in_specs, out_specs=out_specs, check_vma=False)
```

```python
import functools
import math

import jax
import jax.numpy as jnp
from jax import lax
from jax.experimental import pallas as pl
from jax.experimental.pallas import tpu as pltpu
from jax.sharding import PartitionSpec as P

HEAD_WIDTH = 128
MASKED = -1e30
MESH = pl.DeviceIdType.MESH


class Sizes:
    def __init__(self, mesh_shape, queries, visible, prefix_keys, out_weight):
        self.seq = mesh_shape["seq"]
        self.tp = mesh_shape["tp"]
        self.rep = mesh_shape["rep"]
        self.tok = queries.shape[1]
        self.all_tok = visible.shape[1]
        self.block = prefix_keys.shape[0]
        kv_heads = prefix_keys.shape[1] // HEAD_WIDTH
        self.features, self.cols = out_weight.shape
        self.group = self.features // (kv_heads * HEAD_WIDTH)
        self.a = self.seq if kv_heads % self.seq == 0 else 1
        self.b = self.seq // self.a
        self.kl = kv_heads // self.a
        self.slots = self.a * self.tp
        self.nt = self.slots * self.tok
        self.np = self.tp if self.b == 1 else 1
        self.pt = self.nt // self.np
        self.ps = self.slots // self.np
        self.fb = self.kl * self.group * HEAD_WIDTH
        self.kb = self.kl * HEAD_WIDTH
        self.rows = self.group * self.pt
        self.no = self.all_tok // self.tp
        self.tile = math.gcd(self.cols, 512)
        self.tiles = self.cols // self.tile


def kernel(
    z, q_hbm, fk_hbm, fv_hbm, vis_ref, k_hbm, v_hbm, w_hbm, out_ref,
    qbuf, fkbuf, fvbuf, kbuf, vbuf, wbuf, qs, lens, peak, total, acc, cbuf, oacc, osend, orecv,
    q_send, q_recv, kv_send, kv_recv, f_send, f_recv, kv_own, w_sem, c_send, c_recv, o_send, o_recv,
):
    s, t, r = lax.axis_index("seq"), lax.axis_index("tp"), lax.axis_index("rep")
    partner = lax.rem(r + 1, z.rep)
    scale = 1.0 / math.sqrt(HEAD_WIDTH)

    def near(base, step, size):
        return lax.rem(base + step, size)

    def head_of(index):
        return index if z.a > 1 else 0

    barrier = pltpu.get_barrier_semaphore()
    for j in range(z.seq):
        for i in range(z.tp):
            if i or j:
                pl.semaphore_signal(
                    barrier, inc=1, device_id={"seq": near(s, j, z.seq), "tp": near(t, i, z.tp)},
                    device_id_type=MESH,
                )
    pl.semaphore_signal(barrier, inc=1, device_id={"rep": partner}, device_id_type=MESH)

    my_slot = head_of(s) * z.tp + t

    def query_parts(s_to, t_to):
        head = t_to * z.a + head_of(s_to)
        wide = pl.ds(pl.multiple_of(head * z.fb, 128), z.fb)
        thin = pl.ds(pl.multiple_of(head * z.kb, 128), z.kb)
        return (
            (q_hbm.at[0, :, wide], qbuf.at[my_slot]),
            (fk_hbm.at[0, :, thin], fkbuf.at[my_slot]),
            (fv_hbm.at[0, :, thin], fvbuf.at[my_slot]),
        )

    own_parts = [
        pltpu.make_async_copy(src, dst, q_recv.at[n, my_slot])
        for n, (src, dst) in enumerate(query_parts(s, t))
    ]
    thin_own = pl.ds(pl.multiple_of(head_of(s) * z.kb, 128), z.kb)
    own_kv = [
        pltpu.make_async_copy(k_hbm.at[:, thin_own], kbuf.at[s], kv_own.at[0]),
        pltpu.make_async_copy(v_hbm.at[:, thin_own], vbuf.at[s], kv_own.at[1]),
    ]
    weights = [
        pltpu.make_async_copy(w_hbm.at[pl.ds(n * z.fb, z.fb), :], wbuf.at[n], w_sem.at[n])
        for n in range(z.a)
    ]
    for copy in own_parts + own_kv + weights:
        copy.start()
    pl.semaphore_wait(barrier, z.seq * z.tp)

    sent, sent_if = [], []

    def send(copy, s_to=None):
        if s_to is None:
            copy.start()
            sent.append(copy)
        else:
            pl.when(s != s_to)(copy.start)
            sent_if.append((s_to, copy))

    def send_queries(s_to, t_step, only_if):
        t_to = near(t, t_step, z.tp)
        slot = (s_to if z.a > 1 else 0) * z.tp + t_step
        for n, (src, dst) in enumerate(query_parts(s_to, t_to)):
            send(pltpu.make_async_remote_copy(
                src_ref=src, dst_ref=dst, send_sem=q_send.at[n, slot],
                recv_sem=q_recv.at[n, my_slot], device_id={"seq": s_to, "tp": t_to},
                device_id_type=MESH,
            ), s_to if only_if else None)

    half = z.block // z.rep
    my_rows = pl.ds(pl.multiple_of(r * half, half), half)
    if z.a == 1:
        for i in range(1, z.tp):
            send_queries(s, i, False)
    for s_to in sorted(range(z.seq), key=lambda n: abs(2 * n + 1 - z.seq)):
        if z.a > 1:
            for i in range(z.tp):
                send_queries(s_to, i, i == 0)
        thin = pl.ds(head_of(s_to) * z.kb, z.kb)
        for n, (src, dst) in enumerate(((k_hbm, kbuf), (v_hbm, vbuf))):
            send(pltpu.make_async_remote_copy(
                src_ref=src.at[my_rows, thin], dst_ref=dst.at[s, my_rows, :],
                send_sem=kv_send.at[n, s_to], recv_sem=kv_recv.at[n, s],
                device_id={"seq": s_to}, device_id_type=MESH,
            ), s_to)

    def nearest(k):
        flip = s // (z.seq // 2) if z.seq > 1 else 0
        edge = s + flip * (z.seq - 1 - 2 * s)
        both = k <= 2 * edge
        away = jnp.where(both, (k + 1) // 2 * (1 - 2 * (k % 2)), k - edge)
        return s + away * (1 - 2 * flip)

    def owner_of(p):
        return near(t, p + 1, z.tp) if z.np > 1 else 0

    for p in range(z.np):
        want = lax.broadcasted_iota(jnp.int32, (z.pt, z.all_tok), 0) + owner_of(p) * z.pt
        if z.b > 1:
            want = want + s * z.nt
        have = lax.broadcasted_iota(jnp.int32, (z.pt, z.all_tok), 1)
        seen = jnp.where(want == have, jnp.broadcast_to(vis_ref[...], (z.pt, z.all_tok)), 0)
        column = jnp.sum(seen.astype(jnp.float32), axis=1, keepdims=True)
        lens[p] = jnp.concatenate([column] * z.group, axis=0)

    for j in range(z.a):
        for i in range(z.tp):
            slot = (near(s, j, z.seq) if z.a > 1 else 0) * z.tp + near(t, i, z.tp)
            for n, buf in enumerate((qbuf, fkbuf, fvbuf)):
                pltpu.make_async_copy(buf.at[slot], buf.at[slot], q_recv.at[n, slot]).wait()

    def rows_of(buf, p, first):
        some = pl.ds(owner_of(p) * z.ps, z.ps)
        value = buf[some, :, first:first + HEAD_WIDTH].astype(jnp.float32)
        return value.reshape(z.pt, HEAD_WIDTH)

    for p in range(z.np):
        for h in range(z.kl):
            own_key = rows_of(fkbuf, p, h * HEAD_WIDTH)
            own_value = rows_of(fvbuf, p, h * HEAD_WIDTH)
            for g in range(z.group):
                query = rows_of(qbuf, p, (h * z.group + g) * HEAD_WIDTH)
                span = slice(g * z.pt, (g + 1) * z.pt)
                qs[p, h, span, :] = query.astype(jnp.bfloat16)
                peak[p, h, span, :] = jnp.sum(query * own_key, axis=1, keepdims=True) * scale
                total[p, h, span, :] = jnp.ones((z.pt, 1), jnp.float32)
                acc[p, h, span, :] = own_value

    def attend(p, source):
        for h in range(z.kl):
            at = slice(h * HEAD_WIDTH, (h + 1) * HEAD_WIDTH)
            keys, values = kbuf[source, :, at], vbuf[source, :, at]
            scores = lax.dot_general(
                qs[p, h], keys, (((1,), (1,)), ((), ())), preferred_element_type=jnp.float32
            ) * scale
            spot = lax.broadcasted_iota(jnp.int32, scores.shape, 1) + source * z.block
            scores = jnp.where(spot.astype(jnp.float32) < lens[p], scores, MASKED)
            before = peak[p, h]
            now = jnp.maximum(before, jnp.max(scores, axis=1, keepdims=True))
            fade = jnp.exp(before - now)
            part = jnp.exp(scores - now)
            peak[p, h] = now
            total[p, h] = total[p, h] * fade + jnp.sum(part, axis=1, keepdims=True)
            acc[p, h] = acc[p, h] * fade + jnp.dot(
                part.astype(jnp.bfloat16), values, preferred_element_type=jnp.float32
            )

    def finish(p):
        for h in range(z.kl):
            context = (acc[p, h] / total[p, h]).astype(jnp.bfloat16)
            for g in range(z.group):
                at = (h * z.group + g) * HEAD_WIDTH
                cbuf[s, p, :, at:at + HEAD_WIDTH] = context[g * z.pt:(g + 1) * z.pt, :]
        for j in range(1, z.seq):
            sent.append(pltpu.make_async_remote_copy(
                src_ref=cbuf.at[s, p], dst_ref=cbuf.at[s, p],
                send_sem=c_send.at[j, p], recv_sem=c_recv.at[s, p],
                device_id={"seq": near(s, j, z.seq)}, device_id_type=MESH,
            ))
            sent[-1].start()

    for j in range(z.seq):
        source = nearest(j) if j else s
        if j == 0:
            for copy in own_kv:
                copy.wait()
        else:
            passed = []
            for n, buf in enumerate((kbuf, vbuf)):
                mine = buf.at[source, my_rows, :]
                pltpu.make_async_copy(mine, mine, kv_recv.at[n, source]).wait()
                passed.append(pltpu.make_async_remote_copy(
                    src_ref=mine, dst_ref=mine, send_sem=f_send.at[n, j], recv_sem=f_recv.at[n, source],
                    device_id={"rep": partner}, device_id_type=MESH,
                ))
                passed[-1].start()
            other = pl.ds(pl.multiple_of(partner * half, half), half)
            for n, buf in enumerate((kbuf, vbuf)):
                theirs = buf.at[source, other, :]
                pltpu.make_async_copy(theirs, theirs, f_recv.at[n, source]).wait()
            sent.extend(passed)
        for p in range(z.np):
            attend(p, source)
            if j == z.seq - 1:
                finish(p)

    for copy in weights:
        copy.wait()

    def project(j, source, p, at):
        value = jnp.dot(
            cbuf[source, p], wbuf[head_of(source), :, at], preferred_element_type=jnp.float32
        )
        if z.b > 1:
            oacc[pl.ds(pl.multiple_of(source * z.nt, z.nt), z.nt), at] = value
            return value
        rows = slice(p * z.pt, (p + 1) * z.pt)
        if j:
            value = value + oacc[rows, at]
        if j < z.seq - 1:
            oacc[rows, at] = value
        return value

    def give(i, n, value):
        osend[i, n] = value.astype(jnp.bfloat16)
        sent.append(pltpu.make_async_remote_copy(
            src_ref=osend.at[i, n], dst_ref=orecv.at[i, n],
            send_sem=o_send.at[i, n], recv_sem=o_recv.at[i, n],
            device_id={"tp": near(t, i + 1, z.tp)}, device_id_type=MESH,
        ))
        sent[-1].start()

    def keep(n, at, value):
        for i in range(z.tp - 1):
            pltpu.make_async_copy(orecv.at[i, n], orecv.at[i, n], o_recv.at[i, n]).wait()
            value = value + orecv[i, n].astype(jnp.float32)
        out_ref[0, :, at] = value.astype(jnp.bfloat16)

    spans = [slice(n * z.tile, (n + 1) * z.tile) for n in range(z.tiles)]
    for p in range(z.np):
        for j in range(z.seq):
            source = nearest(j) if j else s
            if j:
                landed = cbuf.at[source, p]
                pltpu.make_async_copy(landed, landed, c_recv.at[source, p]).wait()
            for n, at in enumerate(spans):
                value = project(j, source, p, at)
                if z.b == 1 and j == z.seq - 1:
                    if p < z.np - 1:
                        give(p, n, value)
                    else:
                        keep(n, at, value)
    if z.b > 1:
        for n, at in enumerate(spans):
            for i in range(z.tp - 1):
                rows = pl.ds(pl.multiple_of(near(t, i + 1, z.tp) * z.no, z.no), z.no)
                give(i, n, oacc[rows, at])
        for n, at in enumerate(spans):
            keep(n, at, oacc[pl.ds(pl.multiple_of(t * z.no, z.no), z.no), at])
    for copy in sent:
        copy.wait_send()
    for s_to, copy in sent_if:
        pl.when(s != s_to)(copy.wait_send)


def line_kernel(
    z, q_hbm, fk_hbm, fv_hbm, vis_hbm, k_hbm, v_hbm, w_hbm, out_ref,
    qbuf, fkbuf, fvbuf, kbuf, vbuf, wbuf, qs, lens, peak, acc, cbuf, oacc, osend, orecv,
    q_send, q_recv, kv_send, kv_recv, f_send, f_recv, kv_own, w_sem, c_send, c_recv, o_send, o_recv,
    vis_ref, vis_sem,
):
    s, t, r = lax.axis_index("seq"), lax.axis_index("tp"), lax.axis_index("rep")
    partner, t_other = 1 - r, 1 - t
    log_scale = math.log2(math.e) / math.sqrt(HEAD_WIDTH)
    low = s < 2
    is_end = (s == 0) | (s == 3)
    mate = s + 1 - 2 * lax.rem(s, 2)
    far_end = jnp.where(low, 3, 0)
    far_mid = jnp.where(low, 2, 1)

    barrier = pltpu.get_barrier_semaphore()
    for s_to, t_to in (
        (far_end, t), (far_mid, t), (far_end, t_other), (far_mid, t_other), (mate, t), (mate, t_other), (s, t_other)
    ):
        pl.semaphore_signal(barrier, inc=1, device_id={"seq": s_to, "tp": t_to}, device_id_type=MESH)
    pl.semaphore_signal(barrier, inc=1, device_id={"rep": partner}, device_id_type=MESH)

    my_slot = s * 2 + t

    def query_parts(s_to, t_to):
        head = t_to * 4 + s_to
        wide = pl.ds(pl.multiple_of(head * z.fb, 128), z.fb)
        thin = pl.ds(pl.multiple_of(head * z.kb, 128), z.kb)
        return (
            (q_hbm.at[0, :, wide], qbuf.at[my_slot]),
            (fk_hbm.at[0, :, thin], fkbuf.at[my_slot]),
            (fv_hbm.at[0, :, thin], fvbuf.at[my_slot]),
        )

    own_parts = [
        pltpu.make_async_copy(src, dst, q_recv.at[n, my_slot])
        for n, (src, dst) in enumerate(query_parts(s, t))
    ]
    thin_own = pl.ds(pl.multiple_of(s * z.kb, 128), z.kb)
    own_kv = [
        pltpu.make_async_copy(k_hbm.at[:, thin_own], kbuf.at[s], kv_own.at[0]),
        pltpu.make_async_copy(v_hbm.at[:, thin_own], vbuf.at[s, :, 0:HEAD_WIDTH], kv_own.at[1]),
    ]
    weights = [
        pltpu.make_async_copy(w_hbm.at[pl.ds(n * z.fb, z.fb), :], wbuf.at[n], w_sem.at[n])
        for n in range(4)
    ]
    def column_of_lengths(p):
        want = lax.broadcasted_iota(jnp.int32, (z.pt, z.all_tok), 0) + owner_of(p) * z.pt
        have = lax.broadcasted_iota(jnp.int32, (z.pt, z.all_tok), 1)
        seen = jnp.where(want == have, jnp.broadcast_to(vis_ref[...], (z.pt, z.all_tok)), 0)
        column = jnp.sum(seen.astype(jnp.float32), axis=1, keepdims=True)
        lens[p] = jnp.broadcast_to(jnp.concatenate([column] * z.group, axis=0), (z.rows, HEAD_WIDTH))

    def owner_of(p):
        return t_other if p == 0 else t

    pl.semaphore_wait(barrier, 8)

    sent = []

    def send(copy):
        copy.start()
        sent.append(copy)

    def query_copies(k, s_to, t_to):
        return [
            pltpu.make_async_remote_copy(
                src_ref=src, dst_ref=dst, send_sem=q_send.at[n, k],
                recv_sem=q_recv.at[n, my_slot], device_id={"seq": s_to, "tp": t_to},
                device_id_type=MESH,
            )
            for n, (src, dst) in enumerate(query_parts(s_to, t_to))
        ]

    half = z.block // 2
    my_rows = pl.ds(pl.multiple_of(r * half, half), half)
    other_rows = pl.ds(pl.multiple_of(partner * half, half), half)

    def prefix_copies(k, s_to):
        thin = pl.ds(pl.multiple_of(s_to * z.kb, 128), z.kb)
        return [
            pltpu.make_async_remote_copy(
                src_ref=src.at[my_rows, thin], dst_ref=dst.at[s, my_rows, 0:HEAD_WIDTH],
                send_sem=kv_send.at[n, k], recv_sem=kv_recv.at[n, s],
                device_id={"seq": s_to}, device_id_type=MESH,
            )
            for n, (src, dst) in enumerate(((k_hbm, kbuf), (v_hbm, vbuf)))
        ]

    targets = (far_end, far_mid, mate)
    queries = [query_copies(2 * k + 2, s_to, t) + query_copies(2 * k + 3, s_to, t_other) for k, s_to in enumerate(targets)]
    prefix = [prefix_copies(k, s_to) for k, s_to in enumerate(targets)]
    for copy in query_copies(0, s, t_other) + queries[0]:
        send(copy)

    @pl.when(is_end)
    def _():
        for copy in prefix[0] + queries[1] + queries[2] + prefix[2] + prefix[1]:
            copy.start()

    @pl.when(jnp.logical_not(is_end))
    def _():
        for copy in prefix[0] + queries[2] + prefix[2] + queries[1] + prefix[1]:
            copy.start()

    for k in range(3):
        sent.extend(prefix[k])
    sent.extend(queries[1] + queries[2])

    lengths = pltpu.make_async_copy(vis_hbm, vis_ref, vis_sem)
    for copy in [lengths] + own_parts + own_kv + weights:
        copy.start()
    lengths.wait()

    for p in range(2):
        column_of_lengths(p)
    head_lanes = slice(0, HEAD_WIDTH)
    vbuf[:, :, HEAD_WIDTH:] = jnp.ones((4, z.block, HEAD_WIDTH), jnp.bfloat16)
    for slot in range(8):
        for n, buf in enumerate((qbuf, fkbuf, fvbuf)):
            pltpu.make_async_copy(buf.at[slot], buf.at[slot], q_recv.at[n, slot]).wait()

    def rows_of(buf, p, first):
        some = pl.ds(owner_of(p) * z.ps, z.ps)
        value = buf[some, :, first:first + HEAD_WIDTH].astype(jnp.float32)
        return value.reshape(z.pt, HEAD_WIDTH)

    for p in range(2):
        own_key, own_value = rows_of(fkbuf, p, 0), rows_of(fvbuf, p, 0)
        for g in range(z.group):
            query = rows_of(qbuf, p, g * HEAD_WIDTH)
            span = slice(g * z.pt, (g + 1) * z.pt)
            qs[p, span, :] = query.astype(jnp.bfloat16)
            own = jnp.sum(query * own_key, axis=1, keepdims=True)
            peak[p, span, :] = jnp.broadcast_to(own, (z.pt, HEAD_WIDTH))
            acc[p, span, head_lanes] = own_value
            acc[p, span, HEAD_WIDTH:] = jnp.ones((z.pt, HEAD_WIDTH), jnp.float32)

    def attend(p, source, first=0, count=None):
        count = count or z.block
        repeat = count // HEAD_WIDTH
        rows = pl.ds(first if isinstance(first, int) else pl.multiple_of(first, half), count)
        scores = lax.dot_general(
            qs[p], kbuf[source, rows, :], (((1,), (1,)), ((), ())), preferred_element_type=jnp.float32
        )
        spot = lax.broadcasted_iota(jnp.int32, scores.shape, 1).astype(jnp.float32)
        left = lens[p] - (source * z.block + first).astype(jnp.float32)
        scores = jnp.where(spot < jnp.concatenate([left] * repeat, axis=1), scores, MASKED)
        before = peak[p]
        now = jnp.maximum(before, jnp.broadcast_to(jnp.max(scores, axis=1, keepdims=True), before.shape))
        fade = jnp.exp2((before - now) * log_scale)
        part = jnp.exp2((scores - jnp.concatenate([now] * repeat, axis=1)) * log_scale)
        peak[p] = now
        acc[p] = acc[p] * jnp.concatenate([fade] * 2, axis=1) + jnp.dot(
            part.astype(jnp.bfloat16), vbuf[source, rows, :], preferred_element_type=jnp.float32
        )

    def pass_kv(j, source):
        passed = []
        for n, buf in enumerate((kbuf, vbuf)):
            mine = buf.at[source, my_rows, 0:HEAD_WIDTH]
            pltpu.make_async_copy(mine, mine, kv_recv.at[n, source]).wait()
            passed.append(pltpu.make_async_remote_copy(
                src_ref=mine, dst_ref=mine, send_sem=f_send.at[n, j], recv_sem=f_recv.at[n, source],
                device_id={"rep": partner}, device_id_type=MESH,
            ))
            passed[-1].start()
        return passed

    def passed_kv(source):
        for n, buf in enumerate((kbuf, vbuf)):
            theirs = buf.at[source, other_rows, 0:HEAD_WIDTH]
            pltpu.make_async_copy(theirs, theirs, f_recv.at[n, source]).wait()

    def finish(p):
        context = (acc[p, :, head_lanes] / acc[p, :, HEAD_WIDTH:]).astype(jnp.bfloat16)
        for g in range(z.group):
            cbuf[s, p, :, g * HEAD_WIDTH:(g + 1) * HEAD_WIDTH] = context[g * z.pt:(g + 1) * z.pt, :]
        send(context_copy(0, s, p, far_end))

        @pl.when(jnp.logical_not(is_end))
        def _():
            context_copy(2, s, p, far_mid).start()
            context_copy(1, s, p, mate).start()

        sent.append(context_copy(1, s, p, mate))

    def context_copy(k, source, p, s_to):
        return pltpu.make_async_remote_copy(
            src_ref=cbuf.at[source, p], dst_ref=cbuf.at[source, p],
            send_sem=c_send.at[k, p], recv_sem=c_recv.at[source, p],
            device_id={"seq": s_to}, device_id_type=MESH,
        )

    def landed(source, p):
        pltpu.make_async_copy(cbuf.at[source, p], cbuf.at[source, p], c_recv.at[source, p]).wait()

    spans = [slice(n * z.tile, (n + 1) * z.tile) for n in range(z.tiles)]

    def project_all(source, first):
        for at in spans:
            value = jnp.dot(
                cbuf[source].reshape(2 * z.pt, z.fb), wbuf[source, :, at], preferred_element_type=jnp.float32
            )
            oacc[:, at] = value if first else oacc[:, at] + value

    def project_half(source, p, at):
        return oacc[p * z.pt:(p + 1) * z.pt, at] + jnp.dot(
            cbuf[source, p], wbuf[source, :, at], preferred_element_type=jnp.float32
        )

    for copy in own_kv:
        copy.wait()
    for p in range(2):
        attend(p, s)
    sources = (
        jnp.where(is_end, far_end, mate), jnp.where(is_end, far_mid, far_end), jnp.where(is_end, mate, far_mid)
    )
    for j in range(2):
        sent.extend(pass_kv(j, sources[j]))
        passed_kv(sources[j])
        for p in range(2):
            attend(p, sources[j])
    sent.extend(pass_kv(2, sources[2]))
    for p in range(2):
        attend(p, sources[2], r * half, half)
    passed_kv(sources[2])
    for p in range(2):
        attend(p, sources[2], partner * half, half)
        finish(p)

    @pl.when(is_end)
    def _():
        for p in range(2):
            context_copy(1, s, p, mate).start()

    for copy in weights:
        copy.wait()
    project_all(s, True)
    second = jnp.where(is_end, far_end, mate)
    for p in range(2):
        landed(second, p)

        @pl.when(is_end)
        def _():
            context_copy(2, far_end, p, mate).start()
    project_all(second, False)

    third = jnp.where(is_end, mate, far_end)
    for p in range(2):
        landed(third, p)
        for at in spans:
            oacc[p * z.pt:(p + 1) * z.pt, at] = project_half(third, p, at)
        landed(far_mid, p)
        for n, at in enumerate(spans):
            value = project_half(far_mid, p, at)
            if p == 0:
                osend[0, n] = value.astype(jnp.bfloat16)
                send(pltpu.make_async_remote_copy(
                    src_ref=osend.at[0, n], dst_ref=orecv.at[0, n],
                    send_sem=o_send.at[0, n], recv_sem=o_recv.at[0, n],
                    device_id={"tp": t_other}, device_id_type=MESH,
                ))
            else:
                pltpu.make_async_copy(orecv.at[0, n], orecv.at[0, n], o_recv.at[0, n]).wait()
                out_ref[0, :, at] = (value + orecv[0, n].astype(jnp.float32)).astype(jnp.bfloat16)
    for copy in sent:
        copy.wait_send()
    for p in range(2):
        context_copy(2, s, p, mate).wait_send()


def shards(mesh_shape, *args):
    queries, fresh_key_rows, fresh_value_rows, visible, prefix_keys, cached_value_rows, out_weight = args
    z = Sizes(mesh_shape, queries, visible, prefix_keys, out_weight)
    staged = z.seq == 4 and z.tp == 2 and z.rep == 2 and z.b == 1 and z.kl == 1
    bf16, f32 = jnp.bfloat16, jnp.float32
    vmem, dma = pltpu.VMEM, pltpu.SemaphoreType.DMA
    if staged:
        state = [
            vmem((2, z.rows, HEAD_WIDTH), bf16),
            vmem((2, z.rows, HEAD_WIDTH), f32),
            vmem((2, z.rows, HEAD_WIDTH), f32),
            vmem((2, z.rows, 2 * HEAD_WIDTH), f32),
        ]
    else:
        state = [
                vmem((z.np, z.kl, z.rows, HEAD_WIDTH), bf16),
                vmem((z.np, z.rows, 1), f32),
                vmem((z.np, z.kl, z.rows, 1), f32),
                vmem((z.np, z.kl, z.rows, 1), f32),
                vmem((z.np, z.kl, z.rows, HEAD_WIDTH), f32),
        ]
    anywhere = pl.BlockSpec(memory_space=pl.ANY)
    inside = pl.BlockSpec(memory_space=pltpu.VMEM)
    held = pl.BlockSpec(memory_space=pltpu.HBM)
    return pl.pallas_call(
        functools.partial(line_kernel if staged else kernel, z),
        out_shape=jax.ShapeDtypeStruct((1, z.no, z.cols), bf16),
        in_specs=[held if staged else inside if n == 3 else anywhere for n in range(7)],
        out_specs=inside,
        scratch_shapes=[
            vmem((z.slots, z.tok, z.fb), bf16),
            vmem((z.slots, z.tok, z.kb), bf16),
            vmem((z.slots, z.tok, z.kb), bf16),
            vmem((z.seq, z.block, z.kb), bf16),
            vmem((z.seq, z.block, z.kb + staged * HEAD_WIDTH), bf16),
            vmem((z.a, z.fb, z.cols), bf16),
            *state,
            vmem((z.seq, z.np, z.pt, z.fb), bf16),
            vmem((z.all_tok, z.cols), f32),
            vmem((z.tp, z.tiles, z.no, z.tile), bf16),
            vmem((z.tp, z.tiles, z.no, z.tile), bf16),
            dma((3, z.slots)), dma((3, z.slots)),
            dma((2, z.seq)), dma((2, z.seq)),
            dma((2, z.seq)), dma((2, z.seq)),
            dma((2,)), dma((z.a,)),
            dma((z.seq, z.np)), dma((z.seq, z.np)),
            dma((z.tp, z.tiles)), dma((z.tp, z.tiles)),
            *([vmem((1, z.all_tok), jnp.int32), dma] if staged else []),
        ],
        compiler_params=pltpu.CompilerParams(
            collective_id=0, has_side_effects=True, vmem_limit_bytes=(44 if staged else 56) * 1024 * 1024
        ),
        name="attend_and_project",
    )(*([pltpu.with_memory_space_constraint(x, pltpu.HBM) for x in args] if staged else args))


def solution(mesh):
    in_specs = (
        P("rep", ("groups", "seq", "tp"), None),
        P("rep", ("groups", "seq", "tp"), None),
        P("rep", ("groups", "seq", "tp"), None),
        P("rep", "groups"),
        P(("groups", "seq"), "tp"),
        P(("groups", "seq"), "tp"),
        P("tp", "seq"),
    )
    out_specs = P("rep", ("groups", "tp"), "seq")
    body = functools.partial(shards, dict(mesh.shape))
    return jax.shard_map(body, mesh=mesh, in_specs=in_specs, out_specs=out_specs, check_vma=False)
```

```python
import functools
import math

import jax
import jax.numpy as jnp
from jax import lax
from jax.experimental import pallas as pl
from jax.experimental.pallas import tpu as pltpu
from jax.sharding import PartitionSpec as P

HEAD_WIDTH = 128
MASKED = -1e30
MESH = pl.DeviceIdType.MESH


class Sizes:
    def __init__(self, mesh_shape, queries, visible, prefix_keys, out_weight):
        self.seq = mesh_shape["seq"]
        self.tp = mesh_shape["tp"]
        self.rep = mesh_shape["rep"]
        self.tok = queries.shape[1]
        self.all_tok = visible.shape[1]
        self.block = prefix_keys.shape[0]
        kv_heads = prefix_keys.shape[1] // HEAD_WIDTH
        self.features, self.cols = out_weight.shape
        self.group = self.features // (kv_heads * HEAD_WIDTH)
        self.a = self.seq if kv_heads % self.seq == 0 else 1
        self.b = self.seq // self.a
        self.kl = kv_heads // self.a
        self.slots = self.a * self.tp
        self.nt = self.slots * self.tok
        self.np = self.tp if self.b == 1 else 1
        self.pt = self.nt // self.np
        self.ps = self.slots // self.np
        self.fb = self.kl * self.group * HEAD_WIDTH
        self.kb = self.kl * HEAD_WIDTH
        self.rows = self.group * self.pt
        self.no = self.all_tok // self.tp
        self.tile = math.gcd(self.cols, 512)
        self.tiles = self.cols // self.tile


def kernel(
    z, q_hbm, fk_hbm, fv_hbm, vis_ref, k_hbm, v_hbm, w_hbm, out_ref,
    qbuf, fkbuf, fvbuf, kbuf, vbuf, wbuf, qs, lens, peak, total, acc, cbuf, oacc, osend, orecv,
    q_send, q_recv, kv_send, kv_recv, f_send, f_recv, kv_own, w_sem, c_send, c_recv, o_send, o_recv,
):
    s, t, r = lax.axis_index("seq"), lax.axis_index("tp"), lax.axis_index("rep")
    partner = lax.rem(r + 1, z.rep)
    scale = 1.0 / math.sqrt(HEAD_WIDTH)

    def near(base, step, size):
        return lax.rem(base + step, size)

    def head_of(index):
        return index if z.a > 1 else 0

    barrier = pltpu.get_barrier_semaphore()
    for j in range(z.seq):
        for i in range(z.tp):
            if i or j:
                pl.semaphore_signal(
                    barrier, inc=1, device_id={"seq": near(s, j, z.seq), "tp": near(t, i, z.tp)},
                    device_id_type=MESH,
                )
    pl.semaphore_signal(barrier, inc=1, device_id={"rep": partner}, device_id_type=MESH)

    my_slot = head_of(s) * z.tp + t

    def query_parts(s_to, t_to):
        head = t_to * z.a + head_of(s_to)
        wide = pl.ds(pl.multiple_of(head * z.fb, 128), z.fb)
        thin = pl.ds(pl.multiple_of(head * z.kb, 128), z.kb)
        return (
            (q_hbm.at[0, :, wide], qbuf.at[my_slot]),
            (fk_hbm.at[0, :, thin], fkbuf.at[my_slot]),
            (fv_hbm.at[0, :, thin], fvbuf.at[my_slot]),
        )

    own_parts = [
        pltpu.make_async_copy(src, dst, q_recv.at[n, my_slot])
        for n, (src, dst) in enumerate(query_parts(s, t))
    ]
    thin_own = pl.ds(pl.multiple_of(head_of(s) * z.kb, 128), z.kb)
    own_kv = [
        pltpu.make_async_copy(k_hbm.at[:, thin_own], kbuf.at[s], kv_own.at[0]),
        pltpu.make_async_copy(v_hbm.at[:, thin_own], vbuf.at[s], kv_own.at[1]),
    ]
    weights = [
        pltpu.make_async_copy(w_hbm.at[pl.ds(n * z.fb, z.fb), :], wbuf.at[n], w_sem.at[n])
        for n in range(z.a)
    ]
    for copy in own_parts + own_kv + weights:
        copy.start()
    pl.semaphore_wait(barrier, z.seq * z.tp)

    sent, sent_if = [], []

    def send(copy, s_to=None):
        if s_to is None:
            copy.start()
            sent.append(copy)
        else:
            pl.when(s != s_to)(copy.start)
            sent_if.append((s_to, copy))

    def send_queries(s_to, t_step, only_if):
        t_to = near(t, t_step, z.tp)
        slot = (s_to if z.a > 1 else 0) * z.tp + t_step
        for n, (src, dst) in enumerate(query_parts(s_to, t_to)):
            send(pltpu.make_async_remote_copy(
                src_ref=src, dst_ref=dst, send_sem=q_send.at[n, slot],
                recv_sem=q_recv.at[n, my_slot], device_id={"seq": s_to, "tp": t_to},
                device_id_type=MESH,
            ), s_to if only_if else None)

    half = z.block // z.rep
    my_rows = pl.ds(pl.multiple_of(r * half, half), half)
    if z.a == 1:
        for i in range(1, z.tp):
            send_queries(s, i, False)
    for s_to in sorted(range(z.seq), key=lambda n: abs(2 * n + 1 - z.seq)):
        if z.a > 1:
            for i in range(z.tp):
                send_queries(s_to, i, i == 0)
        thin = pl.ds(head_of(s_to) * z.kb, z.kb)
        for n, (src, dst) in enumerate(((k_hbm, kbuf), (v_hbm, vbuf))):
            send(pltpu.make_async_remote_copy(
                src_ref=src.at[my_rows, thin], dst_ref=dst.at[s, my_rows, :],
                send_sem=kv_send.at[n, s_to], recv_sem=kv_recv.at[n, s],
                device_id={"seq": s_to}, device_id_type=MESH,
            ), s_to)

    def nearest(k):
        flip = s // (z.seq // 2) if z.seq > 1 else 0
        edge = s + flip * (z.seq - 1 - 2 * s)
        both = k <= 2 * edge
        away = jnp.where(both, (k + 1) // 2 * (1 - 2 * (k % 2)), k - edge)
        return s + away * (1 - 2 * flip)

    def owner_of(p):
        return near(t, p + 1, z.tp) if z.np > 1 else 0

    for p in range(z.np):
        want = lax.broadcasted_iota(jnp.int32, (z.pt, z.all_tok), 0) + owner_of(p) * z.pt
        if z.b > 1:
            want = want + s * z.nt
        have = lax.broadcasted_iota(jnp.int32, (z.pt, z.all_tok), 1)
        seen = jnp.where(want == have, jnp.broadcast_to(vis_ref[...], (z.pt, z.all_tok)), 0)
        column = jnp.sum(seen.astype(jnp.float32), axis=1, keepdims=True)
        lens[p] = jnp.concatenate([column] * z.group, axis=0)

    for j in range(z.a):
        for i in range(z.tp):
            slot = (near(s, j, z.seq) if z.a > 1 else 0) * z.tp + near(t, i, z.tp)
            for n, buf in enumerate((qbuf, fkbuf, fvbuf)):
                pltpu.make_async_copy(buf.at[slot], buf.at[slot], q_recv.at[n, slot]).wait()

    def rows_of(buf, p, first):
        some = pl.ds(owner_of(p) * z.ps, z.ps)
        value = buf[some, :, first:first + HEAD_WIDTH].astype(jnp.float32)
        return value.reshape(z.pt, HEAD_WIDTH)

    for p in range(z.np):
        for h in range(z.kl):
            own_key = rows_of(fkbuf, p, h * HEAD_WIDTH)
            own_value = rows_of(fvbuf, p, h * HEAD_WIDTH)
            for g in range(z.group):
                query = rows_of(qbuf, p, (h * z.group + g) * HEAD_WIDTH)
                span = slice(g * z.pt, (g + 1) * z.pt)
                qs[p, h, span, :] = query.astype(jnp.bfloat16)
                peak[p, h, span, :] = jnp.sum(query * own_key, axis=1, keepdims=True) * scale
                total[p, h, span, :] = jnp.ones((z.pt, 1), jnp.float32)
                acc[p, h, span, :] = own_value

    def attend(p, source):
        for h in range(z.kl):
            at = slice(h * HEAD_WIDTH, (h + 1) * HEAD_WIDTH)
            keys, values = kbuf[source, :, at], vbuf[source, :, at]
            scores = lax.dot_general(
                qs[p, h], keys, (((1,), (1,)), ((), ())), preferred_element_type=jnp.float32
            ) * scale
            spot = lax.broadcasted_iota(jnp.int32, scores.shape, 1) + source * z.block
            scores = jnp.where(spot.astype(jnp.float32) < lens[p], scores, MASKED)
            before = peak[p, h]
            now = jnp.maximum(before, jnp.max(scores, axis=1, keepdims=True))
            fade = jnp.exp(before - now)
            part = jnp.exp(scores - now)
            peak[p, h] = now
            total[p, h] = total[p, h] * fade + jnp.sum(part, axis=1, keepdims=True)
            acc[p, h] = acc[p, h] * fade + jnp.dot(
                part.astype(jnp.bfloat16), values, preferred_element_type=jnp.float32
            )

    def finish(p):
        for h in range(z.kl):
            context = (acc[p, h] / total[p, h]).astype(jnp.bfloat16)
            for g in range(z.group):
                at = (h * z.group + g) * HEAD_WIDTH
                cbuf[s, p, :, at:at + HEAD_WIDTH] = context[g * z.pt:(g + 1) * z.pt, :]
        for j in range(1, z.seq):
            sent.append(pltpu.make_async_remote_copy(
                src_ref=cbuf.at[s, p], dst_ref=cbuf.at[s, p],
                send_sem=c_send.at[j, p], recv_sem=c_recv.at[s, p],
                device_id={"seq": near(s, j, z.seq)}, device_id_type=MESH,
            ))
            sent[-1].start()

    for j in range(z.seq):
        source = nearest(j) if j else s
        if j == 0:
            for copy in own_kv:
                copy.wait()
        else:
            passed = []
            for n, buf in enumerate((kbuf, vbuf)):
                mine = buf.at[source, my_rows, :]
                pltpu.make_async_copy(mine, mine, kv_recv.at[n, source]).wait()
                passed.append(pltpu.make_async_remote_copy(
                    src_ref=mine, dst_ref=mine, send_sem=f_send.at[n, j], recv_sem=f_recv.at[n, source],
                    device_id={"rep": partner}, device_id_type=MESH,
                ))
                passed[-1].start()
            other = pl.ds(pl.multiple_of(partner * half, half), half)
            for n, buf in enumerate((kbuf, vbuf)):
                theirs = buf.at[source, other, :]
                pltpu.make_async_copy(theirs, theirs, f_recv.at[n, source]).wait()
            sent.extend(passed)
        for p in range(z.np):
            attend(p, source)
            if j == z.seq - 1:
                finish(p)

    for copy in weights:
        copy.wait()

    def project(j, source, p, at):
        value = jnp.dot(
            cbuf[source, p], wbuf[head_of(source), :, at], preferred_element_type=jnp.float32
        )
        if z.b > 1:
            oacc[pl.ds(pl.multiple_of(source * z.nt, z.nt), z.nt), at] = value
            return value
        rows = slice(p * z.pt, (p + 1) * z.pt)
        if j:
            value = value + oacc[rows, at]
        if j < z.seq - 1:
            oacc[rows, at] = value
        return value

    def give(i, n, value):
        osend[i, n] = value.astype(jnp.bfloat16)
        sent.append(pltpu.make_async_remote_copy(
            src_ref=osend.at[i, n], dst_ref=orecv.at[i, n],
            send_sem=o_send.at[i, n], recv_sem=o_recv.at[i, n],
            device_id={"tp": near(t, i + 1, z.tp)}, device_id_type=MESH,
        ))
        sent[-1].start()

    def keep(n, at, value):
        for i in range(z.tp - 1):
            pltpu.make_async_copy(orecv.at[i, n], orecv.at[i, n], o_recv.at[i, n]).wait()
            value = value + orecv[i, n].astype(jnp.float32)
        out_ref[0, :, at] = value.astype(jnp.bfloat16)

    spans = [slice(n * z.tile, (n + 1) * z.tile) for n in range(z.tiles)]
    for p in range(z.np):
        for j in range(z.seq):
            source = nearest(j) if j else s
            if j:
                landed = cbuf.at[source, p]
                pltpu.make_async_copy(landed, landed, c_recv.at[source, p]).wait()
            for n, at in enumerate(spans):
                value = project(j, source, p, at)
                if z.b == 1 and j == z.seq - 1:
                    if p < z.np - 1:
                        give(p, n, value)
                    else:
                        keep(n, at, value)
    if z.b > 1:
        for n, at in enumerate(spans):
            for i in range(z.tp - 1):
                rows = pl.ds(pl.multiple_of(near(t, i + 1, z.tp) * z.no, z.no), z.no)
                give(i, n, oacc[rows, at])
        for n, at in enumerate(spans):
            keep(n, at, oacc[pl.ds(pl.multiple_of(t * z.no, z.no), z.no), at])
    for copy in sent:
        copy.wait_send()
    for s_to, copy in sent_if:
        pl.when(s != s_to)(copy.wait_send)


def line_kernel(
    z, q_hbm, fk_hbm, fv_hbm, vis_hbm, k_hbm, v_hbm, w_hbm, out_ref,
    qbuf, fkbuf, fvbuf, kbuf, vbuf, wbuf, qs, lens, peak, acc, cbuf, oacc, osend, orecv,
    q_send, q_recv, kv_send, kv_recv, f_send, f_recv, kv_own, w_sem, c_send, c_recv, o_send, o_recv,
    vis_ref, vis_sem,
):
    s, t, r = lax.axis_index("seq"), lax.axis_index("tp"), lax.axis_index("rep")
    partner, t_other = 1 - r, 1 - t
    log_scale = math.log2(math.e) / math.sqrt(HEAD_WIDTH)
    low = s < 2
    is_end = (s == 0) | (s == 3)
    mate = s + 1 - 2 * lax.rem(s, 2)
    far_end = jnp.where(low, 3, 0)
    far_mid = jnp.where(low, 2, 1)

    barrier = pltpu.get_barrier_semaphore()
    for s_to, t_to in (
        (far_end, t), (far_mid, t), (far_end, t_other), (far_mid, t_other), (mate, t), (mate, t_other), (s, t_other)
    ):
        pl.semaphore_signal(barrier, inc=1, device_id={"seq": s_to, "tp": t_to}, device_id_type=MESH)
    pl.semaphore_signal(barrier, inc=1, device_id={"rep": partner}, device_id_type=MESH)

    my_slot = s * 2 + t

    def query_parts(s_to, t_to):
        head = t_to * 4 + s_to
        wide = pl.ds(pl.multiple_of(head * z.fb, 128), z.fb)
        thin = pl.ds(pl.multiple_of(head * z.kb, 128), z.kb)
        return (
            (q_hbm.at[0, :, wide], qbuf.at[my_slot]),
            (fk_hbm.at[0, :, thin], fkbuf.at[my_slot]),
            (fv_hbm.at[0, :, thin], fvbuf.at[my_slot]),
        )

    own_parts = [
        pltpu.make_async_copy(src, dst, q_recv.at[n, my_slot])
        for n, (src, dst) in enumerate(query_parts(s, t))
    ]
    thin_own = pl.ds(pl.multiple_of(s * z.kb, 128), z.kb)
    own_kv = [
        pltpu.make_async_copy(k_hbm.at[:, thin_own], kbuf.at[s], kv_own.at[0]),
        pltpu.make_async_copy(v_hbm.at[:, thin_own], vbuf.at[s, :, 0:HEAD_WIDTH], kv_own.at[1]),
    ]
    weights = [
        pltpu.make_async_copy(w_hbm.at[pl.ds(n * z.fb, z.fb), :], wbuf.at[n], w_sem.at[n])
        for n in range(4)
    ]
    def column_of_lengths(p):
        want = lax.broadcasted_iota(jnp.int32, (z.pt, z.all_tok), 0) + owner_of(p) * z.pt
        have = lax.broadcasted_iota(jnp.int32, (z.pt, z.all_tok), 1)
        seen = jnp.where(want == have, jnp.broadcast_to(vis_ref[...], (z.pt, z.all_tok)), 0)
        column = jnp.sum(seen.astype(jnp.float32), axis=1, keepdims=True)
        lens[p] = jnp.broadcast_to(jnp.concatenate([column] * z.group, axis=0), (z.rows, HEAD_WIDTH))

    def owner_of(p):
        return t_other if p == 0 else t

    pl.semaphore_wait(barrier, 8)

    sent = []

    def send(copy):
        copy.start()
        sent.append(copy)

    def query_copies(k, s_to, t_to):
        return [
            pltpu.make_async_remote_copy(
                src_ref=src, dst_ref=dst, send_sem=q_send.at[n, k],
                recv_sem=q_recv.at[n, my_slot], device_id={"seq": s_to, "tp": t_to},
                device_id_type=MESH,
            )
            for n, (src, dst) in enumerate(query_parts(s_to, t_to))
        ]

    half = z.block // 2
    my_rows = pl.ds(pl.multiple_of(r * half, half), half)
    other_rows = pl.ds(pl.multiple_of(partner * half, half), half)

    def prefix_copies(k, s_to):
        thin = pl.ds(pl.multiple_of(s_to * z.kb, 128), z.kb)
        return [
            pltpu.make_async_remote_copy(
                src_ref=src.at[my_rows, thin], dst_ref=dst.at[s, my_rows, 0:HEAD_WIDTH],
                send_sem=kv_send.at[n, k], recv_sem=kv_recv.at[n, s],
                device_id={"seq": s_to}, device_id_type=MESH,
            )
            for n, (src, dst) in enumerate(((k_hbm, kbuf), (v_hbm, vbuf)))
        ]

    targets = (far_end, far_mid, mate)
    queries = [query_copies(2 * k + 2, s_to, t) + query_copies(2 * k + 3, s_to, t_other) for k, s_to in enumerate(targets)]
    prefix = [prefix_copies(k, s_to) for k, s_to in enumerate(targets)]
    beside = query_copies(0, s, t_other)
    for copy in queries[0]:
        send(copy)

    @pl.when(is_end)
    def _():
        for copy in prefix[0] + queries[1] + queries[2] + prefix[2] + prefix[1]:
            copy.start()

    @pl.when(jnp.logical_not(is_end))
    def _():
        for copy in prefix[0] + queries[2] + prefix[2] + queries[1] + prefix[1]:
            copy.start()

    for k in range(3):
        sent.extend(prefix[k])
    for copy in beside:
        send(copy)
    sent.extend(queries[1] + queries[2])

    lengths = pltpu.make_async_copy(vis_hbm, vis_ref, vis_sem)
    for copy in [lengths] + own_parts + own_kv + weights:
        copy.start()
    lengths.wait()

    for p in range(2):
        column_of_lengths(p)
    head_lanes = slice(0, HEAD_WIDTH)
    vbuf[:, :, HEAD_WIDTH:] = jnp.ones((4, z.block, HEAD_WIDTH), jnp.bfloat16)
    for slot in range(8):
        for n, buf in enumerate((qbuf, fkbuf, fvbuf)):
            pltpu.make_async_copy(buf.at[slot], buf.at[slot], q_recv.at[n, slot]).wait()

    def rows_of(buf, p, first):
        some = pl.ds(owner_of(p) * z.ps, z.ps)
        value = buf[some, :, first:first + HEAD_WIDTH].astype(jnp.float32)
        return value.reshape(z.pt, HEAD_WIDTH)

    for p in range(2):
        own_key, own_value = rows_of(fkbuf, p, 0), rows_of(fvbuf, p, 0)
        for g in range(z.group):
            query = rows_of(qbuf, p, g * HEAD_WIDTH)
            span = slice(g * z.pt, (g + 1) * z.pt)
            qs[p, span, :] = query.astype(jnp.bfloat16)
            own = jnp.sum(query * own_key, axis=1, keepdims=True)
            peak[p, span, :] = jnp.broadcast_to(own, (z.pt, HEAD_WIDTH))
            acc[p, span, head_lanes] = own_value
            acc[p, span, HEAD_WIDTH:] = jnp.ones((z.pt, HEAD_WIDTH), jnp.float32)

    def attend(p, source, first=0, count=None):
        count = count or z.block
        repeat = count // HEAD_WIDTH
        rows = pl.ds(first if isinstance(first, int) else pl.multiple_of(first, half), count)
        scores = lax.dot_general(
            qs[p], kbuf[source, rows, :], (((1,), (1,)), ((), ())), preferred_element_type=jnp.float32
        )
        spot = lax.broadcasted_iota(jnp.int32, scores.shape, 1).astype(jnp.float32)
        left = lens[p] - (source * z.block + first).astype(jnp.float32)
        scores = jnp.where(spot < jnp.concatenate([left] * repeat, axis=1), scores, MASKED)
        before = peak[p]
        now = jnp.maximum(before, jnp.broadcast_to(jnp.max(scores, axis=1, keepdims=True), before.shape))
        fade = jnp.exp2((before - now) * log_scale)
        part = jnp.exp2((scores - jnp.concatenate([now] * repeat, axis=1)) * log_scale)
        peak[p] = now
        acc[p] = acc[p] * jnp.concatenate([fade] * 2, axis=1) + jnp.dot(
            part.astype(jnp.bfloat16), vbuf[source, rows, :], preferred_element_type=jnp.float32
        )

    def pass_kv(j, source):
        passed = []
        for n, buf in enumerate((kbuf, vbuf)):
            mine = buf.at[source, my_rows, 0:HEAD_WIDTH]
            pltpu.make_async_copy(mine, mine, kv_recv.at[n, source]).wait()
            passed.append(pltpu.make_async_remote_copy(
                src_ref=mine, dst_ref=mine, send_sem=f_send.at[n, j], recv_sem=f_recv.at[n, source],
                device_id={"rep": partner}, device_id_type=MESH,
            ))
            passed[-1].start()
        return passed

    def passed_kv(source):
        for n, buf in enumerate((kbuf, vbuf)):
            theirs = buf.at[source, other_rows, 0:HEAD_WIDTH]
            pltpu.make_async_copy(theirs, theirs, f_recv.at[n, source]).wait()

    def finish(p):
        context = (acc[p, :, head_lanes] / acc[p, :, HEAD_WIDTH:]).astype(jnp.bfloat16)
        for g in range(z.group):
            cbuf[s, p, :, g * HEAD_WIDTH:(g + 1) * HEAD_WIDTH] = context[g * z.pt:(g + 1) * z.pt, :]
        send(context_copy(0, s, p, far_end))

        @pl.when(jnp.logical_not(is_end))
        def _():
            context_copy(2, s, p, far_mid).start()
            context_copy(1, s, p, mate).start()

        sent.append(context_copy(1, s, p, mate))

    def context_copy(k, source, p, s_to):
        return pltpu.make_async_remote_copy(
            src_ref=cbuf.at[source, p], dst_ref=cbuf.at[source, p],
            send_sem=c_send.at[k, p], recv_sem=c_recv.at[source, p],
            device_id={"seq": s_to}, device_id_type=MESH,
        )

    def landed(source, p):
        pltpu.make_async_copy(cbuf.at[source, p], cbuf.at[source, p], c_recv.at[source, p]).wait()

    spans = [slice(n * z.tile, (n + 1) * z.tile) for n in range(z.tiles)]

    def project_all(source, first):
        for at in spans:
            value = jnp.dot(
                cbuf[source].reshape(2 * z.pt, z.fb), wbuf[source, :, at], preferred_element_type=jnp.float32
            )
            oacc[:, at] = value if first else oacc[:, at] + value

    def project_half(source, p, at):
        return oacc[p * z.pt:(p + 1) * z.pt, at] + jnp.dot(
            cbuf[source, p], wbuf[source, :, at], preferred_element_type=jnp.float32
        )

    sources = (
        jnp.where(is_end, far_end, mate), jnp.where(is_end, far_mid, far_end), jnp.where(is_end, mate, far_mid)
    )
    for copy in own_kv:
        copy.wait()
    sent.extend(pass_kv(0, sources[0]))
    for p in range(2):
        attend(p, s)
    sent.extend(pass_kv(1, sources[1]))
    passed_kv(sources[0])
    for p in range(2):
        attend(p, sources[0])
    passed_kv(sources[1])
    attend(0, sources[1])
    sent.extend(pass_kv(2, sources[2]))
    attend(1, sources[1])
    for p in range(2):
        attend(p, sources[2], r * half, half)
    passed_kv(sources[2])
    for p in range(2):
        attend(p, sources[2], partner * half, half)
        finish(p)

    @pl.when(is_end)
    def _():
        for p in range(2):
            context_copy(1, s, p, mate).start()

    for copy in weights:
        copy.wait()
    project_all(s, True)
    second = jnp.where(is_end, far_end, mate)
    for p in range(2):
        landed(second, p)

        @pl.when(is_end)
        def _():
            context_copy(2, far_end, p, mate).start()
    project_all(second, False)

    third = jnp.where(is_end, mate, far_end)
    for p in range(2):
        landed(third, p)
        for at in spans:
            oacc[p * z.pt:(p + 1) * z.pt, at] = project_half(third, p, at)
        landed(far_mid, p)
        for n, at in enumerate(spans):
            value = project_half(far_mid, p, at)
            if p == 0:
                osend[0, n] = value.astype(jnp.bfloat16)
                send(pltpu.make_async_remote_copy(
                    src_ref=osend.at[0, n], dst_ref=orecv.at[0, n],
                    send_sem=o_send.at[0, n], recv_sem=o_recv.at[0, n],
                    device_id={"tp": t_other}, device_id_type=MESH,
                ))
            else:
                pltpu.make_async_copy(orecv.at[0, n], orecv.at[0, n], o_recv.at[0, n]).wait()
                out_ref[0, :, at] = (value + orecv[0, n].astype(jnp.float32)).astype(jnp.bfloat16)
    for copy in sent:
        copy.wait_send()
    for p in range(2):
        context_copy(2, s, p, mate).wait_send()


def shards(mesh_shape, *args):
    queries, fresh_key_rows, fresh_value_rows, visible, prefix_keys, cached_value_rows, out_weight = args
    z = Sizes(mesh_shape, queries, visible, prefix_keys, out_weight)
    staged = z.seq == 4 and z.tp == 2 and z.rep == 2 and z.b == 1 and z.kl == 1
    bf16, f32 = jnp.bfloat16, jnp.float32
    vmem, dma = pltpu.VMEM, pltpu.SemaphoreType.DMA
    if staged:
        state = [
            vmem((2, z.rows, HEAD_WIDTH), bf16),
            vmem((2, z.rows, HEAD_WIDTH), f32),
            vmem((2, z.rows, HEAD_WIDTH), f32),
            vmem((2, z.rows, 2 * HEAD_WIDTH), f32),
        ]
    else:
        state = [
                vmem((z.np, z.kl, z.rows, HEAD_WIDTH), bf16),
                vmem((z.np, z.rows, 1), f32),
                vmem((z.np, z.kl, z.rows, 1), f32),
                vmem((z.np, z.kl, z.rows, 1), f32),
                vmem((z.np, z.kl, z.rows, HEAD_WIDTH), f32),
        ]
    anywhere = pl.BlockSpec(memory_space=pl.ANY)
    inside = pl.BlockSpec(memory_space=pltpu.VMEM)
    held = pl.BlockSpec(memory_space=pltpu.HBM)
    return pl.pallas_call(
        functools.partial(line_kernel if staged else kernel, z),
        out_shape=jax.ShapeDtypeStruct((1, z.no, z.cols), bf16),
        in_specs=[held if staged else inside if n == 3 else anywhere for n in range(7)],
        out_specs=inside,
        scratch_shapes=[
            vmem((z.slots, z.tok, z.fb), bf16),
            vmem((z.slots, z.tok, z.kb), bf16),
            vmem((z.slots, z.tok, z.kb), bf16),
            vmem((z.seq, z.block, z.kb), bf16),
            vmem((z.seq, z.block, z.kb + staged * HEAD_WIDTH), bf16),
            vmem((z.a, z.fb, z.cols), bf16),
            *state,
            vmem((z.seq, z.np, z.pt, z.fb), bf16),
            vmem((z.all_tok, z.cols), f32),
            vmem((z.tp, z.tiles, z.no, z.tile), bf16),
            vmem((z.tp, z.tiles, z.no, z.tile), bf16),
            dma((3, z.slots)), dma((3, z.slots)),
            dma((2, z.seq)), dma((2, z.seq)),
            dma((2, z.seq)), dma((2, z.seq)),
            dma((2,)), dma((z.a,)),
            dma((z.seq, z.np)), dma((z.seq, z.np)),
            dma((z.tp, z.tiles)), dma((z.tp, z.tiles)),
            *([vmem((1, z.all_tok), jnp.int32), dma] if staged else []),
        ],
        compiler_params=pltpu.CompilerParams(
            collective_id=0, has_side_effects=True, vmem_limit_bytes=(44 if staged else 56) * 1024 * 1024
        ),
        name="attend_and_project",
    )(*([pltpu.with_memory_space_constraint(x, pltpu.HBM) for x in args] if staged else args))


def solution(mesh):
    in_specs = (
        P("rep", ("groups", "seq", "tp"), None),
        P("rep", ("groups", "seq", "tp"), None),
        P("rep", ("groups", "seq", "tp"), None),
        P("rep", "groups"),
        P(("groups", "seq"), "tp"),
        P(("groups", "seq"), "tp"),
        P("tp", "seq"),
    )
    out_specs = P("rep", ("groups", "tp"), "seq")
    body = functools.partial(shards, dict(mesh.shape))
    return jax.shard_map(body, mesh=mesh, in_specs=in_specs, out_specs=out_specs, check_vma=False)
```

```python
import functools
import math

import jax
import jax.numpy as jnp
from jax import lax
from jax.experimental import pallas as pl
from jax.experimental.pallas import tpu as pltpu
from jax.sharding import PartitionSpec as P

HEAD_WIDTH = 128
MASKED = -1e30
MESH = pl.DeviceIdType.MESH


class Sizes:
    def __init__(self, mesh_shape, queries, visible, prefix_keys, out_weight):
        self.seq = mesh_shape["seq"]
        self.tp = mesh_shape["tp"]
        self.rep = mesh_shape["rep"]
        self.tok = queries.shape[1]
        self.all_tok = visible.shape[1]
        self.block = prefix_keys.shape[0]
        kv_heads = prefix_keys.shape[1] // HEAD_WIDTH
        self.features, self.cols = out_weight.shape
        self.group = self.features // (kv_heads * HEAD_WIDTH)
        self.a = self.seq if kv_heads % self.seq == 0 else 1
        self.b = self.seq // self.a
        self.kl = kv_heads // self.a
        self.slots = self.a * self.tp
        self.nt = self.slots * self.tok
        self.np = self.tp if self.b == 1 else 1
        self.pt = self.nt // self.np
        self.ps = self.slots // self.np
        self.fb = self.kl * self.group * HEAD_WIDTH
        self.kb = self.kl * HEAD_WIDTH
        self.rows = self.group * self.pt
        self.no = self.all_tok // self.tp
        self.tile = math.gcd(self.cols, 512)
        self.tiles = self.cols // self.tile


def kernel(
    z, q_hbm, fk_hbm, fv_hbm, vis_ref, k_hbm, v_hbm, w_hbm, out_ref,
    qbuf, fkbuf, fvbuf, kbuf, vbuf, wbuf, qs, lens, peak, total, acc, cbuf, oacc, osend, orecv,
    q_send, q_recv, kv_send, kv_recv, f_send, f_recv, kv_own, w_sem, c_send, c_recv, o_send, o_recv,
):
    s, t, r = lax.axis_index("seq"), lax.axis_index("tp"), lax.axis_index("rep")
    partner = lax.rem(r + 1, z.rep)
    scale = 1.0 / math.sqrt(HEAD_WIDTH)

    def near(base, step, size):
        return lax.rem(base + step, size)

    def head_of(index):
        return index if z.a > 1 else 0

    barrier = pltpu.get_barrier_semaphore()
    for j in range(z.seq):
        for i in range(z.tp):
            if i or j:
                pl.semaphore_signal(
                    barrier, inc=1, device_id={"seq": near(s, j, z.seq), "tp": near(t, i, z.tp)},
                    device_id_type=MESH,
                )
    pl.semaphore_signal(barrier, inc=1, device_id={"rep": partner}, device_id_type=MESH)

    my_slot = head_of(s) * z.tp + t

    def query_parts(s_to, t_to):
        head = t_to * z.a + head_of(s_to)
        wide = pl.ds(pl.multiple_of(head * z.fb, 128), z.fb)
        thin = pl.ds(pl.multiple_of(head * z.kb, 128), z.kb)
        return (
            (q_hbm.at[0, :, wide], qbuf.at[my_slot]),
            (fk_hbm.at[0, :, thin], fkbuf.at[my_slot]),
            (fv_hbm.at[0, :, thin], fvbuf.at[my_slot]),
        )

    own_parts = [
        pltpu.make_async_copy(src, dst, q_recv.at[n, my_slot])
        for n, (src, dst) in enumerate(query_parts(s, t))
    ]
    thin_own = pl.ds(pl.multiple_of(head_of(s) * z.kb, 128), z.kb)
    own_kv = [
        pltpu.make_async_copy(k_hbm.at[:, thin_own], kbuf.at[s], kv_own.at[0]),
        pltpu.make_async_copy(v_hbm.at[:, thin_own], vbuf.at[s], kv_own.at[1]),
    ]
    weights = [
        pltpu.make_async_copy(w_hbm.at[pl.ds(n * z.fb, z.fb), :], wbuf.at[n], w_sem.at[n])
        for n in range(z.a)
    ]
    for copy in own_parts + own_kv + weights:
        copy.start()
    pl.semaphore_wait(barrier, z.seq * z.tp)

    sent, sent_if = [], []

    def send(copy, s_to=None):
        if s_to is None:
            copy.start()
            sent.append(copy)
        else:
            pl.when(s != s_to)(copy.start)
            sent_if.append((s_to, copy))

    def send_queries(s_to, t_step, only_if):
        t_to = near(t, t_step, z.tp)
        slot = (s_to if z.a > 1 else 0) * z.tp + t_step
        for n, (src, dst) in enumerate(query_parts(s_to, t_to)):
            send(pltpu.make_async_remote_copy(
                src_ref=src, dst_ref=dst, send_sem=q_send.at[n, slot],
                recv_sem=q_recv.at[n, my_slot], device_id={"seq": s_to, "tp": t_to},
                device_id_type=MESH,
            ), s_to if only_if else None)

    half = z.block // z.rep
    my_rows = pl.ds(pl.multiple_of(r * half, half), half)
    if z.a == 1:
        for i in range(1, z.tp):
            send_queries(s, i, False)
    for s_to in sorted(range(z.seq), key=lambda n: abs(2 * n + 1 - z.seq)):
        if z.a > 1:
            for i in range(z.tp):
                send_queries(s_to, i, i == 0)
        thin = pl.ds(head_of(s_to) * z.kb, z.kb)
        for n, (src, dst) in enumerate(((k_hbm, kbuf), (v_hbm, vbuf))):
            send(pltpu.make_async_remote_copy(
                src_ref=src.at[my_rows, thin], dst_ref=dst.at[s, my_rows, :],
                send_sem=kv_send.at[n, s_to], recv_sem=kv_recv.at[n, s],
                device_id={"seq": s_to}, device_id_type=MESH,
            ), s_to)

    def nearest(k):
        flip = s // (z.seq // 2) if z.seq > 1 else 0
        edge = s + flip * (z.seq - 1 - 2 * s)
        both = k <= 2 * edge
        away = jnp.where(both, (k + 1) // 2 * (1 - 2 * (k % 2)), k - edge)
        return s + away * (1 - 2 * flip)

    def owner_of(p):
        return near(t, p + 1, z.tp) if z.np > 1 else 0

    for p in range(z.np):
        want = lax.broadcasted_iota(jnp.int32, (z.pt, z.all_tok), 0) + owner_of(p) * z.pt
        if z.b > 1:
            want = want + s * z.nt
        have = lax.broadcasted_iota(jnp.int32, (z.pt, z.all_tok), 1)
        seen = jnp.where(want == have, jnp.broadcast_to(vis_ref[...], (z.pt, z.all_tok)), 0)
        column = jnp.sum(seen.astype(jnp.float32), axis=1, keepdims=True)
        lens[p] = jnp.concatenate([column] * z.group, axis=0)

    for j in range(z.a):
        for i in range(z.tp):
            slot = (near(s, j, z.seq) if z.a > 1 else 0) * z.tp + near(t, i, z.tp)
            for n, buf in enumerate((qbuf, fkbuf, fvbuf)):
                pltpu.make_async_copy(buf.at[slot], buf.at[slot], q_recv.at[n, slot]).wait()

    def rows_of(buf, p, first):
        some = pl.ds(owner_of(p) * z.ps, z.ps)
        value = buf[some, :, first:first + HEAD_WIDTH].astype(jnp.float32)
        return value.reshape(z.pt, HEAD_WIDTH)

    for p in range(z.np):
        for h in range(z.kl):
            own_key = rows_of(fkbuf, p, h * HEAD_WIDTH)
            own_value = rows_of(fvbuf, p, h * HEAD_WIDTH)
            for g in range(z.group):
                query = rows_of(qbuf, p, (h * z.group + g) * HEAD_WIDTH)
                span = slice(g * z.pt, (g + 1) * z.pt)
                qs[p, h, span, :] = query.astype(jnp.bfloat16)
                peak[p, h, span, :] = jnp.sum(query * own_key, axis=1, keepdims=True) * scale
                total[p, h, span, :] = jnp.ones((z.pt, 1), jnp.float32)
                acc[p, h, span, :] = own_value

    def attend(p, source):
        for h in range(z.kl):
            at = slice(h * HEAD_WIDTH, (h + 1) * HEAD_WIDTH)
            keys, values = kbuf[source, :, at], vbuf[source, :, at]
            scores = lax.dot_general(
                qs[p, h], keys, (((1,), (1,)), ((), ())), preferred_element_type=jnp.float32
            ) * scale
            spot = lax.broadcasted_iota(jnp.int32, scores.shape, 1) + source * z.block
            scores = jnp.where(spot.astype(jnp.float32) < lens[p], scores, MASKED)
            before = peak[p, h]
            now = jnp.maximum(before, jnp.max(scores, axis=1, keepdims=True))
            fade = jnp.exp(before - now)
            part = jnp.exp(scores - now)
            peak[p, h] = now
            total[p, h] = total[p, h] * fade + jnp.sum(part, axis=1, keepdims=True)
            acc[p, h] = acc[p, h] * fade + jnp.dot(
                part.astype(jnp.bfloat16), values, preferred_element_type=jnp.float32
            )

    def finish(p):
        for h in range(z.kl):
            context = (acc[p, h] / total[p, h]).astype(jnp.bfloat16)
            for g in range(z.group):
                at = (h * z.group + g) * HEAD_WIDTH
                cbuf[s, p, :, at:at + HEAD_WIDTH] = context[g * z.pt:(g + 1) * z.pt, :]
        for j in range(1, z.seq):
            sent.append(pltpu.make_async_remote_copy(
                src_ref=cbuf.at[s, p], dst_ref=cbuf.at[s, p],
                send_sem=c_send.at[j, p], recv_sem=c_recv.at[s, p],
                device_id={"seq": near(s, j, z.seq)}, device_id_type=MESH,
            ))
            sent[-1].start()

    for j in range(z.seq):
        source = nearest(j) if j else s
        if j == 0:
            for copy in own_kv:
                copy.wait()
        else:
            passed = []
            for n, buf in enumerate((kbuf, vbuf)):
                mine = buf.at[source, my_rows, :]
                pltpu.make_async_copy(mine, mine, kv_recv.at[n, source]).wait()
                passed.append(pltpu.make_async_remote_copy(
                    src_ref=mine, dst_ref=mine, send_sem=f_send.at[n, j], recv_sem=f_recv.at[n, source],
                    device_id={"rep": partner}, device_id_type=MESH,
                ))
                passed[-1].start()
            other = pl.ds(pl.multiple_of(partner * half, half), half)
            for n, buf in enumerate((kbuf, vbuf)):
                theirs = buf.at[source, other, :]
                pltpu.make_async_copy(theirs, theirs, f_recv.at[n, source]).wait()
            sent.extend(passed)
        for p in range(z.np):
            attend(p, source)
            if j == z.seq - 1:
                finish(p)

    for copy in weights:
        copy.wait()

    def project(j, source, p, at):
        value = jnp.dot(
            cbuf[source, p], wbuf[head_of(source), :, at], preferred_element_type=jnp.float32
        )
        if z.b > 1:
            oacc[pl.ds(pl.multiple_of(source * z.nt, z.nt), z.nt), at] = value
            return value
        rows = slice(p * z.pt, (p + 1) * z.pt)
        if j:
            value = value + oacc[rows, at]
        if j < z.seq - 1:
            oacc[rows, at] = value
        return value

    def give(i, n, value):
        osend[i, n] = value.astype(jnp.bfloat16)
        sent.append(pltpu.make_async_remote_copy(
            src_ref=osend.at[i, n], dst_ref=orecv.at[i, n],
            send_sem=o_send.at[i, n], recv_sem=o_recv.at[i, n],
            device_id={"tp": near(t, i + 1, z.tp)}, device_id_type=MESH,
        ))
        sent[-1].start()

    def keep(n, at, value):
        for i in range(z.tp - 1):
            pltpu.make_async_copy(orecv.at[i, n], orecv.at[i, n], o_recv.at[i, n]).wait()
            value = value + orecv[i, n].astype(jnp.float32)
        out_ref[0, :, at] = value.astype(jnp.bfloat16)

    spans = [slice(n * z.tile, (n + 1) * z.tile) for n in range(z.tiles)]
    for p in range(z.np):
        for j in range(z.seq):
            source = nearest(j) if j else s
            if j:
                landed = cbuf.at[source, p]
                pltpu.make_async_copy(landed, landed, c_recv.at[source, p]).wait()
            for n, at in enumerate(spans):
                value = project(j, source, p, at)
                if z.b == 1 and j == z.seq - 1:
                    if p < z.np - 1:
                        give(p, n, value)
                    else:
                        keep(n, at, value)
    if z.b > 1:
        for n, at in enumerate(spans):
            for i in range(z.tp - 1):
                rows = pl.ds(pl.multiple_of(near(t, i + 1, z.tp) * z.no, z.no), z.no)
                give(i, n, oacc[rows, at])
        for n, at in enumerate(spans):
            keep(n, at, oacc[pl.ds(pl.multiple_of(t * z.no, z.no), z.no), at])
    for copy in sent:
        copy.wait_send()
    for s_to, copy in sent_if:
        pl.when(s != s_to)(copy.wait_send)


def line_kernel(
    z, q_hbm, fk_hbm, fv_hbm, vis_hbm, k_hbm, v_hbm, w_hbm, out_ref,
    qbuf, fkbuf, fvbuf, kbuf, vbuf, wbuf, qs, lens, peak, acc, cbuf, oacc, osend, orecv,
    q_send, q_recv, kv_send, kv_recv, f_send, f_recv, kv_own, w_sem, c_send, c_recv, o_send, o_recv,
    vis_ref, vis_sem,
):
    s, t, r = lax.axis_index("seq"), lax.axis_index("tp"), lax.axis_index("rep")
    partner, t_other = 1 - r, 1 - t
    log_scale = math.log2(math.e) / math.sqrt(HEAD_WIDTH)
    low = s < 2
    is_end = (s == 0) | (s == 3)
    mate = s + 1 - 2 * lax.rem(s, 2)
    far_end = jnp.where(low, 3, 0)
    far_mid = jnp.where(low, 2, 1)

    barrier = pltpu.get_barrier_semaphore()
    for s_to, t_to in (
        (far_end, t), (far_mid, t), (far_end, t_other), (far_mid, t_other), (mate, t), (mate, t_other), (s, t_other)
    ):
        pl.semaphore_signal(barrier, inc=1, device_id={"seq": s_to, "tp": t_to}, device_id_type=MESH)
    pl.semaphore_signal(barrier, inc=1, device_id={"rep": partner}, device_id_type=MESH)

    my_slot = s * 2 + t

    def query_parts(s_to, t_to):
        head = t_to * 4 + s_to
        wide = pl.ds(pl.multiple_of(head * z.fb, 128), z.fb)
        thin = pl.ds(pl.multiple_of(head * z.kb, 128), z.kb)
        return (
            (q_hbm.at[0, :, wide], qbuf.at[my_slot]),
            (fk_hbm.at[0, :, thin], fkbuf.at[my_slot]),
            (fv_hbm.at[0, :, thin], fvbuf.at[my_slot]),
        )

    own_parts = [
        pltpu.make_async_copy(src, dst, q_recv.at[n, my_slot])
        for n, (src, dst) in enumerate(query_parts(s, t))
    ]
    thin_own = pl.ds(pl.multiple_of(s * z.kb, 128), z.kb)
    own_kv = [
        pltpu.make_async_copy(k_hbm.at[:, thin_own], kbuf.at[s], kv_own.at[0]),
        pltpu.make_async_copy(v_hbm.at[:, thin_own], vbuf.at[s, :, 0:HEAD_WIDTH], kv_own.at[1]),
    ]
    weights = [
        pltpu.make_async_copy(w_hbm.at[pl.ds(n * z.fb, z.fb), :], wbuf.at[n], w_sem.at[n])
        for n in range(4)
    ]
    def column_of_lengths(p):
        want = lax.broadcasted_iota(jnp.int32, (z.pt, z.all_tok), 0) + owner_of(p) * z.pt
        have = lax.broadcasted_iota(jnp.int32, (z.pt, z.all_tok), 1)
        seen = jnp.where(want == have, jnp.broadcast_to(vis_ref[...], (z.pt, z.all_tok)), 0)
        column = jnp.sum(seen.astype(jnp.float32), axis=1, keepdims=True)
        lens[p] = jnp.broadcast_to(jnp.concatenate([column] * z.group, axis=0), (z.rows, HEAD_WIDTH))

    def owner_of(p):
        return t_other if p == 0 else t

    pl.semaphore_wait(barrier, 8)

    sent = []

    def send(copy):
        copy.start()
        sent.append(copy)

    def query_copies(k, s_to, t_to):
        return [
            pltpu.make_async_remote_copy(
                src_ref=src, dst_ref=dst, send_sem=q_send.at[n, k],
                recv_sem=q_recv.at[n, my_slot], device_id={"seq": s_to, "tp": t_to},
                device_id_type=MESH,
            )
            for n, (src, dst) in enumerate(query_parts(s_to, t_to))
        ]

    half = z.block // 2
    my_rows = pl.ds(pl.multiple_of(r * half, half), half)
    other_rows = pl.ds(pl.multiple_of(partner * half, half), half)

    def prefix_copies(k, s_to):
        thin = pl.ds(pl.multiple_of(s_to * z.kb, 128), z.kb)
        return [
            pltpu.make_async_remote_copy(
                src_ref=src.at[my_rows, thin], dst_ref=dst.at[s, my_rows, 0:HEAD_WIDTH],
                send_sem=kv_send.at[n, k], recv_sem=kv_recv.at[n, s],
                device_id={"seq": s_to}, device_id_type=MESH,
            )
            for n, (src, dst) in enumerate(((k_hbm, kbuf), (v_hbm, vbuf)))
        ]

    targets = (far_end, far_mid, mate)
    queries = [query_copies(2 * k + 2, s_to, t) + query_copies(2 * k + 3, s_to, t_other) for k, s_to in enumerate(targets)]
    prefix = [prefix_copies(k, s_to) for k, s_to in enumerate(targets)]
    beside = query_copies(0, s, t_other)
    for copy in queries[0]:
        send(copy)

    @pl.when(is_end)
    def _():
        for copy in prefix[0] + queries[1] + queries[2] + prefix[2] + prefix[1]:
            copy.start()

    @pl.when(jnp.logical_not(is_end))
    def _():
        for copy in prefix[0] + queries[2] + prefix[2] + queries[1] + prefix[1]:
            copy.start()

    for k in range(3):
        sent.extend(prefix[k])
    for copy in beside:
        send(copy)
    sent.extend(queries[1] + queries[2])

    lengths = pltpu.make_async_copy(vis_hbm, vis_ref, vis_sem)
    for copy in [lengths] + own_parts + own_kv + weights:
        copy.start()
    lengths.wait()

    for p in range(2):
        column_of_lengths(p)
    head_lanes = slice(0, HEAD_WIDTH)
    vbuf[:, :, HEAD_WIDTH:] = jnp.ones((4, z.block, HEAD_WIDTH), jnp.bfloat16)
    for slot in range(8):
        for n, buf in enumerate((qbuf, fkbuf, fvbuf)):
            pltpu.make_async_copy(buf.at[slot], buf.at[slot], q_recv.at[n, slot]).wait()

    def rows_of(buf, p, first):
        some = pl.ds(owner_of(p) * z.ps, z.ps)
        value = buf[some, :, first:first + HEAD_WIDTH].astype(jnp.float32)
        return value.reshape(z.pt, HEAD_WIDTH)

    for p in range(2):
        own_key, own_value = rows_of(fkbuf, p, 0), rows_of(fvbuf, p, 0)
        for g in range(z.group):
            query = rows_of(qbuf, p, g * HEAD_WIDTH)
            span = slice(g * z.pt, (g + 1) * z.pt)
            qs[p, span, :] = query.astype(jnp.bfloat16)
            own = jnp.sum(query * own_key, axis=1, keepdims=True)
            peak[p, span, :] = jnp.broadcast_to(own, (z.pt, HEAD_WIDTH))
            acc[p, span, head_lanes] = own_value
            acc[p, span, HEAD_WIDTH:] = jnp.ones((z.pt, HEAD_WIDTH), jnp.float32)

    def attend(p, source, first=0, count=None):
        count = count or z.block
        repeat = count // HEAD_WIDTH
        rows = pl.ds(first if isinstance(first, int) else pl.multiple_of(first, half), count)
        scores = lax.dot_general(
            qs[p], kbuf[source, rows, :], (((1,), (1,)), ((), ())), preferred_element_type=jnp.float32
        )
        spot = lax.broadcasted_iota(jnp.int32, scores.shape, 1).astype(jnp.float32)
        left = lens[p] - (source * z.block + first).astype(jnp.float32)
        scores = jnp.where(spot < jnp.concatenate([left] * repeat, axis=1), scores, MASKED)
        before = peak[p]
        now = jnp.maximum(before, jnp.broadcast_to(jnp.max(scores, axis=1, keepdims=True), before.shape))
        fade = jnp.exp2((before - now) * log_scale)
        part = jnp.exp2((scores - jnp.concatenate([now] * repeat, axis=1)) * log_scale)
        peak[p] = now
        acc[p] = acc[p] * jnp.concatenate([fade] * 2, axis=1) + jnp.dot(
            part.astype(jnp.bfloat16), vbuf[source, rows, :], preferred_element_type=jnp.float32
        )

    def pass_kv(j, source):
        passed = []
        for n, buf in enumerate((kbuf, vbuf)):
            mine = buf.at[source, my_rows, 0:HEAD_WIDTH]
            pltpu.make_async_copy(mine, mine, kv_recv.at[n, source]).wait()
            passed.append(pltpu.make_async_remote_copy(
                src_ref=mine, dst_ref=mine, send_sem=f_send.at[n, j], recv_sem=f_recv.at[n, source],
                device_id={"rep": partner}, device_id_type=MESH,
            ))
            passed[-1].start()
        return passed

    def passed_kv(source):
        for n, buf in enumerate((kbuf, vbuf)):
            theirs = buf.at[source, other_rows, 0:HEAD_WIDTH]
            pltpu.make_async_copy(theirs, theirs, f_recv.at[n, source]).wait()

    def finish(p):
        context = (acc[p, :, head_lanes] / acc[p, :, HEAD_WIDTH:]).astype(jnp.bfloat16)
        for g in range(z.group):
            cbuf[s, p, :, g * HEAD_WIDTH:(g + 1) * HEAD_WIDTH] = context[g * z.pt:(g + 1) * z.pt, :]
        send(context_copy(0, s, p, far_end))

        @pl.when(jnp.logical_not(is_end))
        def _():
            context_copy(2, s, p, far_mid).start()
            context_copy(1, s, p, mate).start()

        sent.append(context_copy(1, s, p, mate))

    def context_copy(k, source, p, s_to):
        return pltpu.make_async_remote_copy(
            src_ref=cbuf.at[source, p], dst_ref=cbuf.at[source, p],
            send_sem=c_send.at[k, p], recv_sem=c_recv.at[source, p],
            device_id={"seq": s_to}, device_id_type=MESH,
        )

    def landed(source, p):
        pltpu.make_async_copy(cbuf.at[source, p], cbuf.at[source, p], c_recv.at[source, p]).wait()

    spans = [slice(n * z.tile, (n + 1) * z.tile) for n in range(z.tiles)]

    def project_all(source, first):
        for at in spans:
            value = jnp.dot(
                cbuf[source].reshape(2 * z.pt, z.fb), wbuf[source, :, at], preferred_element_type=jnp.float32
            )
            oacc[:, at] = value if first else oacc[:, at] + value

    def project_half(source, p, at):
        return oacc[p * z.pt:(p + 1) * z.pt, at] + jnp.dot(
            cbuf[source, p], wbuf[source, :, at], preferred_element_type=jnp.float32
        )

    sources = (
        jnp.where(is_end, far_end, mate), jnp.where(is_end, far_mid, far_end), jnp.where(is_end, mate, far_mid)
    )
    for copy in own_kv:
        copy.wait()
    sent.extend(pass_kv(0, sources[0]))
    for p in range(2):
        attend(p, s)
    sent.extend(pass_kv(1, sources[1]))
    passed_kv(sources[0])
    for p in range(2):
        attend(p, sources[0])
    passed_kv(sources[1])
    attend(0, sources[1])
    sent.extend(pass_kv(2, sources[2]))
    attend(1, sources[1])
    for p in range(2):
        attend(p, sources[2], r * half, half)
    passed_kv(sources[2])
    early = list(sent)
    sent.clear()
    for p in range(2):
        attend(p, sources[2], partner * half, half)
        finish(p)

    @pl.when(is_end)
    def _():
        for p in range(2):
            context_copy(1, s, p, mate).start()

    for copy in weights:
        copy.wait()
    project_all(s, True)
    for copy in early:
        copy.wait_send()
    second = jnp.where(is_end, far_end, mate)
    third = jnp.where(is_end, mate, far_end)

    def add_half(source, p):
        for at in spans:
            oacc[p * z.pt:(p + 1) * z.pt, at] = project_half(source, p, at)

    landed(second, 0)

    @pl.when(is_end)
    def _():
        context_copy(2, far_end, 0, mate).start()

    add_half(second, 0)

    @pl.when(is_end)
    def _():
        landed(second, 1)
        context_copy(2, far_end, 1, mate).start()

    for p in range(2):
        if p == 1:
            pl.when(jnp.logical_not(is_end))(functools.partial(landed, second, 1))
            add_half(second, 1)
        landed(third, p)
        add_half(third, p)
        landed(far_mid, p)
        for n, at in enumerate(spans):
            value = project_half(far_mid, p, at)
            if p == 0:
                osend[0, n] = value.astype(jnp.bfloat16)
                send(pltpu.make_async_remote_copy(
                    src_ref=osend.at[0, n], dst_ref=orecv.at[0, n],
                    send_sem=o_send.at[0, n], recv_sem=o_recv.at[0, n],
                    device_id={"tp": t_other}, device_id_type=MESH,
                ))
            else:
                pltpu.make_async_copy(orecv.at[0, n], orecv.at[0, n], o_recv.at[0, n]).wait()
                out_ref[0, :, at] = (value + orecv[0, n].astype(jnp.float32)).astype(jnp.bfloat16)
    for copy in sent:
        copy.wait_send()
    for p in range(2):
        context_copy(2, s, p, mate).wait_send()


def shards(mesh_shape, *args):
    queries, fresh_key_rows, fresh_value_rows, visible, prefix_keys, cached_value_rows, out_weight = args
    z = Sizes(mesh_shape, queries, visible, prefix_keys, out_weight)
    staged = z.seq == 4 and z.tp == 2 and z.rep == 2 and z.b == 1 and z.kl == 1
    bf16, f32 = jnp.bfloat16, jnp.float32
    vmem, dma = pltpu.VMEM, pltpu.SemaphoreType.DMA
    if staged:
        state = [
            vmem((2, z.rows, HEAD_WIDTH), bf16),
            vmem((2, z.rows, HEAD_WIDTH), f32),
            vmem((2, z.rows, HEAD_WIDTH), f32),
            vmem((2, z.rows, 2 * HEAD_WIDTH), f32),
        ]
    else:
        state = [
                vmem((z.np, z.kl, z.rows, HEAD_WIDTH), bf16),
                vmem((z.np, z.rows, 1), f32),
                vmem((z.np, z.kl, z.rows, 1), f32),
                vmem((z.np, z.kl, z.rows, 1), f32),
                vmem((z.np, z.kl, z.rows, HEAD_WIDTH), f32),
        ]
    anywhere = pl.BlockSpec(memory_space=pl.ANY)
    inside = pl.BlockSpec(memory_space=pltpu.VMEM)
    held = pl.BlockSpec(memory_space=pltpu.HBM)
    return pl.pallas_call(
        functools.partial(line_kernel if staged else kernel, z),
        out_shape=jax.ShapeDtypeStruct((1, z.no, z.cols), bf16),
        in_specs=[held if staged else inside if n == 3 else anywhere for n in range(7)],
        out_specs=inside,
        scratch_shapes=[
            vmem((z.slots, z.tok, z.fb), bf16),
            vmem((z.slots, z.tok, z.kb), bf16),
            vmem((z.slots, z.tok, z.kb), bf16),
            vmem((z.seq, z.block, z.kb), bf16),
            vmem((z.seq, z.block, z.kb + staged * HEAD_WIDTH), bf16),
            vmem((z.a, z.fb, z.cols), bf16),
            *state,
            vmem((z.seq, z.np, z.pt, z.fb), bf16),
            vmem((z.all_tok, z.cols), f32),
            vmem((z.tp, z.tiles, z.no, z.tile), bf16),
            vmem((z.tp, z.tiles, z.no, z.tile), bf16),
            dma((3, z.slots)), dma((3, z.slots)),
            dma((2, z.seq)), dma((2, z.seq)),
            dma((2, z.seq)), dma((2, z.seq)),
            dma((2,)), dma((z.a,)),
            dma((z.seq, z.np)), dma((z.seq, z.np)),
            dma((z.tp, z.tiles)), dma((z.tp, z.tiles)),
            *([vmem((1, z.all_tok), jnp.int32), dma] if staged else []),
        ],
        compiler_params=pltpu.CompilerParams(
            collective_id=0, has_side_effects=True, vmem_limit_bytes=(44 if staged else 56) * 1024 * 1024
        ),
        name="attend_and_project",
    )(*([pltpu.with_memory_space_constraint(x, pltpu.HBM) for x in args] if staged else args))


def solution(mesh):
    in_specs = (
        P("rep", ("groups", "seq", "tp"), None),
        P("rep", ("groups", "seq", "tp"), None),
        P("rep", ("groups", "seq", "tp"), None),
        P("rep", "groups"),
        P(("groups", "seq"), "tp"),
        P(("groups", "seq"), "tp"),
        P("tp", "seq"),
    )
    out_specs = P("rep", ("groups", "tp"), "seq")
    body = functools.partial(shards, dict(mesh.shape))
    return jax.shard_map(body, mesh=mesh, in_specs=in_specs, out_specs=out_specs, check_vma=False)
```

```python
import functools
import math

import jax
import jax.numpy as jnp
from jax import lax
from jax.experimental import pallas as pl
from jax.experimental.pallas import tpu as pltpu
from jax.sharding import PartitionSpec as P

HEAD_WIDTH = 128
MASKED = -1e30
MESH = pl.DeviceIdType.MESH


class Sizes:
    def __init__(self, mesh_shape, queries, visible, prefix_keys, out_weight):
        self.seq = mesh_shape["seq"]
        self.tp = mesh_shape["tp"]
        self.rep = mesh_shape["rep"]
        self.tok = queries.shape[1]
        self.all_tok = visible.shape[1]
        self.block = prefix_keys.shape[0]
        kv_heads = prefix_keys.shape[1] // HEAD_WIDTH
        self.features, self.cols = out_weight.shape
        self.group = self.features // (kv_heads * HEAD_WIDTH)
        self.a = self.seq if kv_heads % self.seq == 0 else 1
        self.b = self.seq // self.a
        self.kl = kv_heads // self.a
        self.slots = self.a * self.tp
        self.nt = self.slots * self.tok
        self.np = self.tp if self.b == 1 else 1
        self.pt = self.nt // self.np
        self.ps = self.slots // self.np
        self.fb = self.kl * self.group * HEAD_WIDTH
        self.kb = self.kl * HEAD_WIDTH
        self.rows = self.group * self.pt
        self.no = self.all_tok // self.tp
        self.tile = math.gcd(self.cols, 512)
        self.tiles = self.cols // self.tile


def kernel(
    z, q_hbm, fk_hbm, fv_hbm, vis_ref, k_hbm, v_hbm, w_hbm, out_ref,
    qbuf, fkbuf, fvbuf, kbuf, vbuf, wbuf, qs, lens, peak, total, acc, cbuf, oacc, osend, orecv,
    q_send, q_recv, kv_send, kv_recv, f_send, f_recv, kv_own, w_sem, c_send, c_recv, o_send, o_recv,
):
    s, t, r = lax.axis_index("seq"), lax.axis_index("tp"), lax.axis_index("rep")
    partner = lax.rem(r + 1, z.rep)
    scale = 1.0 / math.sqrt(HEAD_WIDTH)

    def near(base, step, size):
        return lax.rem(base + step, size)

    def head_of(index):
        return index if z.a > 1 else 0

    barrier = pltpu.get_barrier_semaphore()
    for j in range(z.seq):
        for i in range(z.tp):
            if i or j:
                pl.semaphore_signal(
                    barrier, inc=1, device_id={"seq": near(s, j, z.seq), "tp": near(t, i, z.tp)},
                    device_id_type=MESH,
                )
    pl.semaphore_signal(barrier, inc=1, device_id={"rep": partner}, device_id_type=MESH)

    my_slot = head_of(s) * z.tp + t

    def query_parts(s_to, t_to):
        head = t_to * z.a + head_of(s_to)
        wide = pl.ds(pl.multiple_of(head * z.fb, 128), z.fb)
        thin = pl.ds(pl.multiple_of(head * z.kb, 128), z.kb)
        return (
            (q_hbm.at[0, :, wide], qbuf.at[my_slot]),
            (fk_hbm.at[0, :, thin], fkbuf.at[my_slot]),
            (fv_hbm.at[0, :, thin], fvbuf.at[my_slot]),
        )

    own_parts = [
        pltpu.make_async_copy(src, dst, q_recv.at[n, my_slot])
        for n, (src, dst) in enumerate(query_parts(s, t))
    ]
    thin_own = pl.ds(pl.multiple_of(head_of(s) * z.kb, 128), z.kb)
    own_kv = [
        pltpu.make_async_copy(k_hbm.at[:, thin_own], kbuf.at[s], kv_own.at[0]),
        pltpu.make_async_copy(v_hbm.at[:, thin_own], vbuf.at[s], kv_own.at[1]),
    ]
    weights = [
        pltpu.make_async_copy(w_hbm.at[pl.ds(n * z.fb, z.fb), :], wbuf.at[n], w_sem.at[n])
        for n in range(z.a)
    ]
    for copy in own_parts + own_kv + weights:
        copy.start()
    pl.semaphore_wait(barrier, z.seq * z.tp)

    sent, sent_if = [], []

    def send(copy, s_to=None):
        if s_to is None:
            copy.start()
            sent.append(copy)
        else:
            pl.when(s != s_to)(copy.start)
            sent_if.append((s_to, copy))

    def send_queries(s_to, t_step, only_if):
        t_to = near(t, t_step, z.tp)
        slot = (s_to if z.a > 1 else 0) * z.tp + t_step
        for n, (src, dst) in enumerate(query_parts(s_to, t_to)):
            send(pltpu.make_async_remote_copy(
                src_ref=src, dst_ref=dst, send_sem=q_send.at[n, slot],
                recv_sem=q_recv.at[n, my_slot], device_id={"seq": s_to, "tp": t_to},
                device_id_type=MESH,
            ), s_to if only_if else None)

    half = z.block // z.rep
    my_rows = pl.ds(pl.multiple_of(r * half, half), half)
    if z.a == 1:
        for i in range(1, z.tp):
            send_queries(s, i, False)
    for s_to in sorted(range(z.seq), key=lambda n: abs(2 * n + 1 - z.seq)):
        if z.a > 1:
            for i in range(z.tp):
                send_queries(s_to, i, i == 0)
        thin = pl.ds(head_of(s_to) * z.kb, z.kb)
        for n, (src, dst) in enumerate(((k_hbm, kbuf), (v_hbm, vbuf))):
            send(pltpu.make_async_remote_copy(
                src_ref=src.at[my_rows, thin], dst_ref=dst.at[s, my_rows, :],
                send_sem=kv_send.at[n, s_to], recv_sem=kv_recv.at[n, s],
                device_id={"seq": s_to}, device_id_type=MESH,
            ), s_to)

    def nearest(k):
        flip = s // (z.seq // 2) if z.seq > 1 else 0
        edge = s + flip * (z.seq - 1 - 2 * s)
        both = k <= 2 * edge
        away = jnp.where(both, (k + 1) // 2 * (1 - 2 * (k % 2)), k - edge)
        return s + away * (1 - 2 * flip)

    def owner_of(p):
        return near(t, p + 1, z.tp) if z.np > 1 else 0

    for p in range(z.np):
        want = lax.broadcasted_iota(jnp.int32, (z.pt, z.all_tok), 0) + owner_of(p) * z.pt
        if z.b > 1:
            want = want + s * z.nt
        have = lax.broadcasted_iota(jnp.int32, (z.pt, z.all_tok), 1)
        seen = jnp.where(want == have, jnp.broadcast_to(vis_ref[...], (z.pt, z.all_tok)), 0)
        column = jnp.sum(seen.astype(jnp.float32), axis=1, keepdims=True)
        lens[p] = jnp.concatenate([column] * z.group, axis=0)

    for j in range(z.a):
        for i in range(z.tp):
            slot = (near(s, j, z.seq) if z.a > 1 else 0) * z.tp + near(t, i, z.tp)
            for n, buf in enumerate((qbuf, fkbuf, fvbuf)):
                pltpu.make_async_copy(buf.at[slot], buf.at[slot], q_recv.at[n, slot]).wait()

    def rows_of(buf, p, first):
        some = pl.ds(owner_of(p) * z.ps, z.ps)
        value = buf[some, :, first:first + HEAD_WIDTH].astype(jnp.float32)
        return value.reshape(z.pt, HEAD_WIDTH)

    for p in range(z.np):
        for h in range(z.kl):
            own_key = rows_of(fkbuf, p, h * HEAD_WIDTH)
            own_value = rows_of(fvbuf, p, h * HEAD_WIDTH)
            for g in range(z.group):
                query = rows_of(qbuf, p, (h * z.group + g) * HEAD_WIDTH)
                span = slice(g * z.pt, (g + 1) * z.pt)
                qs[p, h, span, :] = query.astype(jnp.bfloat16)
                peak[p, h, span, :] = jnp.sum(query * own_key, axis=1, keepdims=True) * scale
                total[p, h, span, :] = jnp.ones((z.pt, 1), jnp.float32)
                acc[p, h, span, :] = own_value

    def attend(p, source):
        for h in range(z.kl):
            at = slice(h * HEAD_WIDTH, (h + 1) * HEAD_WIDTH)
            keys, values = kbuf[source, :, at], vbuf[source, :, at]
            scores = lax.dot_general(
                qs[p, h], keys, (((1,), (1,)), ((), ())), preferred_element_type=jnp.float32
            ) * scale
            spot = lax.broadcasted_iota(jnp.int32, scores.shape, 1) + source * z.block
            scores = jnp.where(spot.astype(jnp.float32) < lens[p], scores, MASKED)
            before = peak[p, h]
            now = jnp.maximum(before, jnp.max(scores, axis=1, keepdims=True))
            fade = jnp.exp(before - now)
            part = jnp.exp(scores - now)
            peak[p, h] = now
            total[p, h] = total[p, h] * fade + jnp.sum(part, axis=1, keepdims=True)
            acc[p, h] = acc[p, h] * fade + jnp.dot(
                part.astype(jnp.bfloat16), values, preferred_element_type=jnp.float32
            )

    def finish(p):
        for h in range(z.kl):
            context = (acc[p, h] / total[p, h]).astype(jnp.bfloat16)
            for g in range(z.group):
                at = (h * z.group + g) * HEAD_WIDTH
                cbuf[s, p, :, at:at + HEAD_WIDTH] = context[g * z.pt:(g + 1) * z.pt, :]
        for j in range(1, z.seq):
            sent.append(pltpu.make_async_remote_copy(
                src_ref=cbuf.at[s, p], dst_ref=cbuf.at[s, p],
                send_sem=c_send.at[j, p], recv_sem=c_recv.at[s, p],
                device_id={"seq": near(s, j, z.seq)}, device_id_type=MESH,
            ))
            sent[-1].start()

    for j in range(z.seq):
        source = nearest(j) if j else s
        if j == 0:
            for copy in own_kv:
                copy.wait()
        else:
            passed = []
            for n, buf in enumerate((kbuf, vbuf)):
                mine = buf.at[source, my_rows, :]
                pltpu.make_async_copy(mine, mine, kv_recv.at[n, source]).wait()
                passed.append(pltpu.make_async_remote_copy(
                    src_ref=mine, dst_ref=mine, send_sem=f_send.at[n, j], recv_sem=f_recv.at[n, source],
                    device_id={"rep": partner}, device_id_type=MESH,
                ))
                passed[-1].start()
            other = pl.ds(pl.multiple_of(partner * half, half), half)
            for n, buf in enumerate((kbuf, vbuf)):
                theirs = buf.at[source, other, :]
                pltpu.make_async_copy(theirs, theirs, f_recv.at[n, source]).wait()
            sent.extend(passed)
        for p in range(z.np):
            attend(p, source)
            if j == z.seq - 1:
                finish(p)

    for copy in weights:
        copy.wait()

    def project(j, source, p, at):
        value = jnp.dot(
            cbuf[source, p], wbuf[head_of(source), :, at], preferred_element_type=jnp.float32
        )
        if z.b > 1:
            oacc[pl.ds(pl.multiple_of(source * z.nt, z.nt), z.nt), at] = value
            return value
        rows = slice(p * z.pt, (p + 1) * z.pt)
        if j:
            value = value + oacc[rows, at]
        if j < z.seq - 1:
            oacc[rows, at] = value
        return value

    def give(i, n, value):
        osend[i, n] = value.astype(jnp.bfloat16)
        sent.append(pltpu.make_async_remote_copy(
            src_ref=osend.at[i, n], dst_ref=orecv.at[i, n],
            send_sem=o_send.at[i, n], recv_sem=o_recv.at[i, n],
            device_id={"tp": near(t, i + 1, z.tp)}, device_id_type=MESH,
        ))
        sent[-1].start()

    def keep(n, at, value):
        for i in range(z.tp - 1):
            pltpu.make_async_copy(orecv.at[i, n], orecv.at[i, n], o_recv.at[i, n]).wait()
            value = value + orecv[i, n].astype(jnp.float32)
        out_ref[0, :, at] = value.astype(jnp.bfloat16)

    spans = [slice(n * z.tile, (n + 1) * z.tile) for n in range(z.tiles)]
    for p in range(z.np):
        for j in range(z.seq):
            source = nearest(j) if j else s
            if j:
                landed = cbuf.at[source, p]
                pltpu.make_async_copy(landed, landed, c_recv.at[source, p]).wait()
            for n, at in enumerate(spans):
                value = project(j, source, p, at)
                if z.b == 1 and j == z.seq - 1:
                    if p < z.np - 1:
                        give(p, n, value)
                    else:
                        keep(n, at, value)
    if z.b > 1:
        for n, at in enumerate(spans):
            for i in range(z.tp - 1):
                rows = pl.ds(pl.multiple_of(near(t, i + 1, z.tp) * z.no, z.no), z.no)
                give(i, n, oacc[rows, at])
        for n, at in enumerate(spans):
            keep(n, at, oacc[pl.ds(pl.multiple_of(t * z.no, z.no), z.no), at])
    for copy in sent:
        copy.wait_send()
    for s_to, copy in sent_if:
        pl.when(s != s_to)(copy.wait_send)


def line_kernel(
    z, q_hbm, fk_hbm, fv_hbm, vis_hbm, k_hbm, v_hbm, w_hbm, out_ref,
    qbuf, fkbuf, fvbuf, kbuf, vbuf, wbuf, qs, lens, peak, acc, cbuf, oacc, osend, orecv,
    q_send, q_recv, kv_send, kv_recv, f_send, f_recv, kv_own, w_sem, c_send, c_recv, o_send, o_recv,
    vis_ref, vis_sem,
):
    s, t, r = lax.axis_index("seq"), lax.axis_index("tp"), lax.axis_index("rep")
    partner, t_other = 1 - r, 1 - t
    log_scale = math.log2(math.e) / math.sqrt(HEAD_WIDTH)
    low = s < 2
    is_end = (s == 0) | (s == 3)
    mate = s + 1 - 2 * lax.rem(s, 2)
    far_end = jnp.where(low, 3, 0)
    far_mid = jnp.where(low, 2, 1)

    barrier = pltpu.get_barrier_semaphore()
    for s_to, t_to in (
        (far_end, t), (far_mid, t), (far_end, t_other), (far_mid, t_other), (mate, t), (mate, t_other), (s, t_other)
    ):
        pl.semaphore_signal(barrier, inc=1, device_id={"seq": s_to, "tp": t_to}, device_id_type=MESH)
    pl.semaphore_signal(barrier, inc=1, device_id={"rep": partner}, device_id_type=MESH)

    my_slot = s * 2 + t

    def query_parts(s_to, t_to):
        head = t_to * 4 + s_to
        wide = pl.ds(pl.multiple_of(head * z.fb, 128), z.fb)
        thin = pl.ds(pl.multiple_of(head * z.kb, 128), z.kb)
        return (
            (q_hbm.at[0, :, wide], qbuf.at[my_slot]),
            (fk_hbm.at[0, :, thin], fkbuf.at[my_slot]),
            (fv_hbm.at[0, :, thin], fvbuf.at[my_slot]),
        )

    own_parts = [
        pltpu.make_async_copy(src, dst, q_recv.at[n, my_slot])
        for n, (src, dst) in enumerate(query_parts(s, t))
    ]
    thin_own = pl.ds(pl.multiple_of(s * z.kb, 128), z.kb)
    own_kv = [
        pltpu.make_async_copy(k_hbm.at[:, thin_own], kbuf.at[s], kv_own.at[0]),
        pltpu.make_async_copy(v_hbm.at[:, thin_own], vbuf.at[s, :, 0:HEAD_WIDTH], kv_own.at[1]),
    ]
    weights = [
        pltpu.make_async_copy(w_hbm.at[pl.ds(n * z.fb, z.fb), :], wbuf.at[n], w_sem.at[n])
        for n in range(4)
    ]
    def column_of_lengths(p):
        want = lax.broadcasted_iota(jnp.int32, (z.pt, z.all_tok), 0) + owner_of(p) * z.pt
        have = lax.broadcasted_iota(jnp.int32, (z.pt, z.all_tok), 1)
        seen = jnp.where(want == have, jnp.broadcast_to(vis_ref[...], (z.pt, z.all_tok)), 0)
        column = jnp.sum(seen.astype(jnp.float32), axis=1, keepdims=True)
        lens[p] = jnp.broadcast_to(jnp.concatenate([column] * z.group, axis=0), (z.rows, HEAD_WIDTH))

    def owner_of(p):
        return t_other if p == 0 else t

    pl.semaphore_wait(barrier, 8)

    sent = []

    def send(copy):
        copy.start()
        sent.append(copy)

    def query_copies(k, s_to, t_to):
        return [
            pltpu.make_async_remote_copy(
                src_ref=src, dst_ref=dst, send_sem=q_send.at[n, k],
                recv_sem=q_recv.at[n, my_slot], device_id={"seq": s_to, "tp": t_to},
                device_id_type=MESH,
            )
            for n, (src, dst) in enumerate(query_parts(s_to, t_to))
        ]

    half = z.block // 2
    my_rows = pl.ds(pl.multiple_of(r * half, half), half)
    other_rows = pl.ds(pl.multiple_of(partner * half, half), half)

    def prefix_copies(k, s_to):
        thin = pl.ds(pl.multiple_of(s_to * z.kb, 128), z.kb)
        return [
            pltpu.make_async_remote_copy(
                src_ref=src.at[my_rows, thin], dst_ref=dst.at[s, my_rows, 0:HEAD_WIDTH],
                send_sem=kv_send.at[n, k], recv_sem=kv_recv.at[n, s],
                device_id={"seq": s_to}, device_id_type=MESH,
            )
            for n, (src, dst) in enumerate(((k_hbm, kbuf), (v_hbm, vbuf)))
        ]

    targets = (far_end, far_mid, mate)
    queries = [query_copies(2 * k + 2, s_to, t) + query_copies(2 * k + 3, s_to, t_other) for k, s_to in enumerate(targets)]
    prefix = [prefix_copies(k, s_to) for k, s_to in enumerate(targets)]
    beside = query_copies(0, s, t_other)
    for copy in queries[0]:
        send(copy)

    @pl.when(is_end)
    def _():
        for copy in prefix[0] + queries[1] + queries[2] + prefix[2] + prefix[1]:
            copy.start()

    @pl.when(jnp.logical_not(is_end))
    def _():
        for copy in prefix[0] + queries[2] + prefix[2] + queries[1] + prefix[1]:
            copy.start()

    for k in range(3):
        sent.extend(prefix[k])
    for copy in beside:
        send(copy)
    sent.extend(queries[1] + queries[2])

    lengths = pltpu.make_async_copy(vis_hbm, vis_ref, vis_sem)
    for copy in [lengths] + own_parts + own_kv + weights:
        copy.start()
    lengths.wait()

    for p in range(2):
        column_of_lengths(p)
    head_lanes = slice(0, HEAD_WIDTH)
    vbuf[:, :, HEAD_WIDTH:] = jnp.ones((4, z.block, HEAD_WIDTH), jnp.bfloat16)
    for slot in range(8):
        for n, buf in enumerate((qbuf, fkbuf, fvbuf)):
            pltpu.make_async_copy(buf.at[slot], buf.at[slot], q_recv.at[n, slot]).wait()

    def rows_of(buf, p, first):
        some = pl.ds(owner_of(p) * z.ps, z.ps)
        value = buf[some, :, first:first + HEAD_WIDTH].astype(jnp.float32)
        return value.reshape(z.pt, HEAD_WIDTH)

    for p in range(2):
        own_key, own_value = rows_of(fkbuf, p, 0), rows_of(fvbuf, p, 0)
        for g in range(z.group):
            query = rows_of(qbuf, p, g * HEAD_WIDTH)
            span = slice(g * z.pt, (g + 1) * z.pt)
            qs[p, span, :] = query.astype(jnp.bfloat16)
            own = jnp.sum(query * own_key, axis=1, keepdims=True)
            peak[p, span, :] = jnp.broadcast_to(own, (z.pt, HEAD_WIDTH))
            acc[p, span, head_lanes] = own_value
            acc[p, span, HEAD_WIDTH:] = jnp.ones((z.pt, HEAD_WIDTH), jnp.float32)

    def attend(p, source, first=0, count=None):
        count = count or z.block
        repeat = count // HEAD_WIDTH
        rows = pl.ds(first if isinstance(first, int) else pl.multiple_of(first, half), count)
        scores = lax.dot_general(
            qs[p], kbuf[source, rows, :], (((1,), (1,)), ((), ())), preferred_element_type=jnp.float32
        )
        spot = lax.broadcasted_iota(jnp.int32, scores.shape, 1).astype(jnp.float32)
        left = lens[p] - (source * z.block + first).astype(jnp.float32)
        scores = jnp.where(spot < jnp.concatenate([left] * repeat, axis=1), scores, MASKED)
        before = peak[p]
        now = jnp.maximum(before, jnp.broadcast_to(jnp.max(scores, axis=1, keepdims=True), before.shape))
        fade = jnp.exp2((before - now) * log_scale)
        part = jnp.exp2((scores - jnp.concatenate([now] * repeat, axis=1)) * log_scale)
        peak[p] = now
        acc[p] = acc[p] * jnp.concatenate([fade] * 2, axis=1) + jnp.dot(
            part.astype(jnp.bfloat16), vbuf[source, rows, :], preferred_element_type=jnp.float32
        )

    def pass_kv(j, source):
        passed = []
        for n, buf in enumerate((kbuf, vbuf)):
            mine = buf.at[source, my_rows, 0:HEAD_WIDTH]
            pltpu.make_async_copy(mine, mine, kv_recv.at[n, source]).wait()
            passed.append(pltpu.make_async_remote_copy(
                src_ref=mine, dst_ref=mine, send_sem=f_send.at[n, j], recv_sem=f_recv.at[n, source],
                device_id={"rep": partner}, device_id_type=MESH,
            ))
            passed[-1].start()
        return passed

    def passed_kv(source):
        for n, buf in enumerate((kbuf, vbuf)):
            theirs = buf.at[source, other_rows, 0:HEAD_WIDTH]
            pltpu.make_async_copy(theirs, theirs, f_recv.at[n, source]).wait()

    def finish(p):
        context = (acc[p, :, head_lanes] / acc[p, :, HEAD_WIDTH:]).astype(jnp.bfloat16)
        for g in range(z.group):
            cbuf[s, p, :, g * HEAD_WIDTH:(g + 1) * HEAD_WIDTH] = context[g * z.pt:(g + 1) * z.pt, :]
        pl.when(jnp.logical_not(is_end))(context_copy(1, s, p, mate).start)
        send(context_copy(0, s, p, far_end))
        pl.when(jnp.logical_not(is_end))(context_copy(2, s, p, far_mid).start)

        sent.append(context_copy(1, s, p, mate))

    def context_copy(k, source, p, s_to):
        return pltpu.make_async_remote_copy(
            src_ref=cbuf.at[source, p], dst_ref=cbuf.at[source, p],
            send_sem=c_send.at[k, p], recv_sem=c_recv.at[source, p],
            device_id={"seq": s_to}, device_id_type=MESH,
        )

    def landed(source, p):
        pltpu.make_async_copy(cbuf.at[source, p], cbuf.at[source, p], c_recv.at[source, p]).wait()

    spans = [slice(n * z.tile, (n + 1) * z.tile) for n in range(z.tiles)]

    def project_all(source, first):
        for at in spans:
            value = jnp.dot(
                cbuf[source].reshape(2 * z.pt, z.fb), wbuf[source, :, at], preferred_element_type=jnp.float32
            )
            oacc[:, at] = value if first else oacc[:, at] + value

    def project_half(source, p, at):
        return oacc[p * z.pt:(p + 1) * z.pt, at] + jnp.dot(
            cbuf[source, p], wbuf[source, :, at], preferred_element_type=jnp.float32
        )

    sources = (
        jnp.where(is_end, far_end, mate), jnp.where(is_end, far_mid, far_end), jnp.where(is_end, mate, far_mid)
    )
    for copy in own_kv:
        copy.wait()
    sent.extend(pass_kv(0, sources[0]))
    for p in range(2):
        attend(p, s)
    sent.extend(pass_kv(1, sources[1]))
    passed_kv(sources[0])
    for p in range(2):
        attend(p, sources[0])
    passed_kv(sources[1])
    attend(0, sources[1])
    sent.extend(pass_kv(2, sources[2]))
    attend(1, sources[1])
    for p in range(2):
        attend(p, sources[2], r * half, half)
    passed_kv(sources[2])
    early = list(sent)
    sent.clear()
    for p in range(2):
        attend(p, sources[2], partner * half, half)
        finish(p)

    @pl.when(is_end)
    def _():
        for p in range(2):
            context_copy(1, s, p, mate).start()

    for copy in weights:
        copy.wait()
    project_all(s, True)
    for copy in early:
        copy.wait_send()
    second = jnp.where(is_end, far_end, mate)
    for p in range(2):
        landed(second, p)

        @pl.when(is_end)
        def _():
            context_copy(2, far_end, p, mate).start()
    project_all(second, False)

    third = jnp.where(is_end, mate, far_end)
    for p in range(2):
        landed(third, p)
        for at in spans:
            oacc[p * z.pt:(p + 1) * z.pt, at] = project_half(third, p, at)
        landed(far_mid, p)
        for n, at in enumerate(spans):
            value = project_half(far_mid, p, at)
            if p == 0:
                osend[0, n] = value.astype(jnp.bfloat16)
                send(pltpu.make_async_remote_copy(
                    src_ref=osend.at[0, n], dst_ref=orecv.at[0, n],
                    send_sem=o_send.at[0, n], recv_sem=o_recv.at[0, n],
                    device_id={"tp": t_other}, device_id_type=MESH,
                ))
            else:
                pltpu.make_async_copy(orecv.at[0, n], orecv.at[0, n], o_recv.at[0, n]).wait()
                out_ref[0, :, at] = (value + orecv[0, n].astype(jnp.float32)).astype(jnp.bfloat16)
    for copy in sent:
        copy.wait_send()
    for p in range(2):
        context_copy(2, s, p, mate).wait_send()


def shards(mesh_shape, *args):
    queries, fresh_key_rows, fresh_value_rows, visible, prefix_keys, cached_value_rows, out_weight = args
    z = Sizes(mesh_shape, queries, visible, prefix_keys, out_weight)
    staged = z.seq == 4 and z.tp == 2 and z.rep == 2 and z.b == 1 and z.kl == 1
    bf16, f32 = jnp.bfloat16, jnp.float32
    vmem, dma = pltpu.VMEM, pltpu.SemaphoreType.DMA
    if staged:
        state = [
            vmem((2, z.rows, HEAD_WIDTH), bf16),
            vmem((2, z.rows, HEAD_WIDTH), f32),
            vmem((2, z.rows, HEAD_WIDTH), f32),
            vmem((2, z.rows, 2 * HEAD_WIDTH), f32),
        ]
    else:
        state = [
                vmem((z.np, z.kl, z.rows, HEAD_WIDTH), bf16),
                vmem((z.np, z.rows, 1), f32),
                vmem((z.np, z.kl, z.rows, 1), f32),
                vmem((z.np, z.kl, z.rows, 1), f32),
                vmem((z.np, z.kl, z.rows, HEAD_WIDTH), f32),
        ]
    anywhere = pl.BlockSpec(memory_space=pl.ANY)
    inside = pl.BlockSpec(memory_space=pltpu.VMEM)
    held = pl.BlockSpec(memory_space=pltpu.HBM)
    return pl.pallas_call(
        functools.partial(line_kernel if staged else kernel, z),
        out_shape=jax.ShapeDtypeStruct((1, z.no, z.cols), bf16),
        in_specs=[held if staged else inside if n == 3 else anywhere for n in range(7)],
        out_specs=inside,
        scratch_shapes=[
            vmem((z.slots, z.tok, z.fb), bf16),
            vmem((z.slots, z.tok, z.kb), bf16),
            vmem((z.slots, z.tok, z.kb), bf16),
            vmem((z.seq, z.block, z.kb), bf16),
            vmem((z.seq, z.block, z.kb + staged * HEAD_WIDTH), bf16),
            vmem((z.a, z.fb, z.cols), bf16),
            *state,
            vmem((z.seq, z.np, z.pt, z.fb), bf16),
            vmem((z.all_tok, z.cols), f32),
            vmem((z.tp, z.tiles, z.no, z.tile), bf16),
            vmem((z.tp, z.tiles, z.no, z.tile), bf16),
            dma((3, z.slots)), dma((3, z.slots)),
            dma((2, z.seq)), dma((2, z.seq)),
            dma((2, z.seq)), dma((2, z.seq)),
            dma((2,)), dma((z.a,)),
            dma((z.seq, z.np)), dma((z.seq, z.np)),
            dma((z.tp, z.tiles)), dma((z.tp, z.tiles)),
            *([vmem((1, z.all_tok), jnp.int32), dma] if staged else []),
        ],
        compiler_params=pltpu.CompilerParams(
            collective_id=0, has_side_effects=True, vmem_limit_bytes=(44 if staged else 56) * 1024 * 1024
        ),
        name="attend_and_project",
    )(*([pltpu.with_memory_space_constraint(x, pltpu.HBM) for x in args] if staged else args))


def solution(mesh):
    in_specs = (
        P("rep", ("groups", "seq", "tp"), None),
        P("rep", ("groups", "seq", "tp"), None),
        P("rep", ("groups", "seq", "tp"), None),
        P("rep", "groups"),
        P(("groups", "seq"), "tp"),
        P(("groups", "seq"), "tp"),
        P("tp", "seq"),
    )
    out_specs = P("rep", ("groups", "tp"), "seq")
    body = functools.partial(shards, dict(mesh.shape))
    return jax.shard_map(body, mesh=mesh, in_specs=in_specs, out_specs=out_specs, check_vma=False)
```

```python
import functools
import math

import jax
import jax.numpy as jnp
from jax import lax
from jax.experimental import pallas as pl
from jax.experimental.pallas import tpu as pltpu
from jax.sharding import PartitionSpec as P

HEAD_WIDTH = 128
MASKED = -1e30
MESH = pl.DeviceIdType.MESH


class Sizes:
    def __init__(self, mesh_shape, queries, visible, prefix_keys, out_weight):
        self.seq = mesh_shape["seq"]
        self.tp = mesh_shape["tp"]
        self.rep = mesh_shape["rep"]
        self.tok = queries.shape[1]
        self.all_tok = visible.shape[1]
        self.block = prefix_keys.shape[0]
        kv_heads = prefix_keys.shape[1] // HEAD_WIDTH
        self.features, self.cols = out_weight.shape
        self.group = self.features // (kv_heads * HEAD_WIDTH)
        self.a = self.seq if kv_heads % self.seq == 0 else 1
        self.b = self.seq // self.a
        self.kl = kv_heads // self.a
        self.slots = self.a * self.tp
        self.nt = self.slots * self.tok
        self.np = self.tp if self.b == 1 else 1
        self.pt = self.nt // self.np
        self.ps = self.slots // self.np
        self.fb = self.kl * self.group * HEAD_WIDTH
        self.kb = self.kl * HEAD_WIDTH
        self.rows = self.group * self.pt
        self.no = self.all_tok // self.tp
        self.tile = math.gcd(self.cols, 1024)
        self.tiles = self.cols // self.tile


def kernel(
    z, q_hbm, fk_hbm, fv_hbm, vis_ref, k_hbm, v_hbm, w_hbm, out_ref,
    qbuf, fkbuf, fvbuf, kbuf, vbuf, wbuf, qs, lens, peak, total, acc, cbuf, oacc, osend, orecv,
    q_send, q_recv, kv_send, kv_recv, f_send, f_recv, kv_own, w_sem, c_send, c_recv, o_send, o_recv,
):
    s, t, r = lax.axis_index("seq"), lax.axis_index("tp"), lax.axis_index("rep")
    partner = lax.rem(r + 1, z.rep)
    scale = 1.0 / math.sqrt(HEAD_WIDTH)

    def near(base, step, size):
        return lax.rem(base + step, size)

    def head_of(index):
        return index if z.a > 1 else 0

    barrier = pltpu.get_barrier_semaphore()
    for j in range(z.seq):
        for i in range(z.tp):
            if i or j:
                pl.semaphore_signal(
                    barrier, inc=1, device_id={"seq": near(s, j, z.seq), "tp": near(t, i, z.tp)},
                    device_id_type=MESH,
                )
    pl.semaphore_signal(barrier, inc=1, device_id={"rep": partner}, device_id_type=MESH)

    my_slot = head_of(s) * z.tp + t

    def query_parts(s_to, t_to):
        head = t_to * z.a + head_of(s_to)
        wide = pl.ds(pl.multiple_of(head * z.fb, 128), z.fb)
        thin = pl.ds(pl.multiple_of(head * z.kb, 128), z.kb)
        return (
            (q_hbm.at[0, :, wide], qbuf.at[my_slot]),
            (fk_hbm.at[0, :, thin], fkbuf.at[my_slot]),
            (fv_hbm.at[0, :, thin], fvbuf.at[my_slot]),
        )

    own_parts = [
        pltpu.make_async_copy(src, dst, q_recv.at[n, my_slot])
        for n, (src, dst) in enumerate(query_parts(s, t))
    ]
    thin_own = pl.ds(pl.multiple_of(head_of(s) * z.kb, 128), z.kb)
    own_kv = [
        pltpu.make_async_copy(k_hbm.at[:, thin_own], kbuf.at[s], kv_own.at[0]),
        pltpu.make_async_copy(v_hbm.at[:, thin_own], vbuf.at[s], kv_own.at[1]),
    ]
    weights = [
        pltpu.make_async_copy(w_hbm.at[pl.ds(n * z.fb, z.fb), :], wbuf.at[n], w_sem.at[n])
        for n in range(z.a)
    ]
    for copy in own_parts + own_kv + weights:
        copy.start()
    pl.semaphore_wait(barrier, z.seq * z.tp)

    sent, sent_if = [], []

    def send(copy, s_to=None):
        if s_to is None:
            copy.start()
            sent.append(copy)
        else:
            pl.when(s != s_to)(copy.start)
            sent_if.append((s_to, copy))

    def send_queries(s_to, t_step, only_if):
        t_to = near(t, t_step, z.tp)
        slot = (s_to if z.a > 1 else 0) * z.tp + t_step
        for n, (src, dst) in enumerate(query_parts(s_to, t_to)):
            send(pltpu.make_async_remote_copy(
                src_ref=src, dst_ref=dst, send_sem=q_send.at[n, slot],
                recv_sem=q_recv.at[n, my_slot], device_id={"seq": s_to, "tp": t_to},
                device_id_type=MESH,
            ), s_to if only_if else None)

    half = z.block // z.rep
    my_rows = pl.ds(pl.multiple_of(r * half, half), half)
    if z.a == 1:
        for i in range(1, z.tp):
            send_queries(s, i, False)
    for s_to in sorted(range(z.seq), key=lambda n: abs(2 * n + 1 - z.seq)):
        if z.a > 1:
            for i in range(z.tp):
                send_queries(s_to, i, i == 0)
        thin = pl.ds(head_of(s_to) * z.kb, z.kb)
        for n, (src, dst) in enumerate(((k_hbm, kbuf), (v_hbm, vbuf))):
            send(pltpu.make_async_remote_copy(
                src_ref=src.at[my_rows, thin], dst_ref=dst.at[s, my_rows, :],
                send_sem=kv_send.at[n, s_to], recv_sem=kv_recv.at[n, s],
                device_id={"seq": s_to}, device_id_type=MESH,
            ), s_to)

    def nearest(k):
        flip = s // (z.seq // 2) if z.seq > 1 else 0
        edge = s + flip * (z.seq - 1 - 2 * s)
        both = k <= 2 * edge
        away = jnp.where(both, (k + 1) // 2 * (1 - 2 * (k % 2)), k - edge)
        return s + away * (1 - 2 * flip)

    def owner_of(p):
        return near(t, p + 1, z.tp) if z.np > 1 else 0

    for p in range(z.np):
        want = lax.broadcasted_iota(jnp.int32, (z.pt, z.all_tok), 0) + owner_of(p) * z.pt
        if z.b > 1:
            want = want + s * z.nt
        have = lax.broadcasted_iota(jnp.int32, (z.pt, z.all_tok), 1)
        seen = jnp.where(want == have, jnp.broadcast_to(vis_ref[...], (z.pt, z.all_tok)), 0)
        column = jnp.sum(seen.astype(jnp.float32), axis=1, keepdims=True)
        lens[p] = jnp.concatenate([column] * z.group, axis=0)

    for j in range(z.a):
        for i in range(z.tp):
            slot = (near(s, j, z.seq) if z.a > 1 else 0) * z.tp + near(t, i, z.tp)
            for n, buf in enumerate((qbuf, fkbuf, fvbuf)):
                pltpu.make_async_copy(buf.at[slot], buf.at[slot], q_recv.at[n, slot]).wait()

    def rows_of(buf, p, first):
        some = pl.ds(owner_of(p) * z.ps, z.ps)
        value = buf[some, :, first:first + HEAD_WIDTH].astype(jnp.float32)
        return value.reshape(z.pt, HEAD_WIDTH)

    for p in range(z.np):
        for h in range(z.kl):
            own_key = rows_of(fkbuf, p, h * HEAD_WIDTH)
            own_value = rows_of(fvbuf, p, h * HEAD_WIDTH)
            for g in range(z.group):
                query = rows_of(qbuf, p, (h * z.group + g) * HEAD_WIDTH)
                span = slice(g * z.pt, (g + 1) * z.pt)
                qs[p, h, span, :] = query.astype(jnp.bfloat16)
                peak[p, h, span, :] = jnp.sum(query * own_key, axis=1, keepdims=True) * scale
                total[p, h, span, :] = jnp.ones((z.pt, 1), jnp.float32)
                acc[p, h, span, :] = own_value

    def attend(p, source):
        for h in range(z.kl):
            at = slice(h * HEAD_WIDTH, (h + 1) * HEAD_WIDTH)
            keys, values = kbuf[source, :, at], vbuf[source, :, at]
            scores = lax.dot_general(
                qs[p, h], keys, (((1,), (1,)), ((), ())), preferred_element_type=jnp.float32
            ) * scale
            spot = lax.broadcasted_iota(jnp.int32, scores.shape, 1) + source * z.block
            scores = jnp.where(spot.astype(jnp.float32) < lens[p], scores, MASKED)
            before = peak[p, h]
            now = jnp.maximum(before, jnp.max(scores, axis=1, keepdims=True))
            fade = jnp.exp(before - now)
            part = jnp.exp(scores - now)
            peak[p, h] = now
            total[p, h] = total[p, h] * fade + jnp.sum(part, axis=1, keepdims=True)
            acc[p, h] = acc[p, h] * fade + jnp.dot(
                part.astype(jnp.bfloat16), values, preferred_element_type=jnp.float32
            )

    def finish(p):
        for h in range(z.kl):
            context = (acc[p, h] / total[p, h]).astype(jnp.bfloat16)
            for g in range(z.group):
                at = (h * z.group + g) * HEAD_WIDTH
                cbuf[s, p, :, at:at + HEAD_WIDTH] = context[g * z.pt:(g + 1) * z.pt, :]
        for j in range(1, z.seq):
            sent.append(pltpu.make_async_remote_copy(
                src_ref=cbuf.at[s, p], dst_ref=cbuf.at[s, p],
                send_sem=c_send.at[j, p], recv_sem=c_recv.at[s, p],
                device_id={"seq": near(s, j, z.seq)}, device_id_type=MESH,
            ))
            sent[-1].start()

    for j in range(z.seq):
        source = nearest(j) if j else s
        if j == 0:
            for copy in own_kv:
                copy.wait()
        else:
            passed = []
            for n, buf in enumerate((kbuf, vbuf)):
                mine = buf.at[source, my_rows, :]
                pltpu.make_async_copy(mine, mine, kv_recv.at[n, source]).wait()
                passed.append(pltpu.make_async_remote_copy(
                    src_ref=mine, dst_ref=mine, send_sem=f_send.at[n, j], recv_sem=f_recv.at[n, source],
                    device_id={"rep": partner}, device_id_type=MESH,
                ))
                passed[-1].start()
            other = pl.ds(pl.multiple_of(partner * half, half), half)
            for n, buf in enumerate((kbuf, vbuf)):
                theirs = buf.at[source, other, :]
                pltpu.make_async_copy(theirs, theirs, f_recv.at[n, source]).wait()
            sent.extend(passed)
        for p in range(z.np):
            attend(p, source)
            if j == z.seq - 1:
                finish(p)

    for copy in weights:
        copy.wait()

    def project(j, source, p, at):
        value = jnp.dot(
            cbuf[source, p], wbuf[head_of(source), :, at], preferred_element_type=jnp.float32
        )
        if z.b > 1:
            oacc[pl.ds(pl.multiple_of(source * z.nt, z.nt), z.nt), at] = value
            return value
        rows = slice(p * z.pt, (p + 1) * z.pt)
        if j:
            value = value + oacc[rows, at]
        if j < z.seq - 1:
            oacc[rows, at] = value
        return value

    def give(i, n, value):
        osend[i, n] = value.astype(jnp.bfloat16)
        sent.append(pltpu.make_async_remote_copy(
            src_ref=osend.at[i, n], dst_ref=orecv.at[i, n],
            send_sem=o_send.at[i, n], recv_sem=o_recv.at[i, n],
            device_id={"tp": near(t, i + 1, z.tp)}, device_id_type=MESH,
        ))
        sent[-1].start()

    def keep(n, at, value):
        for i in range(z.tp - 1):
            pltpu.make_async_copy(orecv.at[i, n], orecv.at[i, n], o_recv.at[i, n]).wait()
            value = value + orecv[i, n].astype(jnp.float32)
        out_ref[0, :, at] = value.astype(jnp.bfloat16)

    spans = [slice(n * z.tile, (n + 1) * z.tile) for n in range(z.tiles)]
    for p in range(z.np):
        for j in range(z.seq):
            source = nearest(j) if j else s
            if j:
                landed = cbuf.at[source, p]
                pltpu.make_async_copy(landed, landed, c_recv.at[source, p]).wait()
            for n, at in enumerate(spans):
                value = project(j, source, p, at)
                if z.b == 1 and j == z.seq - 1:
                    if p < z.np - 1:
                        give(p, n, value)
                    else:
                        keep(n, at, value)
    if z.b > 1:
        for n, at in enumerate(spans):
            for i in range(z.tp - 1):
                rows = pl.ds(pl.multiple_of(near(t, i + 1, z.tp) * z.no, z.no), z.no)
                give(i, n, oacc[rows, at])
        for n, at in enumerate(spans):
            keep(n, at, oacc[pl.ds(pl.multiple_of(t * z.no, z.no), z.no), at])
    for copy in sent:
        copy.wait_send()
    for s_to, copy in sent_if:
        pl.when(s != s_to)(copy.wait_send)


def line_kernel(
    z, q_hbm, fk_hbm, fv_hbm, vis_hbm, k_hbm, v_hbm, w_hbm, out_ref,
    qbuf, fkbuf, fvbuf, kbuf, vbuf, wbuf, qs, lens, peak, acc, cbuf, oacc, osend, orecv,
    q_send, q_recv, kv_send, kv_recv, f_send, f_recv, kv_own, w_sem, c_send, c_recv, o_send, o_recv,
    vis_ref, vis_sem,
):
    s, t, r = lax.axis_index("seq"), lax.axis_index("tp"), lax.axis_index("rep")
    partner, t_other = 1 - r, 1 - t
    log_scale = math.log2(math.e) / math.sqrt(HEAD_WIDTH)
    low = s < 2
    is_end = (s == 0) | (s == 3)
    mate = s + 1 - 2 * lax.rem(s, 2)
    far_end = jnp.where(low, 3, 0)
    far_mid = jnp.where(low, 2, 1)

    barrier = pltpu.get_barrier_semaphore()
    for s_to, t_to in (
        (far_end, t), (far_mid, t), (far_end, t_other), (far_mid, t_other), (mate, t), (mate, t_other), (s, t_other)
    ):
        pl.semaphore_signal(barrier, inc=1, device_id={"seq": s_to, "tp": t_to}, device_id_type=MESH)
    pl.semaphore_signal(barrier, inc=1, device_id={"rep": partner}, device_id_type=MESH)

    my_slot = s * 2 + t

    def query_parts(s_to, t_to):
        head = t_to * 4 + s_to
        wide = pl.ds(pl.multiple_of(head * z.fb, 128), z.fb)
        thin = pl.ds(pl.multiple_of(head * z.kb, 128), z.kb)
        return (
            (q_hbm.at[0, :, wide], qbuf.at[my_slot]),
            (fk_hbm.at[0, :, thin], fkbuf.at[my_slot]),
            (fv_hbm.at[0, :, thin], fvbuf.at[my_slot]),
        )

    own_parts = [
        pltpu.make_async_copy(src, dst, q_recv.at[n, my_slot])
        for n, (src, dst) in enumerate(query_parts(s, t))
    ]
    thin_own = pl.ds(pl.multiple_of(s * z.kb, 128), z.kb)
    own_kv = [
        pltpu.make_async_copy(k_hbm.at[:, thin_own], kbuf.at[s], kv_own.at[0]),
        pltpu.make_async_copy(v_hbm.at[:, thin_own], vbuf.at[s, :, 0:HEAD_WIDTH], kv_own.at[1]),
    ]
    weights = [
        pltpu.make_async_copy(w_hbm.at[pl.ds(n * z.fb, z.fb), :], wbuf.at[n], w_sem.at[n])
        for n in range(4)
    ]
    def column_of_lengths(p):
        want = lax.broadcasted_iota(jnp.int32, (z.pt, z.all_tok), 0) + owner_of(p) * z.pt
        have = lax.broadcasted_iota(jnp.int32, (z.pt, z.all_tok), 1)
        seen = jnp.where(want == have, jnp.broadcast_to(vis_ref[...], (z.pt, z.all_tok)), 0)
        column = jnp.sum(seen.astype(jnp.float32), axis=1, keepdims=True)
        lens[p] = jnp.broadcast_to(jnp.concatenate([column] * z.group, axis=0), (z.rows, HEAD_WIDTH))

    def owner_of(p):
        return t_other if p == 0 else t

    pl.semaphore_wait(barrier, 8)

    sent = []

    def send(copy):
        copy.start()
        sent.append(copy)

    def query_copies(k, s_to, t_to):
        return [
            pltpu.make_async_remote_copy(
                src_ref=src, dst_ref=dst, send_sem=q_send.at[n, k],
                recv_sem=q_recv.at[n, my_slot], device_id={"seq": s_to, "tp": t_to},
                device_id_type=MESH,
            )
            for n, (src, dst) in enumerate(query_parts(s_to, t_to))
        ]

    half = z.block // 2
    my_rows = pl.ds(pl.multiple_of(r * half, half), half)
    other_rows = pl.ds(pl.multiple_of(partner * half, half), half)

    def prefix_copies(k, s_to):
        thin = pl.ds(pl.multiple_of(s_to * z.kb, 128), z.kb)
        return [
            pltpu.make_async_remote_copy(
                src_ref=src.at[my_rows, thin], dst_ref=dst.at[s, my_rows, 0:HEAD_WIDTH],
                send_sem=kv_send.at[n, k], recv_sem=kv_recv.at[n, s],
                device_id={"seq": s_to}, device_id_type=MESH,
            )
            for n, (src, dst) in enumerate(((k_hbm, kbuf), (v_hbm, vbuf)))
        ]

    targets = (far_end, far_mid, mate)
    queries = [query_copies(2 * k + 2, s_to, t) + query_copies(2 * k + 3, s_to, t_other) for k, s_to in enumerate(targets)]
    prefix = [prefix_copies(k, s_to) for k, s_to in enumerate(targets)]
    beside = query_copies(0, s, t_other)
    for copy in queries[0]:
        send(copy)

    @pl.when(is_end)
    def _():
        for copy in prefix[0] + queries[1] + queries[2] + prefix[2] + prefix[1]:
            copy.start()

    @pl.when(jnp.logical_not(is_end))
    def _():
        for copy in prefix[0] + queries[2] + prefix[2] + queries[1] + prefix[1]:
            copy.start()

    for k in range(3):
        sent.extend(prefix[k])
    for copy in beside:
        send(copy)
    sent.extend(queries[1] + queries[2])

    lengths = pltpu.make_async_copy(vis_hbm, vis_ref, vis_sem)
    for copy in [lengths] + own_parts + own_kv + weights:
        copy.start()
    lengths.wait()

    for p in range(2):
        column_of_lengths(p)
    head_lanes = slice(0, HEAD_WIDTH)
    vbuf[:, :, HEAD_WIDTH:] = jnp.ones((4, z.block, HEAD_WIDTH), jnp.bfloat16)
    for slot in range(8):
        for n, buf in enumerate((qbuf, fkbuf, fvbuf)):
            pltpu.make_async_copy(buf.at[slot], buf.at[slot], q_recv.at[n, slot]).wait()

    def rows_of(buf, p, first):
        some = pl.ds(owner_of(p) * z.ps, z.ps)
        value = buf[some, :, first:first + HEAD_WIDTH].astype(jnp.float32)
        return value.reshape(z.pt, HEAD_WIDTH)

    for p in range(2):
        own_key, own_value = rows_of(fkbuf, p, 0), rows_of(fvbuf, p, 0)
        for g in range(z.group):
            query = rows_of(qbuf, p, g * HEAD_WIDTH)
            span = slice(g * z.pt, (g + 1) * z.pt)
            qs[p, span, :] = query.astype(jnp.bfloat16)
            own = jnp.sum(query * own_key, axis=1, keepdims=True)
            peak[p, span, :] = jnp.broadcast_to(own, (z.pt, HEAD_WIDTH))
            acc[p, span, head_lanes] = own_value
            acc[p, span, HEAD_WIDTH:] = jnp.ones((z.pt, HEAD_WIDTH), jnp.float32)

    def attend(p, source, first=0, count=None):
        count = count or z.block
        repeat = count // HEAD_WIDTH
        rows = pl.ds(first if isinstance(first, int) else pl.multiple_of(first, half), count)
        scores = lax.dot_general(
            qs[p], kbuf[source, rows, :], (((1,), (1,)), ((), ())), preferred_element_type=jnp.float32
        )
        spot = lax.broadcasted_iota(jnp.int32, scores.shape, 1).astype(jnp.float32)
        left = lens[p] - (source * z.block + first).astype(jnp.float32)
        scores = jnp.where(spot < jnp.concatenate([left] * repeat, axis=1), scores, MASKED)
        before = peak[p]
        now = jnp.maximum(before, jnp.broadcast_to(jnp.max(scores, axis=1, keepdims=True), before.shape))
        fade = jnp.exp2((before - now) * log_scale)
        part = jnp.exp2((scores - jnp.concatenate([now] * repeat, axis=1)) * log_scale)
        peak[p] = now
        acc[p] = acc[p] * jnp.concatenate([fade] * 2, axis=1) + jnp.dot(
            part.astype(jnp.bfloat16), vbuf[source, rows, :], preferred_element_type=jnp.float32
        )

    def pass_kv(j, source):
        passed = []
        for n, buf in enumerate((kbuf, vbuf)):
            mine = buf.at[source, my_rows, 0:HEAD_WIDTH]
            pltpu.make_async_copy(mine, mine, kv_recv.at[n, source]).wait()
            passed.append(pltpu.make_async_remote_copy(
                src_ref=mine, dst_ref=mine, send_sem=f_send.at[n, j], recv_sem=f_recv.at[n, source],
                device_id={"rep": partner}, device_id_type=MESH,
            ))
            passed[-1].start()
        return passed

    def passed_kv(source):
        for n, buf in enumerate((kbuf, vbuf)):
            theirs = buf.at[source, other_rows, 0:HEAD_WIDTH]
            pltpu.make_async_copy(theirs, theirs, f_recv.at[n, source]).wait()

    def finish(p):
        context = (acc[p, :, head_lanes] / acc[p, :, HEAD_WIDTH:]).astype(jnp.bfloat16)
        for g in range(z.group):
            cbuf[s, p, :, g * HEAD_WIDTH:(g + 1) * HEAD_WIDTH] = context[g * z.pt:(g + 1) * z.pt, :]
        pl.when(jnp.logical_not(is_end))(context_copy(1, s, p, mate).start)
        send(context_copy(0, s, p, far_end))
        pl.when(jnp.logical_not(is_end))(context_copy(2, s, p, far_mid).start)

        sent.append(context_copy(1, s, p, mate))

    def context_copy(k, source, p, s_to):
        return pltpu.make_async_remote_copy(
            src_ref=cbuf.at[source, p], dst_ref=cbuf.at[source, p],
            send_sem=c_send.at[k, p], recv_sem=c_recv.at[source, p],
            device_id={"seq": s_to}, device_id_type=MESH,
        )

    def landed(source, p):
        pltpu.make_async_copy(cbuf.at[source, p], cbuf.at[source, p], c_recv.at[source, p]).wait()

    spans = [slice(n * z.tile, (n + 1) * z.tile) for n in range(z.tiles)]

    def project_all(source, first):
        for at in spans:
            value = jnp.dot(
                cbuf[source].reshape(2 * z.pt, z.fb), wbuf[source, :, at], preferred_element_type=jnp.float32
            )
            oacc[:, at] = value if first else oacc[:, at] + value

    def project_half(source, p, at):
        return oacc[p * z.pt:(p + 1) * z.pt, at] + jnp.dot(
            cbuf[source, p], wbuf[source, :, at], preferred_element_type=jnp.float32
        )

    sources = (
        jnp.where(is_end, far_end, mate), jnp.where(is_end, far_mid, far_end), jnp.where(is_end, mate, far_mid)
    )
    for copy in own_kv:
        copy.wait()
    sent.extend(pass_kv(0, sources[0]))
    for p in range(2):
        attend(p, s)
    sent.extend(pass_kv(1, sources[1]))
    passed_kv(sources[0])
    for p in range(2):
        attend(p, sources[0])
    passed_kv(sources[1])
    attend(0, sources[1])
    sent.extend(pass_kv(2, sources[2]))
    attend(1, sources[1])
    for p in range(2):
        attend(p, sources[2], r * half, half)
    passed_kv(sources[2])
    early = list(sent)
    sent.clear()
    for p in range(2):
        attend(p, sources[2], partner * half, half)
        finish(p)

    @pl.when(is_end)
    def _():
        for p in range(2):
            context_copy(1, s, p, mate).start()

    for copy in weights:
        copy.wait()
    project_all(s, True)
    for copy in early:
        copy.wait_send()
    second = jnp.where(is_end, far_end, mate)
    for p in range(2):
        landed(second, p)

        @pl.when(is_end)
        def _():
            context_copy(2, far_end, p, mate).start()
    project_all(second, False)

    third = jnp.where(is_end, mate, far_end)
    for p in range(2):
        landed(third, p)
        for at in spans:
            oacc[p * z.pt:(p + 1) * z.pt, at] = project_half(third, p, at)
        landed(far_mid, p)
        for n, at in enumerate(spans):
            value = project_half(far_mid, p, at)
            if p == 0:
                osend[0, n] = value.astype(jnp.bfloat16)
                send(pltpu.make_async_remote_copy(
                    src_ref=osend.at[0, n], dst_ref=orecv.at[0, n],
                    send_sem=o_send.at[0, n], recv_sem=o_recv.at[0, n],
                    device_id={"tp": t_other}, device_id_type=MESH,
                ))
            else:
                pltpu.make_async_copy(orecv.at[0, n], orecv.at[0, n], o_recv.at[0, n]).wait()
                out_ref[0, :, at] = (value + orecv[0, n].astype(jnp.float32)).astype(jnp.bfloat16)
    for copy in sent:
        copy.wait_send()
    for p in range(2):
        context_copy(2, s, p, mate).wait_send()


def shards(mesh_shape, *args):
    queries, fresh_key_rows, fresh_value_rows, visible, prefix_keys, cached_value_rows, out_weight = args
    z = Sizes(mesh_shape, queries, visible, prefix_keys, out_weight)
    staged = z.seq == 4 and z.tp == 2 and z.rep == 2 and z.b == 1 and z.kl == 1
    bf16, f32 = jnp.bfloat16, jnp.float32
    vmem, dma = pltpu.VMEM, pltpu.SemaphoreType.DMA
    if staged:
        state = [
            vmem((2, z.rows, HEAD_WIDTH), bf16),
            vmem((2, z.rows, HEAD_WIDTH), f32),
            vmem((2, z.rows, HEAD_WIDTH), f32),
            vmem((2, z.rows, 2 * HEAD_WIDTH), f32),
        ]
    else:
        state = [
                vmem((z.np, z.kl, z.rows, HEAD_WIDTH), bf16),
                vmem((z.np, z.rows, 1), f32),
                vmem((z.np, z.kl, z.rows, 1), f32),
                vmem((z.np, z.kl, z.rows, 1), f32),
                vmem((z.np, z.kl, z.rows, HEAD_WIDTH), f32),
        ]
    anywhere = pl.BlockSpec(memory_space=pl.ANY)
    inside = pl.BlockSpec(memory_space=pltpu.VMEM)
    held = pl.BlockSpec(memory_space=pltpu.HBM)
    return pl.pallas_call(
        functools.partial(line_kernel if staged else kernel, z),
        out_shape=jax.ShapeDtypeStruct((1, z.no, z.cols), bf16),
        in_specs=[held if staged else inside if n == 3 else anywhere for n in range(7)],
        out_specs=inside,
        scratch_shapes=[
            vmem((z.slots, z.tok, z.fb), bf16),
            vmem((z.slots, z.tok, z.kb), bf16),
            vmem((z.slots, z.tok, z.kb), bf16),
            vmem((z.seq, z.block, z.kb), bf16),
            vmem((z.seq, z.block, z.kb + staged * HEAD_WIDTH), bf16),
            vmem((z.a, z.fb, z.cols), bf16),
            *state,
            vmem((z.seq, z.np, z.pt, z.fb), bf16),
            vmem((z.all_tok, z.cols), f32),
            vmem((z.tp, z.tiles, z.no, z.tile), bf16),
            vmem((z.tp, z.tiles, z.no, z.tile), bf16),
            dma((3, z.slots)), dma((3, z.slots)),
            dma((2, z.seq)), dma((2, z.seq)),
            dma((2, z.seq)), dma((2, z.seq)),
            dma((2,)), dma((z.a,)),
            dma((z.seq, z.np)), dma((z.seq, z.np)),
            dma((z.tp, z.tiles)), dma((z.tp, z.tiles)),
            *([vmem((1, z.all_tok), jnp.int32), dma] if staged else []),
        ],
        compiler_params=pltpu.CompilerParams(
            collective_id=0, has_side_effects=True, vmem_limit_bytes=(44 if staged else 56) * 1024 * 1024
        ),
        name="attend_and_project",
    )(*([pltpu.with_memory_space_constraint(x, pltpu.HBM) for x in args] if staged else args))


def solution(mesh):
    in_specs = (
        P("rep", ("groups", "seq", "tp"), None),
        P("rep", ("groups", "seq", "tp"), None),
        P("rep", ("groups", "seq", "tp"), None),
        P("rep", "groups"),
        P(("groups", "seq"), "tp"),
        P(("groups", "seq"), "tp"),
        P("tp", "seq"),
    )
    out_specs = P("rep", ("groups", "tp"), "seq")
    body = functools.partial(shards, dict(mesh.shape))
    return jax.shard_map(body, mesh=mesh, in_specs=in_specs, out_specs=out_specs, check_vma=False)
```
